32 devices in a mesh: fs: 8 (over y, x, core), sp: 4 (over z).
Axes of the slice: x: 2, y: 2, z: 4, core: 2. Of those that a mesh axis runs over, the one named last changes fastest.
Arguments:
- layer_input: bfloat16 [4, 4096, 1280], P(None, ('fs', 'sp')), may hold values from -6 to 6
- output_grad: bfloat16 [4, 4096, 1280], P(None, ('fs', 'sp')), may hold values from -6 to 6
- segment_ids: int32 [4, 4096], replicated, may hold values from 0 to 4, never falling along the last dimension, each value on 1 to 2000 neighbouring positions
- adapter_index: int32 [4, 1], replicated, may hold values from 0 to 3
- gain_attention: float32 [1280], replicated, may hold values from 0.25 to 1.75
- gain_feedforward: float32 [1280], replicated, may hold values from 0.25 to 1.75
- query_scale: float32 [80], replicated, may hold values from 0.4 to 1.2
- weight_qkv: bfloat16 [1280, 3840], P(None, 'fs'), may hold values from -0.15625 to 0.15625
- weight_mixer: bfloat16 [1280, 1280], P(None, 'fs'), may hold values from -1 to 1
- weight_expand: bfloat16 [1280, 1280], P(None, 'fs'), may hold values from -0.15625 to 0.15625
- weight_contract: bfloat16 [1280, 1280], P(None, 'fs'), may hold values from -0.15625 to 0.15625
- qkv_down: bfloat16 [4, 1280, 16], replicated, may hold values from -0.15625 to 0.15625
- qkv_up: bfloat16 [4, 16, 3840], replicated, may hold values from -1.5 to 1.5
- mixer_down: bfloat16 [4, 1280, 16], replicated, may hold values from -1 to 1
- mixer_up: bfloat16 [4, 16, 1280], replicated, may hold values from -1.5 to 1.5
- expand_down: bfloat16 [4, 1280, 16], replicated, may hold values from -0.15625 to 0.15625
- expand_up: bfloat16 [4, 16, 1280], replicated, may hold values from -1.5 to 1.5
- contract_down: bfloat16 [4, 1280, 16], replicated, may hold values from -0.15625 to 0.15625
- contract_up: bfloat16 [4, 16, 1280], replicated, may hold values from -1.5 to 1.5
Outputs:
- layer_output: bfloat16 [4, 4096, 1280], P(None, ('fs', 'sp'))
- input_grad: bfloat16 [4, 4096, 1280], P(None, ('fs', 'sp'))
- gradient_projection_down: float32 [4, 1280, 16], replicated
- gradient_projection_up: float32 [4, 16, 3840], replicated
- grad_mixer_down: float32 [4, 1280, 16], replicated
- grad_mixer_up: float32 [4, 16, 1280], replicated
- grad_expand_down: float32 [4, 1280, 16], replicated
- grad_expand_up: float32 [4, 16, 1280], replicated
- grad_contract_down: float32 [4, 1280, 16], replicated
- grad_contract_up: float32 [4, 16, 1280], replicated
The draws below stay inside these ranges and needn't reach their ends.
Inputs may be any that keep to these rules, and one draw needn't show every extreme that they name: `segment_ids`: within each sequence the document numbers never fall; each document holds 1 to 2000 tokens, one exactly 2000. `adapter_index`: every adapter serves at least one sequence.
All inputs are finite; a program needn't handle non-finite values.
Results may differ from the reference program's by a relative error of at most 0.017.
Values may be sent and summed in bfloat16 or wider, within the bound.
No kernel may reach another device: no remote copies, remote signals or barrier semaphores. Data moves between devices by JAX's collectives and lax.ppermute only.
A program may use at most 320 MiB of HBM per device.

```python
import math
import jax
import jax.numpy as jnp
import numpy as np
from jax import lax

D = 1280
FF = 1280
H = 16
HD = 80
R = 16
NA = 4
SEQS = 4
MOST = 2000
WINDOW = 2048
LEN = 4096
DOCS = 5


def levels(own_key, extent, pieces, low, high):
    def one(dim, shards_of):
        heights = jax.random.uniform(jax.random.fold_in(jax.random.fold_in(own_key, 6), dim), (shards_of,), jnp.float32, low / len(pieces), high / len(pieces))
        return jnp.repeat(jnp.exp(heights), extent[dim] // shards_of).reshape((-1,) + (1,) * (len(extent) - dim - 1))

    level = one(*pieces[0])
    for cut in pieces[1:]:
        level = level * one(*cut)
    return level


def picks_of(rng, rows, number_of, top, lift):
    order = jax.random.permutation(jax.random.fold_in(rng, 1), number_of)
    favour = order
    for power in range(3):
        favour = favour * favour // number_of
    favour = favour * lift // number_of
    tickets = jax.random.randint(jax.random.fold_in(rng, 2), (rows, number_of), 0, 4096) + favour
    holders = jax.random.permutation(jax.random.fold_in(rng, 3), rows)[jnp.arange(number_of) % rows]
    tickets = jnp.where(jnp.arange(rows)[:, None] == holders[None, :], 1 << 14, tickets)
    priority = tickets * number_of + jnp.arange(number_of)
    return lax.top_k(priority.astype(jnp.int32), top)[1].astype(jnp.int32)


def length_profile(number_of, total, bound, skew):
    weights = [(1 << 20) // math.isqrt(standing ** skew) + 1 for standing in range(2, number_of + 1)]
    rest, given = total - bound - (number_of - 1), [1] * (number_of - 1)
    while rest > 0:
        free = [i for i in range(number_of - 1) if given[i] < bound]
        mass, budget = sum([weights[i] for i in free]), rest
        for i in free:
            addition = min(bound - given[i], max(1, budget * weights[i] // mass), rest)
            given[i] = given[i] + addition
            rest = rest - addition
    return np.array([bound] + given)


def uneven(stream_key, amount, total, limit, lean):
    if amount == 2:
        one = jax.random.randint(stream_key, (), max(1, total - limit), min(limit, total - 1) + 1)
        return jnp.stack([one, total - one])
    sizes = jnp.asarray(length_profile(amount, total, limit, lean), jnp.int32)
    pairs = (amount - 1) // 2
    source_of, taker = sizes[1:1 + 2 * pairs:2], sizes[2:2 + 2 * pairs:2]
    margin = jnp.minimum(source_of - 1, limit - taker)
    moved = jax.random.randint(jax.random.fold_in(stream_key, 1), (pairs,), 0, 1 << 20) % (margin + 1)
    sizes = sizes.at[1:1 + 2 * pairs:2].set(source_of - moved).at[2:2 + 2 * pairs:2].set(taker + moved)
    return sizes[jax.random.permutation(jax.random.fold_in(stream_key, 2), amount)]


def scatter_about(own_key, shape, spread, limit, split=(), kind=jnp.bfloat16):
    values = spread * jax.random.normal(own_key, shape, jnp.float32)
    if split:
        values = values * levels(own_key, shape, split, -0.22, 0.18)
    return jnp.clip(values, -limit, limit).astype(kind)


def setup_inputs(seed: int = 0) -> dict:
    key_list = jax.random.split(jax.random.key(seed), 20)
    return {
        "layer_input": scatter_about(key_list[0], (SEQS, LEN, D), 1.0, 6.0, ((1, 32),)),
        "output_grad": scatter_about(key_list[1], (SEQS, LEN, D), 1.0, 6.0, ((1, 32),)),
        "segment_ids": jax.vmap(lambda own: jnp.searchsorted(jnp.cumsum(uneven(own, DOCS, LEN, MOST, 1)), jnp.arange(LEN), side="right"))(jax.random.split(key_list[2], SEQS)).reshape((SEQS, LEN)).astype(jnp.int32),
        "adapter_index": picks_of(key_list[3], SEQS, NA, 1, 0),
        "gain_attention": jnp.clip(1.0 + 0.15 * jax.random.normal(key_list[4], (D,), jnp.float32), 0.25, 1.75),
        "gain_feedforward": jnp.clip(1.0 + 0.15 * jax.random.normal(key_list[5], (D,), jnp.float32), 0.25, 1.75),
        "query_scale": jnp.clip(jnp.exp(jax.random.uniform(key_list[6], (HD,), jnp.float32, math.log(0.4), math.log(1.2))), 0.4, 1.2),
        "weight_qkv": scatter_about(key_list[7], (D, 3 * D), D ** -0.5, 0.15625, ((1, 8),)),
        "weight_mixer": scatter_about(key_list[8], (D, D), (D // 32) ** -0.5, 1.0, ((1, 8),)),
        "weight_expand": scatter_about(key_list[9], (D, FF), D ** -0.5, 0.15625, ((1, 8),)),
        "weight_contract": scatter_about(key_list[10], (FF, D), FF ** -0.5, 0.15625, ((1, 8),)),
        "qkv_down": scatter_about(key_list[11], (NA, D, R), D ** -0.5, 0.15625),
        "qkv_up": scatter_about(key_list[12], (NA, R, 3 * D), R ** -0.5, 1.5),
        "mixer_down": scatter_about(key_list[13], (NA, D, R), (D // 32) ** -0.5, 1.0),
        "mixer_up": scatter_about(key_list[14], (NA, R, D), R ** -0.5, 1.5),
        "expand_down": scatter_about(key_list[15], (NA, D, R), D ** -0.5, 0.15625),
        "expand_up": scatter_about(key_list[16], (NA, R, FF), R ** -0.5, 1.5),
        "contract_down": scatter_about(key_list[17], (NA, FF, R), FF ** -0.5, 0.15625),
        "contract_up": scatter_about(key_list[18], (NA, R, D), R ** -0.5, 1.5),
    }


EPSILON = 1e-06

@jax.custom_vjp
def low(v):
    return lax.optimization_barrier(v.astype(jnp.bfloat16)).astype(jnp.float32)

@jax.custom_vjp
def low_back(v):
    return v

def low_keep(v):
    return (low(v), None)

def low_pass(kept, grad):
    return (grad,)

def back_keep(v):
    return (v, None)

def back_low(kept, grad):
    return (low(grad),)
low.defvjp(low_keep, low_pass)
low_back.defvjp(back_keep, back_low)

def matmul(left, right):
    return jnp.dot(left, right, precision=lax.Precision.HIGHEST)

def rms_scale(values):
    return lax.rsqrt(lax.optimization_barrier(jnp.mean(values * values, axis=-1, keepdims=True)) + EPSILON)

def select_table(adapter_pick, table_array):
    return jnp.einsum('a,a...->...', adapter_pick, table_array, precision=lax.Precision.HIGHEST)

def adapter_path(inputs, table_down, table_up, adapter_pick):
    narrow = low(low_back(matmul(inputs, select_table(adapter_pick, table_down))))
    return matmul(narrow, select_table(adapter_pick, table_up))

def attention_sequence(queries, key_rows, value_rows, segments):
    length = queries.shape[0]
    block_rows = min(512, length)
    key_span = WINDOW + block_rows
    padded_keys = jnp.pad(key_rows, ((WINDOW, 0), (0, 0), (0, 0)))
    padded_values = jnp.pad(value_rows, ((WINDOW, 0), (0, 0), (0, 0)))
    padded_ids = jnp.concatenate([jnp.full((WINDOW,), -1, jnp.int32), segments.astype(jnp.int32)])
    order_mask = jnp.arange(key_span)[None, :] <= WINDOW + jnp.arange(block_rows)[:, None]

    def one_block(block_number):
        first_row = (block_number * block_rows).astype(jnp.int32)
        query_block = lax.dynamic_slice_in_dim(queries, first_row, block_rows, 0)
        key_block = lax.dynamic_slice_in_dim(padded_keys, first_row, key_span, 0)
        value_block = lax.dynamic_slice_in_dim(padded_values, first_row, key_span, 0)
        query_ids = lax.dynamic_slice_in_dim(segments.astype(jnp.int32), first_row, block_rows, 0)
        key_ids = lax.dynamic_slice_in_dim(padded_ids, first_row, key_span, 0)
        scores = low_back(jnp.einsum('qhd,khd->hqk', query_block, key_block, precision=lax.Precision.HIGHEST))
        allowed = (key_ids[None, :] == query_ids[:, None]) & order_mask
        scores = jnp.where(allowed[None], scores, -1e+30)
        weights = low(jax.nn.softmax(scores, axis=-1))
        mixed_rows = jnp.einsum('hqk,khd->qhd', weights, value_block, precision=lax.Precision.HIGHEST)
        return mixed_rows.reshape(block_rows, -1)
    blocks = lax.map(jax.checkpoint(one_block), jnp.arange(length // block_rows, dtype=jnp.int32))
    return blocks.reshape(length, -1)

def sequence_layer(tokens_in, segment_row, adapter_pick, frozen, adapted):
    gain_one, gain_two, query_gain, weight_qkv, weight_mixer, weight_expand, weight_contract = frozen
    table_qd, table_qu, table_md, table_mu, table_ed, table_eu, table_cd, table_cu = adapted
    length = tokens_in.shape[0]
    first_normalized = low(tokens_in * rms_scale(tokens_in) * gain_one)
    joined = low_back(matmul(first_normalized, weight_qkv) + adapter_path(first_normalized, table_qd, table_qu, adapter_pick))
    scale_row = query_gain * (1.0 / math.sqrt(HD))
    queries = low(low_back(joined[:, :D].reshape(length, H, HD) * scale_row))
    key_rows = low(low_back(joined[:, D:2 * D].reshape(length, H, HD)))
    value_rows = low(low_back(joined[:, 2 * D:].reshape(length, H, HD)))
    attention_result = low(low_back(attention_sequence(queries, key_rows, value_rows, segment_row)))
    mixer = low_back(matmul(attention_result, weight_mixer) + adapter_path(attention_result, table_md, table_mu, adapter_pick))
    middle = tokens_in + mixer
    second_normalized = low(middle * rms_scale(middle) * gain_two)
    expanded = low_back(matmul(second_normalized, weight_expand) + adapter_path(second_normalized, table_ed, table_eu, adapter_pick))
    hidden_activation = low(jax.nn.silu(expanded))
    contracted = low_back(matmul(hidden_activation, weight_contract) + adapter_path(hidden_activation, table_cd, table_cu, adapter_pick))
    return middle + contracted

def reference(layer_input, output_grad, segment_ids, adapter_index, gain_attention, gain_feedforward, query_scale, weight_qkv, weight_mixer, weight_expand, weight_contract, qkv_down, qkv_up, mixer_down, mixer_up, expand_down, expand_up, contract_down, contract_up):
    frozen = tuple((source.astype(jnp.float32) for source in (gain_attention, gain_feedforward, query_scale, weight_qkv, weight_mixer, weight_expand, weight_contract)))
    adapted = tuple((source.astype(jnp.float32) for source in (qkv_down, qkv_up, mixer_down, mixer_up, expand_down, expand_up, contract_down, contract_up)))
    pick_rows = (adapter_index[:, 0:1] == jnp.arange(NA, dtype=jnp.int32)[None, :]).astype(jnp.float32)

    def whole_layer(inputs, adapt_tables):

        def one_sequence(packed):
            return sequence_layer(packed[0], packed[1], packed[2], frozen, adapt_tables)
        return lax.map(jax.checkpoint(one_sequence), (inputs, segment_ids, pick_rows))
    outputs, pullback = jax.vjp(whole_layer, layer_input.astype(jnp.float32), adapted)
    input_grad, table_grads = pullback(output_grad.astype(jnp.float32))
    factor = 1.0 / math.sqrt(LEN)
    return (outputs.astype(jnp.bfloat16), input_grad.astype(jnp.bfloat16), table_grads[0] * factor, table_grads[1] * factor, table_grads[2] * factor, table_grads[3] * factor, table_grads[4] * factor, table_grads[5] * factor, table_grads[6] * factor, table_grads[7] * factor)
```

```python
import functools
import math

import jax
import jax.numpy as jnp
from jax import lax
from jax.experimental import pallas as pl
from jax.experimental.pallas import tpu as pltpu
from jax.sharding import PartitionSpec as P

EPSILON = 1e-06
BIG = 1e30
LANES = 128
PARTS = 3
TILE = 256
VMEM_LIMIT = 64000000
F32 = jnp.float32
BF16 = jnp.bfloat16
NT = (((1,), (1,)), ((), ()))
TN = (((0,), (0,)), ((), ()))


def dot_nn(a, b):
    return jnp.dot(a, b, preferred_element_type=F32)


def dot_nt(a, b):
    return lax.dot_general(a, b, NT, preferred_element_type=F32)


def dot_tn(a, b):
    return lax.dot_general(a, b, TN, preferred_element_type=F32)


def xor_permute(value, axis, mask):
    count = lax.axis_size(axis)
    return lax.ppermute(value, axis, [(a, a ^ mask) for a in range(count)])


def piece_of(stacked, index):
    return lax.dynamic_index_in_dim(stacked, index, 0, keepdims=False)


def project_kernel(sections, x_ref, gain_ref, w_ref, scale_ref, qpad_ref, kpad_ref, *refs, heads, head_dim):
    q_ref, k_ref, v_ref = refs[-3:]
    x = x_ref[0].astype(F32)
    mean = jnp.mean(x * x, axis=-1, keepdims=True)
    normed = (x * lax.rsqrt(mean + EPSILON) * gain_ref[...]).astype(BF16)
    rows = dot_nn(normed, w_ref[...]) * scale_ref[...]
    width = heads * LANES
    lane = lax.broadcasted_iota(jnp.int32, (1, width), 1) % LANES
    q_ref[...] = (rows[:, :width] + jnp.tile(qpad_ref[...].astype(F32), (1, heads))).astype(BF16)
    k_ref[...] = (rows[:, width : 2 * width] + jnp.tile(kpad_ref[...].astype(F32), (1, heads))).astype(BF16)
    ones = jnp.where((lane >= head_dim) & (lane < head_dim + PARTS), 1.0, 0.0)
    v_ref[...] = (rows[:, 2 * width :] + ones).astype(BF16)


def project(blocks, sections, gain, weight, scale, qpad, kpad, earlier, heads, head_dim, length):
    count, rows, model = blocks.shape
    step = TILE
    per = rows // step
    width = heads * LANES
    out = pl.BlockSpec((step, width), lambda b, h, sec: (sec[b] * per + h, 0))
    pad = pl.BlockSpec((step, LANES), lambda b, h, sec: (sec[b] * per + h, 0))
    fixed = lambda shape: pl.BlockSpec(shape, lambda b, h, sec: (0,) * len(shape))
    in_specs = [
        pl.BlockSpec((1, step, model), lambda b, h, sec: (b, h, 0)),
        fixed((1, model)),
        fixed((model, 3 * width)),
        fixed((1, 3 * width)),
        pad,
        pad,
    ]
    operands = [blocks, gain, weight, scale, qpad, kpad]
    aliases = {}
    if earlier is not None:
        in_specs += [pl.BlockSpec(memory_space=pl.ANY)] * 3
        aliases = {1 + len(operands) + n: n for n in range(3)}
        operands += list(earlier)
    return pl.pallas_call(
        functools.partial(project_kernel, heads=heads, head_dim=head_dim),
        out_shape=[jax.ShapeDtypeStruct((length, width), BF16)] * 3,
        grid_spec=pltpu.PrefetchScalarGridSpec(
            num_scalar_prefetch=1, grid=(count, per), in_specs=in_specs, out_specs=[out] * 3
        ),
        input_output_aliases=aliases,
        compiler_params=pltpu.CompilerParams(vmem_limit_bytes=VMEM_LIMIT),
        cost_estimate=pl.CostEstimate(
            flops=2 * count * rows * model * 3 * width,
            bytes_accessed=2 * (count * rows * (model + 3 * width) + model * 3 * width),
            transcendentals=0,
        ),
        name="project",
    )(sections, *operands)


def spread(column, lane, first):
    high = column.astype(BF16).astype(F32)
    middle = (column - high).astype(BF16).astype(F32)
    last = column - high - middle
    return jnp.where(lane == first, high, jnp.where(lane == first + 1, middle, last))


def attend_kernel(starts, q_ref, k_ref, v_ref, o_ref, aug_ref, s_ref, *, heads, head_dim):
    step = pl.program_id(0)
    first = starts[step]
    tile = q_ref.shape[0]
    lane = lax.broadcasted_iota(jnp.int32, (1, LANES), 1)

    def cols(h):
        return pl.ds(h * LANES, LANES)

    def scores(block, masked):
        out = []
        rows = pl.ds(pl.multiple_of(block * tile, tile), tile)
        for h in range(heads):
            s = dot_nt(q_ref[:, cols(h)], k_ref[rows, cols(h)])
            if masked:
                s = jnp.where(
                    lax.broadcasted_iota(jnp.int32, (tile, tile), 1)
                    <= lax.broadcasted_iota(jnp.int32, (tile, tile), 0),
                    s,
                    -BIG,
                )
            s_ref[h, block - first] = s
            top = s[:, :LANES]
            for c in range(LANES, tile, LANES):
                top = jnp.maximum(top, s[:, c : c + LANES])
            out.append(top)
        return tuple(out)

    def first_pass(block, tops):
        return tuple(jnp.maximum(a, b) for a, b in zip(tops, scores(block, False)))

    tops = lax.fori_loop(first, step, first_pass, scores(step, True))
    peaks = [jnp.max(top, axis=-1, keepdims=True) for top in tops]

    def second_pass(block, totals):
        rows = pl.ds(pl.multiple_of(block * tile, tile), tile)
        out = []
        for h in range(heads):
            p = jnp.exp(s_ref[h, block - first] - peaks[h]).astype(BF16)
            out.append(totals[h] + dot_nn(p, v_ref[rows, cols(h)]))
        return tuple(out)

    zero = jnp.zeros((tile, LANES), F32)
    totals = lax.fori_loop(first, step + 1, second_pass, (zero,) * heads)
    parts = []
    for h in range(heads):
        total = totals[h][:, head_dim : head_dim + 1]
        parts.append((totals[h] / total)[:, :head_dim].astype(BF16))
        lse = -(peaks[h] + jnp.log(total))
        marks = (lane >= head_dim) & (lane < head_dim + PARTS)
        aug_ref[:, cols(h)] = jnp.where(
            marks, spread(lse, lane, head_dim), q_ref[:, cols(h)].astype(F32)
        ).astype(BF16)
    o_ref[...] = jnp.concatenate(parts, axis=1)


def attend(starts, q, k, v, heads, head_dim):
    length, width = q.shape
    blocks = length // TILE
    span = min(blocks, -(-2048 // TILE) + 1)
    row = lambda w: pl.BlockSpec((TILE, w), lambda n, st: (n, 0))
    whole = pl.BlockSpec((length, width), lambda n, st: (0, 0))
    return pl.pallas_call(
        functools.partial(attend_kernel, heads=heads, head_dim=head_dim),
        out_shape=[
            jax.ShapeDtypeStruct((length, heads * head_dim), BF16),
            jax.ShapeDtypeStruct((length, width), BF16),
        ],
        grid_spec=pltpu.PrefetchScalarGridSpec(
            num_scalar_prefetch=1,
            grid=(blocks,),
            in_specs=[row(width), whole, whole],
            out_specs=[row(heads * head_dim), row(width)],
            scratch_shapes=[pltpu.VMEM((heads, span, TILE, TILE), F32)],
        ),
        compiler_params=pltpu.CompilerParams(vmem_limit_bytes=VMEM_LIMIT),
        cost_estimate=pl.CostEstimate(
            flops=4 * heads * length * 1024 * LANES, bytes_accessed=10 * length * width, transcendentals=0
        ),
        name="attend",
    )(starts, q, k, v)


def attend_back_kernel(
    ends, aug_ref, k_ref, v_ref, g_ref, o_ref, scale_ref, d_ref, gaug_ref, dq_ref, dk_ref, dv_ref, *, heads, head_dim
):
    step = pl.program_id(0)
    tile = k_ref.shape[0]
    length = aug_ref.shape[0]
    lane = lax.broadcasted_iota(jnp.int32, (1, LANES), 1)

    def cols(h):
        return pl.ds(h * LANES, LANES)

    @pl.when(step == 0)
    def _():
        @pl.loop(0, length // tile)
        def _(n):
            rows = pl.ds(pl.multiple_of(n * tile, tile), tile)
            g = g_ref[rows, :]
            product = g.astype(F32) * o_ref[rows, :].astype(F32)
            for h in range(heads):
                own = slice(h * head_dim, (h + 1) * head_dim)
                delta = -jnp.sum(product[:, own], axis=-1, keepdims=True)
                mine = jnp.concatenate(
                    [g[:, own].astype(F32), jnp.zeros((tile, LANES - head_dim), F32)], axis=1
                )
                marks = (lane >= head_dim) & (lane < head_dim + PARTS)
                gaug_ref[rows, cols(h)] = jnp.where(
                    marks, spread(delta, lane, head_dim), mine
                ).astype(BF16)
            dq_ref[rows, :] = jnp.zeros((tile, heads * LANES), F32)

    dk_ref[...] = jnp.zeros_like(dk_ref)
    dv_ref[...] = jnp.zeros_like(dv_ref)

    def one(block, masked):
        rows = pl.ds(pl.multiple_of(block * tile, tile), tile)
        for h in range(heads):
            q = aug_ref[rows, cols(h)]
            g = gaug_ref[rows, cols(h)]
            k = k_ref[:, cols(h)]
            s = dot_nt(k, q)
            if masked:
                s = jnp.where(
                    lax.broadcasted_iota(jnp.int32, (tile, tile), 0)
                    <= lax.broadcasted_iota(jnp.int32, (tile, tile), 1),
                    s,
                    -BIG,
                )
            p = jnp.exp(s)
            d = dot_nt(v_ref[:, cols(h)], g)
            dv_ref[:, cols(h)] += dot_nn(p.astype(BF16), g)
            ds = (p * d).astype(BF16)
            dk_ref[:, cols(h)] += dot_nn(ds, q)
            dq_ref[rows, cols(h)] += dot_tn(ds, k)

    one(step, True)

    @pl.loop(step + 1, ends[step])
    def _(block):
        one(block, False)

    own = pl.ds(pl.multiple_of(step * tile, tile), tile)
    pieces = []
    for h in range(heads):
        dq = dq_ref[own, cols(h)].astype(BF16).astype(F32) * scale_ref[...]
        pieces.append(dq[:, :head_dim])
    for ref in (dk_ref, dv_ref):
        for h in range(heads):
            pieces.append(ref[:, h * LANES : h * LANES + head_dim])
    d_ref[...] = jnp.concatenate(pieces, axis=1).astype(BF16)


def attend_back(ends, aug, k, v, grad, attended, scale, heads, head_dim):
    length, width = aug.shape
    blocks = length // TILE
    row = lambda w: pl.BlockSpec((TILE, w), lambda n, st: (n, 0))
    whole = lambda w: pl.BlockSpec((length, w), lambda n, st: (0, 0))
    return pl.pallas_call(
        functools.partial(attend_back_kernel, heads=heads, head_dim=head_dim),
        out_shape=jax.ShapeDtypeStruct((length, 3 * heads * head_dim), BF16),
        grid_spec=pltpu.PrefetchScalarGridSpec(
            num_scalar_prefetch=1,
            grid=(blocks,),
            in_specs=[
                whole(width),
                row(width),
                row(width),
                whole(heads * head_dim),
                whole(heads * head_dim),
                pl.BlockSpec((1, LANES), lambda n, st: (0, 0)),
            ],
            out_specs=row(3 * heads * head_dim),
            scratch_shapes=[
                pltpu.VMEM((length, width), BF16),
                pltpu.VMEM((length, width), F32),
                pltpu.VMEM((TILE, width), F32),
                pltpu.VMEM((TILE, width), F32),
            ],
        ),
        compiler_params=pltpu.CompilerParams(vmem_limit_bytes=VMEM_LIMIT),
        cost_estimate=pl.CostEstimate(
            flops=10 * heads * length * 1024 * LANES, bytes_accessed=14 * length * width, transcendentals=0
        ),
        name="attend_back",
    )(ends, aug, k, v, grad, attended, scale)


def rms_scale(values):
    return lax.rsqrt(jnp.mean(values * values, axis=-1, keepdims=True) + EPSILON)


def rms_back(values, scale_rows, grad_normed):
    cubed = scale_rows * scale_rows * scale_rows
    return scale_rows * grad_normed - values * cubed * jnp.mean(
        grad_normed * values, axis=-1, keepdims=True
    )


def to_sequence(value, groups):
    own = lax.axis_index("sp") % groups
    pieces = [piece_of(value, own)]
    pieces += [xor_permute(piece_of(value, own ^ m), "sp", m) for m in range(1, groups)]
    stacked = jnp.stack(pieces)
    return jnp.concatenate([piece_of(stacked, n ^ own) for n in range(groups)], axis=0)


def from_sequence(value, groups):
    rows = value.shape[0] // groups
    own = lax.axis_index("sp") % groups
    split = value.reshape(groups, rows, -1)
    pieces = [piece_of(split, own)]
    pieces += [xor_permute(piece_of(split, own ^ m), "sp", m) for m in range(1, groups)]
    stacked = jnp.stack(pieces)
    return jnp.stack([piece_of(stacked, n ^ own) for n in range(groups)], axis=0)


def local(
    layer_input,
    output_grad,
    segment_ids,
    adapter_index,
    gain_attention,
    gain_feedforward,
    query_scale,
    weight_qkv,
    weight_mixer,
    weight_expand,
    weight_contract,
    qkv_down,
    qkv_up,
    mixer_down,
    mixer_up,
    expand_down,
    expand_up,
    contract_down,
    contract_up,
):
    sequences, tokens, model = layer_input.shape
    head_dim = query_scale.shape[0]
    n_fs, n_sp = lax.axis_size("fs"), lax.axis_size("sp")
    adapters, rank = qkv_down.shape[0], qkv_down.shape[2]
    length = segment_ids.shape[1]
    folds = n_sp // sequences
    heads = model // head_dim // n_fs
    unit = heads * head_dim
    width = heads * LANES
    rows = sequences * tokens
    fs = lax.axis_index("fs")
    sp = lax.axis_index("sp")
    own_seq = sp % sequences
    fold = sp // sequences
    section = fs * folds + fold

    pick = piece_of(adapter_index, own_seq)[0]
    downs = [piece_of(t, pick) for t in (qkv_down, mixer_down, expand_down, contract_down)]
    ups = [piece_of(t, pick) for t in (qkv_up, mixer_up, expand_up, contract_up)]

    def merged(weight, down, up):
        cols = weight.shape[1]
        own_up = lax.dynamic_slice_in_dim(up, fs * cols, cols, 1)
        return (weight.astype(F32) + dot_nn(down, own_up)).astype(BF16)

    w_mixer, w_expand, w_contract = (
        lax.all_gather(merged(w, d, u), "fs", axis=1, tiled=True)
        for w, d, u in zip((weight_mixer, weight_expand, weight_contract), downs[1:], ups[1:])
    )
    shard = merged(weight_qkv, downs[0], ups[0])
    inverse = pow(3, -1, n_fs)
    received = [
        lax.ppermute(
            shard[:, t * unit : (t + 1) * unit], "fs", [(d, (3 * d + t) % n_fs) for d in range(n_fs)]
        )
        for t in range(3)
    ]
    places = [(3 * ((inverse * (fs - t)) % n_fs) + t) // n_fs for t in range(3)]
    w_parts = []
    for b in range(3):
        part = jnp.zeros_like(received[0])
        for t in range(3):
            part = jnp.where(places[t] == b, received[t], part)
        w_parts.append(part)
    w_own = jnp.concatenate(w_parts, axis=1)
    w_all = lax.all_gather(w_own, "fs", axis=0)
    w_padded = jnp.pad(
        w_own.reshape(model, 3 * heads, head_dim), ((0, 0), (0, 0), (0, LANES - head_dim))
    ).reshape(model, 3 * width)

    x_own = to_sequence(layer_input, sequences)
    g_own = to_sequence(output_grad, sequences)
    segs = piece_of(segment_ids, own_seq)

    scale = query_scale * (1.0 / math.sqrt(head_dim))
    scale_pad = jnp.pad(scale, (0, LANES - head_dim))[None]
    col_scale = jnp.concatenate([jnp.tile(scale_pad, (1, heads)), jnp.ones((1, 2 * width), F32)], axis=1)
    lane = jnp.arange(LANES)[None, :]
    marks = lane >= head_dim + PARTS
    same = lane == segs[:, None] + (head_dim + PARTS)
    qpad = same.astype(BF16)
    kpad = jnp.where(
        marks, jnp.where(same, 0.0, -BIG), jnp.where(lane >= head_dim, 1.0, 0.0)
    ).astype(BF16)

    project_args = (gain_attention[None], w_padded, col_scale, qpad, kpad)
    as_table = lambda *s: jnp.stack(s).astype(jnp.int32)
    if n_fs == 8 and folds == 1:
        half = rows // 2
        blk_y = xor_permute(x_own, "fs", 4)
        blk_x = xor_permute(x_own, "fs", 2)
        top = xor_permute(blk_y[:half], "fs", 2)
        bottom = xor_permute(blk_x[half:], "fs", 4)
        diag = jnp.concatenate([top, bottom], axis=0)
        arrivals = [(0, x_own), (1, xor_permute(x_own, "fs", 1))]
        for mask, block in ((4, blk_y), (2, blk_x), (6, diag)):
            arrivals += [(mask, block), (mask ^ 1, xor_permute(block, "fs", 1))]
        qkv = None
        for mask, block in arrivals:
            qkv = project(
                block[None], as_table(fs ^ mask), *project_args, qkv, heads, head_dim, length
            )
    else:
        gathered = lax.all_gather(x_own, ("fs", "sp"), axis=0)
        gathered = gathered.reshape(n_fs, folds, sequences, rows, model)
        gathered = lax.dynamic_index_in_dim(gathered, own_seq, 2, keepdims=False)
        blocks = gathered.reshape(n_fs * folds, rows, model)
        qkv = project(
            blocks, jnp.arange(n_fs * folds, dtype=jnp.int32), *project_args, None, heads, head_dim, length
        )
    q, k, v = qkv

    firsts, lasts = segs[::TILE], segs[TILE - 1 :: TILE]
    starts = jnp.sum(segs[None, :] < firsts[:, None], axis=1, dtype=jnp.int32) // TILE
    ends = (jnp.sum(segs[None, :] <= lasts[:, None], axis=1, dtype=jnp.int32) + TILE - 1) // TILE

    attended_heads, aug = attend(starts, q, k, v, heads, head_dim)

    def sections_out(value):
        cut = value.reshape(n_fs, folds, rows, value.shape[1])
        mine = lax.dynamic_index_in_dim(cut, fold, 1, keepdims=False)
        return lax.all_to_all(mine, "fs", split_axis=0, concat_axis=0, tiled=True)

    attended = jnp.swapaxes(sections_out(attended_heads), 0, 1).reshape(rows, model)

    x_f = x_own.astype(F32)
    scale_one = rms_scale(x_f)
    normed_one = (x_f * scale_one * gain_attention).astype(BF16)
    narrow = lambda u, down: dot_nn(u, down).astype(BF16)
    mixer = dot_nn(attended, w_mixer)
    middle = x_f + mixer
    scale_two = rms_scale(middle)
    normed_two = (middle * scale_two * gain_feedforward).astype(BF16)
    expanded = dot_nn(normed_two, w_expand)
    gate = jax.nn.sigmoid(expanded)
    hidden = (expanded * gate).astype(BF16)
    contracted = dot_nn(hidden, w_contract)
    layer_output = from_sequence((middle + contracted).astype(BF16), sequences)

    def adapter_back(u, grad, down, up):
        grad_up = dot_tn(narrow(u, down), grad)
        grad_narrow = dot_nt(grad, up).astype(BF16)
        return dot_tn(grad_narrow, u), grad_up

    grads = {}
    grads["contract"] = adapter_back(hidden, g_own, downs[3], ups[3])
    grad_hidden = dot_nt(g_own, w_contract)
    grad_expanded = (grad_hidden * gate * (1.0 + expanded * (1.0 - gate))).astype(BF16)
    grads["expand"] = adapter_back(normed_two, grad_expanded, downs[2], ups[2])
    grad_normed_two = dot_nt(grad_expanded, w_expand)
    grad_middle = g_own.astype(F32) + rms_back(middle, scale_two, grad_normed_two * gain_feedforward)
    grad_mixer = grad_middle.astype(BF16)
    grads["mixer"] = adapter_back(attended, grad_mixer, downs[1], ups[1])
    grad_attended = dot_nt(grad_mixer, w_mixer).astype(BF16)

    to_heads = jnp.swapaxes(grad_attended.reshape(rows, n_fs, unit), 0, 1)
    grad_heads = lax.all_to_all(to_heads, "fs", split_axis=0, concat_axis=0, tiled=True)
    if folds > 1:
        every = lax.all_gather(grad_heads, "sp", axis=0)
        every = every.reshape(folds, sequences, n_fs, rows, unit)
        every = lax.dynamic_index_in_dim(every, own_seq, 1, keepdims=False)
        grad_heads = jnp.swapaxes(every, 0, 1)
    grad_heads = grad_heads.reshape(length, unit)

    grad_qkv = attend_back(ends, aug, k, v, grad_heads, attended_heads, scale_pad, heads, head_dim)
    grad_joined = sections_out(grad_qkv)
    up_all = (
        ups[0].reshape(rank, 3, n_fs, unit).transpose(2, 0, 1, 3).reshape(n_fs, rank, 3 * unit)
    )
    narrow_one = narrow(normed_one, downs[0])
    grad_up = jnp.einsum("tr,htc->rhc", narrow_one, grad_joined, preferred_element_type=F32)
    grad_up = grad_up.reshape(rank, n_fs, 3, unit).transpose(0, 2, 1, 3).reshape(rank, 3 * model)
    grad_narrow = jnp.einsum("htc,hrc->tr", grad_joined, up_all, preferred_element_type=F32).astype(BF16)
    grads["qkv"] = (dot_tn(grad_narrow, normed_one), grad_up)
    grad_normed_one = jnp.einsum("htc,hdc->td", grad_joined, w_all, preferred_element_type=F32)
    input_grad = grad_middle + rms_back(x_f, scale_one, grad_normed_one * gain_attention)
    input_grad = from_sequence(input_grad.astype(BF16), sequences)

    stacked = jnp.concatenate(
        [g.reshape(-1, model) for name in ("qkv", "mixer", "expand", "contract") for g in grads[name]], axis=0
    )
    total_rows = stacked.shape[0]
    pieces = lax.all_to_all(
        stacked.reshape(n_fs, total_rows // n_fs, model), "fs", split_axis=0, concat_axis=0, tiled=True
    )
    summed = jnp.sum(pieces, axis=0)
    every = lax.all_gather(summed, ("fs", "sp"), axis=0)
    every = every.reshape(n_fs, folds, sequences, total_rows // n_fs, model)
    every = jnp.sum(every, axis=1)
    factor = 1.0 / math.sqrt(length)
    tables = []
    for a in range(adapters):
        table = jnp.zeros(every.shape[:1] + every.shape[2:], F32)
        for s in range(sequences):
            table = table + jnp.where(adapter_index[s, 0] == a, every[:, s], 0.0)
        tables.append(table.reshape(total_rows, model) * factor)
    tables = jnp.stack(tables)
    outs = []
    first = 0
    for wide in (3, 1, 1, 1):
        outs.append(jnp.swapaxes(tables[:, first : first + rank], 1, 2))
        first += rank
        outs.append(tables[:, first : first + rank * wide].reshape(adapters, rank, wide * model))
        first += rank * wide
    return (layer_output, input_grad, *outs)


def solution(mesh):
    tokens = P(None, ("fs", "sp"), None)
    in_specs = (tokens, tokens) + (P(),) * 5 + (P(None, "fs"),) * 4 + (P(),) * 8
    out_specs = (tokens, tokens) + (P(),) * 8
    return jax.shard_map(local, mesh=mesh, in_specs=in_specs, out_specs=out_specs, check_vma=False)
```

```python
import functools
import math

import jax
import jax.numpy as jnp
from jax import lax
from jax.experimental import pallas as pl
from jax.experimental.pallas import tpu as pltpu
from jax.sharding import PartitionSpec as P

EPSILON = 1e-06
BIG = 1e30
LANES = 128
PARTS = 3
TILE = 256
VMEM_LIMIT = 64000000
F32 = jnp.float32
BF16 = jnp.bfloat16
NT = (((1,), (1,)), ((), ()))
TN = (((0,), (0,)), ((), ()))


def dot_nn(a, b):
    return jnp.dot(a, b, preferred_element_type=F32)


def dot_nt(a, b):
    return lax.dot_general(a, b, NT, preferred_element_type=F32)


def dot_tn(a, b):
    return lax.dot_general(a, b, TN, preferred_element_type=F32)


def xor_permute(value, axis, mask):
    count = lax.axis_size(axis)
    return lax.ppermute(value, axis, [(a, a ^ mask) for a in range(count)])


def piece_of(stacked, index):
    return lax.dynamic_index_in_dim(stacked, index, 0, keepdims=False)


def project_kernel(sections, x_ref, gain_ref, w_ref, scale_ref, qpad_ref, kpad_ref, *refs, heads, head_dim):
    q_ref, k_ref, v_ref = refs[-3:]
    x = x_ref[0].astype(F32)
    mean = jnp.mean(x * x, axis=-1, keepdims=True)
    normed = (x * lax.rsqrt(mean + EPSILON) * gain_ref[...]).astype(BF16)
    rows = dot_nn(normed, w_ref[...]) * scale_ref[...]
    width = heads * LANES
    lane = lax.broadcasted_iota(jnp.int32, (1, width), 1) % LANES
    q_ref[...] = (rows[:, :width] + jnp.tile(qpad_ref[...].astype(F32), (1, heads))).astype(BF16)
    k_ref[...] = (rows[:, width : 2 * width] + jnp.tile(kpad_ref[...].astype(F32), (1, heads))).astype(BF16)
    ones = jnp.where((lane >= head_dim) & (lane < head_dim + PARTS), 1.0, 0.0)
    v_ref[...] = (rows[:, 2 * width :] + ones).astype(BF16)


def project(blocks, sections, gain, weight, scale, qpad, kpad, earlier, heads, head_dim, length):
    count, rows, model = blocks.shape
    step = TILE
    per = rows // step
    width = heads * LANES
    out = pl.BlockSpec((step, width), lambda b, h, sec: (sec[b] * per + h, 0))
    pad = pl.BlockSpec((step, LANES), lambda b, h, sec: (sec[b] * per + h, 0))
    fixed = lambda shape: pl.BlockSpec(shape, lambda b, h, sec: (0,) * len(shape))
    in_specs = [
        pl.BlockSpec((1, step, model), lambda b, h, sec: (b, h, 0)),
        fixed((1, model)),
        fixed((model, 3 * width)),
        fixed((1, 3 * width)),
        pad,
        pad,
    ]
    operands = [blocks, gain, weight, scale, qpad, kpad]
    aliases = {}
    if earlier is not None:
        in_specs += [pl.BlockSpec(memory_space=pl.ANY)] * 3
        aliases = {1 + len(operands) + n: n for n in range(3)}
        operands += list(earlier)
    return pl.pallas_call(
        functools.partial(project_kernel, heads=heads, head_dim=head_dim),
        out_shape=[jax.ShapeDtypeStruct((length, width), BF16)] * 3,
        grid_spec=pltpu.PrefetchScalarGridSpec(
            num_scalar_prefetch=1, grid=(count, per), in_specs=in_specs, out_specs=[out] * 3
        ),
        input_output_aliases=aliases,
        compiler_params=pltpu.CompilerParams(vmem_limit_bytes=VMEM_LIMIT),
        cost_estimate=pl.CostEstimate(
            flops=2 * count * rows * model * 3 * width,
            bytes_accessed=2 * (count * rows * (model + 3 * width) + model * 3 * width),
            transcendentals=0,
        ),
        name="project",
    )(sections, *operands)


def spread(column, lane, first):
    high = column.astype(BF16).astype(F32)
    middle = (column - high).astype(BF16).astype(F32)
    last = column - high - middle
    return jnp.where(lane == first, high, jnp.where(lane == first + 1, middle, last))


def attend_kernel(starts, q_ref, k_ref, v_ref, o_ref, aug_ref, s_ref, *, heads, head_dim):
    step = pl.program_id(0)
    first = starts[step]
    tile = q_ref.shape[0]
    lane = lax.broadcasted_iota(jnp.int32, (1, LANES), 1)

    def cols(h):
        return pl.ds(h * LANES, LANES)

    def scores(block, masked):
        out = []
        rows = pl.ds(pl.multiple_of(block * tile, tile), tile)
        for h in range(heads):
            s = dot_nt(q_ref[:, cols(h)], k_ref[rows, cols(h)])
            if masked:
                s = jnp.where(
                    lax.broadcasted_iota(jnp.int32, (tile, tile), 1)
                    <= lax.broadcasted_iota(jnp.int32, (tile, tile), 0),
                    s,
                    -BIG,
                )
            s_ref[h, block - first] = s
            top = s[:, :LANES]
            for c in range(LANES, tile, LANES):
                top = jnp.maximum(top, s[:, c : c + LANES])
            out.append(top)
        return tuple(out)

    def first_pass(block, tops):
        return tuple(jnp.maximum(a, b) for a, b in zip(tops, scores(block, False)))

    tops = lax.fori_loop(first, step, first_pass, scores(step, True))
    peaks = [jnp.max(top, axis=-1, keepdims=True) for top in tops]

    def second_pass(block, totals):
        rows = pl.ds(pl.multiple_of(block * tile, tile), tile)
        out = []
        for h in range(heads):
            p = jnp.exp(s_ref[h, block - first] - peaks[h]).astype(BF16)
            out.append(totals[h] + dot_nn(p, v_ref[rows, cols(h)]))
        return tuple(out)

    zero = jnp.zeros((tile, LANES), F32)
    totals = lax.fori_loop(first, step + 1, second_pass, (zero,) * heads)
    parts = []
    for h in range(heads):
        total = totals[h][:, head_dim : head_dim + 1]
        parts.append((totals[h] / total)[:, :head_dim].astype(BF16))
        lse = -(peaks[h] + jnp.log(total))
        marks = (lane >= head_dim) & (lane < head_dim + PARTS)
        aug_ref[:, cols(h)] = jnp.where(
            marks, spread(lse, lane, head_dim), q_ref[:, cols(h)].astype(F32)
        ).astype(BF16)
    o_ref[...] = jnp.concatenate(parts, axis=1)


def attend(starts, q, k, v, heads, head_dim):
    length, width = q.shape
    blocks = length // TILE
    span = min(blocks, -(-2048 // TILE) + 1)
    row = lambda w: pl.BlockSpec((TILE, w), lambda n, st: (n, 0))
    whole = pl.BlockSpec((length, width), lambda n, st: (0, 0))
    return pl.pallas_call(
        functools.partial(attend_kernel, heads=heads, head_dim=head_dim),
        out_shape=[
            jax.ShapeDtypeStruct((length, heads * head_dim), BF16),
            jax.ShapeDtypeStruct((length, width), BF16),
        ],
        grid_spec=pltpu.PrefetchScalarGridSpec(
            num_scalar_prefetch=1,
            grid=(blocks,),
            in_specs=[row(width), whole, whole],
            out_specs=[row(heads * head_dim), row(width)],
            scratch_shapes=[pltpu.VMEM((heads, span, TILE, TILE), F32)],
        ),
        compiler_params=pltpu.CompilerParams(vmem_limit_bytes=VMEM_LIMIT),
        cost_estimate=pl.CostEstimate(
            flops=4 * heads * length * 1024 * LANES, bytes_accessed=10 * length * width, transcendentals=0
        ),
        name="attend",
    )(starts, q, k, v)


def attend_back_kernel(
    ends, aug_ref, k_ref, v_ref, g_ref, o_ref, scale_ref, d_ref, gaug_ref, dq_ref, dk_ref, dv_ref, *, heads, head_dim
):
    step = pl.program_id(0)
    tile = k_ref.shape[0]
    length = aug_ref.shape[0]
    lane = lax.broadcasted_iota(jnp.int32, (1, LANES), 1)

    def cols(h):
        return pl.ds(h * LANES, LANES)

    @pl.when(step == 0)
    def _():
        @pl.loop(0, length // tile)
        def _(n):
            rows = pl.ds(pl.multiple_of(n * tile, tile), tile)
            g = g_ref[rows, :]
            product = g.astype(F32) * o_ref[rows, :].astype(F32)
            for h in range(heads):
                own = slice(h * head_dim, (h + 1) * head_dim)
                delta = -jnp.sum(product[:, own], axis=-1, keepdims=True)
                mine = jnp.concatenate(
                    [g[:, own].astype(F32), jnp.zeros((tile, LANES - head_dim), F32)], axis=1
                )
                marks = (lane >= head_dim) & (lane < head_dim + PARTS)
                gaug_ref[rows, cols(h)] = jnp.where(
                    marks, spread(delta, lane, head_dim), mine
                ).astype(BF16)
            dq_ref[rows, :] = jnp.zeros((tile, heads * LANES), F32)

    dk_ref[...] = jnp.zeros_like(dk_ref)
    dv_ref[...] = jnp.zeros_like(dv_ref)

    def one(block, masked):
        rows = pl.ds(pl.multiple_of(block * tile, tile), tile)
        for h in range(heads):
            q = aug_ref[rows, cols(h)]
            g = gaug_ref[rows, cols(h)]
            k = k_ref[:, cols(h)]
            s = dot_nt(k, q)
            if masked:
                s = jnp.where(
                    lax.broadcasted_iota(jnp.int32, (tile, tile), 0)
                    <= lax.broadcasted_iota(jnp.int32, (tile, tile), 1),
                    s,
                    -BIG,
                )
            p = jnp.exp(s)
            d = dot_nt(v_ref[:, cols(h)], g)
            dv_ref[:, cols(h)] += dot_nn(p.astype(BF16), g)
            ds = (p * d).astype(BF16)
            dk_ref[:, cols(h)] += dot_nn(ds, q)
            dq_ref[rows, cols(h)] += dot_tn(ds, k)

    one(step, True)

    @pl.loop(step + 1, ends[step])
    def _(block):
        one(block, False)

    own = pl.ds(pl.multiple_of(step * tile, tile), tile)
    pieces = []
    for h in range(heads):
        dq = dq_ref[own, cols(h)].astype(BF16).astype(F32) * scale_ref[...]
        pieces.append(dq[:, :head_dim])
    for ref in (dk_ref, dv_ref):
        for h in range(heads):
            pieces.append(ref[:, h * LANES : h * LANES + head_dim])
    d_ref[...] = jnp.concatenate(pieces, axis=1).astype(BF16)


def attend_back(ends, aug, k, v, grad, attended, scale, heads, head_dim):
    length, width = aug.shape
    blocks = length // TILE
    row = lambda w: pl.BlockSpec((TILE, w), lambda n, st: (n, 0))
    whole = lambda w: pl.BlockSpec((length, w), lambda n, st: (0, 0))
    return pl.pallas_call(
        functools.partial(attend_back_kernel, heads=heads, head_dim=head_dim),
        out_shape=jax.ShapeDtypeStruct((length, 3 * heads * head_dim), BF16),
        grid_spec=pltpu.PrefetchScalarGridSpec(
            num_scalar_prefetch=1,
            grid=(blocks,),
            in_specs=[
                whole(width),
                row(width),
                row(width),
                whole(heads * head_dim),
                whole(heads * head_dim),
                pl.BlockSpec((1, LANES), lambda n, st: (0, 0)),
            ],
            out_specs=row(3 * heads * head_dim),
            scratch_shapes=[
                pltpu.VMEM((length, width), BF16),
                pltpu.VMEM((length, width), F32),
                pltpu.VMEM((TILE, width), F32),
                pltpu.VMEM((TILE, width), F32),
            ],
        ),
        compiler_params=pltpu.CompilerParams(vmem_limit_bytes=VMEM_LIMIT),
        cost_estimate=pl.CostEstimate(
            flops=10 * heads * length * 1024 * LANES, bytes_accessed=14 * length * width, transcendentals=0
        ),
        name="attend_back",
    )(ends, aug, k, v, grad, attended, scale)


def rms_scale(values):
    return lax.rsqrt(jnp.mean(values * values, axis=-1, keepdims=True) + EPSILON)


def rms_back(values, scale_rows, grad_normed):
    cubed = scale_rows * scale_rows * scale_rows
    return scale_rows * grad_normed - values * cubed * jnp.mean(
        grad_normed * values, axis=-1, keepdims=True
    )


def after(value, *others):
    return lax.optimization_barrier((value, others))[0]


def together(*values):
    return lax.optimization_barrier(values)


def own_and_sent(value, own, masks):
    return [
        piece_of(value, own) if m == 0 else xor_permute(piece_of(value, own ^ m), "sp", m) for m in masks
    ]


def in_order(pieces, own):
    stacked = jnp.stack(pieces)
    return jnp.stack([piece_of(stacked, n ^ own) for n in range(len(pieces))], axis=0)


def summed_share(part, fs, n_fs):
    mask = n_fs >> 1
    while mask:
        half = part.shape[0] // 2
        upper = (fs & mask) != 0
        keep = jnp.where(upper, part[half:], part[:half])
        send = jnp.where(upper, part[:half], part[half:])
        part = keep + xor_permute(send, "fs", mask)
        mask >>= 1
    return part


def folded(part, adapter_index, adapters, own, groups, n_sp):
    mask = groups
    while mask < n_sp:
        part = part + xor_permute(part, "sp", mask)
        mask <<= 1
    by_seq = in_order([part] + [xor_permute(part, "sp", m) for m in range(1, groups)], own)
    tables = []
    for a in range(adapters):
        table = jnp.zeros_like(part)
        for s in range(groups):
            table = table + jnp.where(adapter_index[s, 0] == a, by_seq[s], 0.0)
        tables.append(table)
    return jnp.stack(tables)


def doubled(table, fs, n_fs):
    every = table[None]
    mask = 1
    while mask < n_fs:
        other = xor_permute(every, "fs", mask)
        upper = (fs & mask) != 0
        every = jnp.where(
            upper, jnp.concatenate([other, every], axis=0), jnp.concatenate([every, other], axis=0)
        )
        mask <<= 1
    return every


def joined_rows(every):
    n, adapters, rows, model = every.shape
    return jnp.swapaxes(every, 0, 1).reshape(adapters, n * rows, model)


def local(
    layer_input,
    output_grad,
    segment_ids,
    adapter_index,
    gain_attention,
    gain_feedforward,
    query_scale,
    weight_qkv,
    weight_mixer,
    weight_expand,
    weight_contract,
    qkv_down,
    qkv_up,
    mixer_down,
    mixer_up,
    expand_down,
    expand_up,
    contract_down,
    contract_up,
):
    sequences, tokens, model = layer_input.shape
    head_dim = query_scale.shape[0]
    n_fs, n_sp = lax.axis_size("fs"), lax.axis_size("sp")
    adapters, rank = qkv_down.shape[0], qkv_down.shape[2]
    length = segment_ids.shape[1]
    folds = n_sp // sequences
    heads = model // head_dim // n_fs
    unit = heads * head_dim
    width = heads * LANES
    rows = sequences * tokens
    fs = lax.axis_index("fs")
    sp = lax.axis_index("sp")
    own = sp % sequences
    fold = sp // sequences

    pick = piece_of(adapter_index, own)[0]
    downs = [piece_of(t, pick) for t in (qkv_down, mixer_down, expand_down, contract_down)]
    ups = [piece_of(t, pick) for t in (qkv_up, mixer_up, expand_up, contract_up)]

    def merged(weight, down, up):
        cols = weight.shape[1]
        own_up = lax.dynamic_slice_in_dim(up, fs * cols, cols, 1)
        return (weight.astype(F32) + dot_nn(down, own_up)).astype(BF16)

    shard = merged(weight_qkv, downs[0], ups[0])
    inverse = pow(3, -1, n_fs)
    received = [
        lax.ppermute(
            shard[:, t * unit : (t + 1) * unit], "fs", [(d, (3 * d + t) % n_fs) for d in range(n_fs)]
        )
        for t in range(3)
    ]
    places = [(3 * ((inverse * (fs - t)) % n_fs) + t) // n_fs for t in range(3)]
    w_parts = []
    for b in range(3):
        part = jnp.zeros_like(received[0])
        for t in range(3):
            part = jnp.where(places[t] == b, received[t], part)
        w_parts.append(part)
    w_own = jnp.concatenate(w_parts, axis=1)
    w_padded = jnp.pad(
        w_own.reshape(model, 3 * heads, head_dim), ((0, 0), (0, 0), (0, LANES - head_dim))
    ).reshape(model, 3 * width)

    segs = piece_of(segment_ids, own)
    scale = query_scale * (1.0 / math.sqrt(head_dim))
    scale_pad = jnp.pad(scale, (0, LANES - head_dim))[None]
    col_scale = jnp.concatenate([jnp.tile(scale_pad, (1, heads)), jnp.ones((1, 2 * width), F32)], axis=1)
    lane = jnp.arange(LANES)[None, :]
    marks = lane >= head_dim + PARTS
    same = lane == segs[:, None] + (head_dim + PARTS)
    qpad = same.astype(BF16)
    kpad = jnp.where(
        marks, jnp.where(same, 0.0, -BIG), jnp.where(lane >= head_dim, 1.0, 0.0)
    ).astype(BF16)

    project_args = (gain_attention[None], w_padded, col_scale, qpad, kpad)
    as_table = lambda *s: jnp.stack(s).astype(jnp.int32)
    if n_fs == 8 and folds == 1 and sequences == 4 and 2 * tokens == TILE:
        pieces = own_and_sent(layer_input, own, (0, 1))
        pieces += own_and_sent(after(layer_input, pieces[1]), own, (2, 3))
        odd = own % 2 == 1
        upper = own // 2

        def pair(low, high):
            return jnp.where(odd, jnp.concatenate([high, low], 0), jnp.concatenate([low, high], 0))

        def arrivals(chunk):
            half = chunk.shape[0] // 2
            by_y = xor_permute(chunk, "fs", 4)
            by_x = xor_permute(chunk, "fs", 2)
            core = xor_permute(chunk, "fs", 1)
            top = xor_permute(by_y[:half], "fs", 2)
            bottom = xor_permute(by_x[half:], "fs", 4)
            core_y = xor_permute(by_y, "fs", 1)
            core_x = xor_permute(by_x, "fs", 1)
            both = jnp.concatenate([top, bottom], axis=0)
            core_both = xor_permute(both, "fs", 1)
            return [
                (0, chunk), (1, core), (4, by_y), (2, by_x), (5, core_y), (3, core_x), (6, both), (7, core_both)
            ]

        first = pair(pieces[0], pieces[1])
        second = pair(pieces[2], pieces[3])
        x_own = jnp.where(
            upper == 0, jnp.concatenate([first, second], 0), jnp.concatenate([second, first], 0)
        )
        come_first = arrivals(first)
        come_second = arrivals(after(second, come_first[2][1], come_first[3][1]))
        qkv = None
        for come, place in ((come_first, upper), (come_second, 1 - upper)):
            for mask, block in come:
                qkv = project(
                    block[None], as_table((fs ^ mask) * 2 + place), *project_args, qkv, heads, head_dim, length
                )
        x_sent, x_here = (pieces[2], pieces[3]), (come_second[6][1],)
    else:
        pieces = own_and_sent(layer_input, own, range(sequences))
        x_own = in_order(pieces, own).reshape(rows, model)
        gathered = lax.all_gather(x_own, ("fs", "sp"), axis=0)
        gathered = gathered.reshape(n_fs, folds, sequences, rows, model)
        gathered = lax.dynamic_index_in_dim(gathered, own, 2, keepdims=False)
        blocks = gathered.reshape(n_fs * folds, rows, model)
        qkv = project(
            blocks, jnp.arange(n_fs * folds, dtype=jnp.int32), *project_args, None, heads, head_dim, length
        )
        x_sent, x_here = (x_own,), (blocks,)
    q, k, v = qkv

    three = jnp.stack(
        [
            merged(w, d, u).T
            for w, d, u in zip((weight_mixer, weight_expand, weight_contract), downs[1:], ups[1:])
        ]
    )
    w_mixer, w_expand, w_contract = lax.all_gather(after(three, *x_here), "fs", axis=1, tiled=True)
    g_pieces = own_and_sent(after(output_grad, *x_sent), own, range(sequences))

    firsts, lasts = segs[::TILE], segs[TILE - 1 :: TILE]
    starts = jnp.sum(segs[None, :] < firsts[:, None], axis=1, dtype=jnp.int32) // TILE
    ends = (jnp.sum(segs[None, :] <= lasts[:, None], axis=1, dtype=jnp.int32) + TILE - 1) // TILE

    attended_heads, aug = attend(starts, q, k, v, heads, head_dim)
    attended_heads, *g_pieces = together(attended_heads, *g_pieces)

    def sections_out(value):
        if folds == 1:
            mine = value.reshape(n_fs, rows, value.shape[1])
        else:
            cut = value.reshape(n_fs, folds, rows, value.shape[1])
            mine = lax.dynamic_index_in_dim(cut, fold, 1, keepdims=False)
        return lax.all_to_all(mine, "fs", split_axis=0, concat_axis=0, tiled=True)

    attended = jnp.swapaxes(sections_out(attended_heads), 0, 1).reshape(rows, model)
    g_own = in_order(g_pieces, own).reshape(rows, model)

    x_f = x_own.astype(F32)
    scale_one = rms_scale(x_f)
    normed_one = (x_f * scale_one * gain_attention).astype(BF16)
    narrow = lambda u, down: dot_nn(u, down).astype(BF16)
    mixer = dot_nt(attended, w_mixer)
    middle = x_f + mixer
    scale_two = rms_scale(middle)
    normed_two = (middle * scale_two * gain_feedforward).astype(BF16)
    expanded = dot_nt(normed_two, w_expand)
    gate = jax.nn.sigmoid(expanded)
    hidden = (expanded * gate).astype(BF16)
    contracted = dot_nt(hidden, w_contract)
    layer_output = (middle + contracted).astype(BF16).reshape(sequences, tokens, model)

    def adapter_back(u, grad, down, up):
        grad_up = dot_tn(narrow(u, down), grad)
        grad_narrow = dot_nt(grad, up).astype(BF16)
        return [dot_tn(grad_narrow, u), grad_up]

    grad_hidden = dot_nn(g_own, w_contract)
    grad_expanded = (grad_hidden * gate * (1.0 + expanded * (1.0 - gate))).astype(BF16)
    grad_normed_two = dot_nn(grad_expanded, w_expand)
    grad_middle = g_own.astype(F32) + rms_back(middle, scale_two, grad_normed_two * gain_feedforward)
    grad_mixer = grad_middle.astype(BF16)
    grad_attended = dot_nn(grad_mixer, w_mixer).astype(BF16)

    to_heads = jnp.swapaxes(grad_attended.reshape(rows, n_fs, unit), 0, 1)
    grad_heads = lax.all_to_all(to_heads, "fs", split_axis=0, concat_axis=0, tiled=True)
    if folds > 1:
        every = lax.all_gather(grad_heads, "sp", axis=0)
        every = every.reshape(folds, sequences, n_fs, rows, unit)
        every = lax.dynamic_index_in_dim(every, own, 1, keepdims=False)
        grad_heads = jnp.swapaxes(every, 0, 1)
    grad_heads = grad_heads.reshape(length, unit)

    early = jnp.concatenate(
        adapter_back(attended, grad_mixer, downs[1], ups[1])
        + adapter_back(normed_two, grad_expanded, downs[2], ups[2])
        + adapter_back(hidden, g_own, downs[3], ups[3]),
        axis=0,
    )
    grad_heads, early = together(grad_heads, early)
    w_all = lax.all_gather(after(w_own.T, grad_heads), "fs", axis=0)
    early = lax.all_to_all(
        early.reshape(n_fs, early.shape[0] // n_fs, model), "fs", split_axis=0, concat_axis=0, tiled=True
    )
    out_pieces = own_and_sent(after(layer_output, grad_heads), own, range(sequences))

    grad_qkv = attend_back(ends, aug, k, v, grad_heads, attended_heads, scale_pad, heads, head_dim)
    grad_qkv, early, *out_pieces = together(grad_qkv, early, *out_pieces)
    grad_joined = sections_out(grad_qkv)
    early = folded(jnp.sum(early, axis=0), adapter_index, adapters, own, sequences, n_sp)
    early = lax.all_gather(early, "fs", axis=0)
    layer_output = in_order(out_pieces, own)

    up_all = (
        ups[0].reshape(rank, 3, n_fs, unit).transpose(2, 0, 1, 3).reshape(n_fs, rank, 3 * unit)
    )
    narrow_one = narrow(normed_one, downs[0])
    grad_up = jnp.einsum("tr,htc->rhc", narrow_one, grad_joined, preferred_element_type=F32)
    grad_up = grad_up.reshape(rank, n_fs, 3, unit).transpose(0, 2, 1, 3).reshape(3 * rank, model)
    grad_narrow = jnp.einsum("htc,hrc->tr", grad_joined, up_all, preferred_element_type=F32).astype(BF16)
    late = jnp.concatenate([dot_tn(grad_narrow, normed_one), grad_up], axis=0)
    grad_joined, late = together(grad_joined, late)
    late = folded(summed_share(late, fs, n_fs), adapter_index, adapters, own, sequences, n_sp)
    late = doubled(late, fs, n_fs)

    grad_normed_one = jnp.einsum("htc,hcd->td", grad_joined, w_all, preferred_element_type=F32)
    input_grad = grad_middle + rms_back(x_f, scale_one, grad_normed_one * gain_attention)
    input_grad = input_grad.astype(BF16).reshape(sequences, tokens, model)
    input_grad = in_order(own_and_sent(input_grad, own, range(sequences)), own)

    factor = 1.0 / math.sqrt(length)
    outs = []
    late, early = joined_rows(late) * factor, joined_rows(early) * factor
    for tables, wides in ((late, (3,)), (early, (1, 1, 1))):
        first = 0
        for wide in wides:
            outs.append(jnp.swapaxes(tables[:, first : first + rank], 1, 2))
            first += rank
            outs.append(tables[:, first : first + rank * wide].reshape(adapters, rank, wide * model))
            first += rank * wide
    return (layer_output, input_grad, *outs)


def solution(mesh):
    tokens = P(None, ("fs", "sp"), None)
    in_specs = (tokens, tokens) + (P(),) * 5 + (P(None, "fs"),) * 4 + (P(),) * 8
    out_specs = (tokens, tokens) + (P(),) * 8
    return jax.shard_map(local, mesh=mesh, in_specs=in_specs, out_specs=out_specs, check_vma=False)
```

```python
import functools
import math

import jax
import jax.numpy as jnp
from jax import lax
from jax.experimental import pallas as pl
from jax.experimental.pallas import tpu as pltpu
from jax.sharding import PartitionSpec as P

EPSILON = 1e-06
BIG = 1e30
LANES = 128
PARTS = 3
TILE = 256
VMEM_LIMIT = 64000000
F32 = jnp.float32
BF16 = jnp.bfloat16
NT = (((1,), (1,)), ((), ()))
TN = (((0,), (0,)), ((), ()))


def dot_nn(a, b):
    return jnp.dot(a, b, preferred_element_type=F32)


def dot_nt(a, b):
    return lax.dot_general(a, b, NT, preferred_element_type=F32)


def dot_tn(a, b):
    return lax.dot_general(a, b, TN, preferred_element_type=F32)


def xor_permute(value, axis, mask):
    count = lax.axis_size(axis)
    return lax.ppermute(value, axis, [(a, a ^ mask) for a in range(count)])


def piece_of(stacked, index):
    return lax.dynamic_index_in_dim(stacked, index, 0, keepdims=False)


def project_kernel(tiles, *refs, count, heads, head_dim):
    x_refs, (gain_ref, w_ref, scale_ref, qpad_ref, kpad_ref) = refs[:count], refs[count : count + 5]
    q_ref, k_ref, v_ref, x_ref = refs[-4:]
    if count > 1:
        for n in range(count):

            @pl.when(pl.program_id(0) == n)
            def _():
                x_ref[...] = x_refs[n][...]

        x = x_ref[...].astype(F32)
    else:
        x = x_refs[0][0].astype(F32)
    mean = jnp.mean(x * x, axis=-1, keepdims=True)
    normed = (x * lax.rsqrt(mean + EPSILON) * gain_ref[...]).astype(BF16)
    rows = dot_nn(normed, w_ref[...]) * scale_ref[...]
    width = heads * LANES
    lane = lax.broadcasted_iota(jnp.int32, (1, width), 1) % LANES
    q_ref[...] = (rows[:, :width] + jnp.tile(qpad_ref[...].astype(F32), (1, heads))).astype(BF16)
    k_ref[...] = (rows[:, width : 2 * width] + jnp.tile(kpad_ref[...].astype(F32), (1, heads))).astype(BF16)
    ones = jnp.where((lane >= head_dim) & (lane < head_dim + PARTS), 1.0, 0.0)
    v_ref[...] = (rows[:, 2 * width :] + ones).astype(BF16)


def project(sources, tiles, gain, weight, scale, qpad, kpad, earlier, heads, head_dim, length):
    model = weight.shape[0]
    step = TILE
    count = len(sources)
    steps = tiles.shape[0]
    width = heads * LANES
    out = pl.BlockSpec((step, width), lambda n, t: (t[n], 0))
    pad = pl.BlockSpec((step, LANES), lambda n, t: (t[n], 0))
    fixed = lambda shape: pl.BlockSpec(shape, lambda n, t: (0,) * len(shape))
    if count > 1:
        in_specs = [fixed((step, model))] * count
    else:
        per = sources[0].shape[1] // step
        in_specs = [pl.BlockSpec((1, step, model), lambda n, t: (n // per, n % per, 0))]
    in_specs += [fixed((1, model)), fixed((model, 3 * width)), fixed((1, 3 * width)), pad, pad]
    operands = [*sources, gain, weight, scale, qpad, kpad]
    aliases = {}
    if earlier is not None:
        in_specs += [pl.BlockSpec(memory_space=pl.ANY)] * 3
        aliases = {1 + len(operands) + n: n for n in range(3)}
        operands += list(earlier)
    return pl.pallas_call(
        functools.partial(project_kernel, count=count, heads=heads, head_dim=head_dim),
        out_shape=[jax.ShapeDtypeStruct((length, width), BF16)] * 3,
        grid_spec=pltpu.PrefetchScalarGridSpec(
            num_scalar_prefetch=1,
            grid=(steps,),
            in_specs=in_specs,
            out_specs=[out] * 3,
            scratch_shapes=[pltpu.VMEM((step, model), BF16)],
        ),
        input_output_aliases=aliases,
        compiler_params=pltpu.CompilerParams(vmem_limit_bytes=VMEM_LIMIT),
        cost_estimate=pl.CostEstimate(
            flops=6 * steps * step * model * 3 * width,
            bytes_accessed=2 * (steps * step * (model + 3 * width) + model * 3 * width),
            transcendentals=0,
        ),
        name="project",
    )(tiles, *operands)


def spread(column, lane, first):
    high = column.astype(BF16).astype(F32)
    middle = (column - high).astype(BF16).astype(F32)
    last = column - high - middle
    return jnp.where(lane == first, high, jnp.where(lane == first + 1, middle, last))


def attend_kernel(starts, q_ref, k_ref, v_ref, o_ref, aug_ref, s_ref, *, heads, head_dim):
    step = pl.program_id(0)
    first = starts[step]
    tile = q_ref.shape[0]
    lane = lax.broadcasted_iota(jnp.int32, (1, LANES), 1)

    def cols(h):
        return pl.ds(h * LANES, LANES)

    def scores(block, masked):
        out = []
        rows = pl.ds(pl.multiple_of(block * tile, tile), tile)
        for h in range(heads):
            s = dot_nt(q_ref[:, cols(h)], k_ref[rows, cols(h)])
            if masked:
                s = jnp.where(
                    lax.broadcasted_iota(jnp.int32, (tile, tile), 1)
                    <= lax.broadcasted_iota(jnp.int32, (tile, tile), 0),
                    s,
                    -BIG,
                )
            s_ref[h, block - first] = s
            top = s[:, :LANES]
            for c in range(LANES, tile, LANES):
                top = jnp.maximum(top, s[:, c : c + LANES])
            out.append(top)
        return tuple(out)

    def first_pass(block, tops):
        return tuple(jnp.maximum(a, b) for a, b in zip(tops, scores(block, False)))

    tops = lax.fori_loop(first, step, first_pass, scores(step, True))
    peaks = [jnp.max(top, axis=-1, keepdims=True) for top in tops]

    def second_pass(block, totals):
        rows = pl.ds(pl.multiple_of(block * tile, tile), tile)
        out = []
        for h in range(heads):
            p = jnp.exp(s_ref[h, block - first] - peaks[h]).astype(BF16)
            out.append(totals[h] + dot_nn(p, v_ref[rows, cols(h)]))
        return tuple(out)

    zero = jnp.zeros((tile, LANES), F32)
    totals = lax.fori_loop(first, step + 1, second_pass, (zero,) * heads)
    parts = []
    for h in range(heads):
        total = totals[h][:, head_dim : head_dim + 1]
        parts.append((totals[h] / total)[:, :head_dim].astype(BF16))
        lse = -(peaks[h] + jnp.log(total))
        marks = (lane >= head_dim) & (lane < head_dim + PARTS)
        aug_ref[:, cols(h)] = jnp.where(
            marks, spread(lse, lane, head_dim), q_ref[:, cols(h)].astype(F32)
        ).astype(BF16)
    o_ref[...] = jnp.concatenate(parts, axis=1)


def attend(starts, q, k, v, heads, head_dim):
    length, width = q.shape
    blocks = length // TILE
    span = min(blocks, -(-2048 // TILE) + 1)
    row = lambda w: pl.BlockSpec((TILE, w), lambda n, st: (n, 0))
    whole = pl.BlockSpec((length, width), lambda n, st: (0, 0))
    return pl.pallas_call(
        functools.partial(attend_kernel, heads=heads, head_dim=head_dim),
        out_shape=[
            jax.ShapeDtypeStruct((length, heads * head_dim), BF16),
            jax.ShapeDtypeStruct((length, width), BF16),
        ],
        grid_spec=pltpu.PrefetchScalarGridSpec(
            num_scalar_prefetch=1,
            grid=(blocks,),
            in_specs=[row(width), whole, whole],
            out_specs=[row(heads * head_dim), row(width)],
            scratch_shapes=[pltpu.VMEM((heads, span, TILE, TILE), F32)],
        ),
        compiler_params=pltpu.CompilerParams(vmem_limit_bytes=VMEM_LIMIT),
        cost_estimate=pl.CostEstimate(
            flops=40 * heads * length * 1024 * LANES, bytes_accessed=10 * length * width, transcendentals=0
        ),
        name="attend",
    )(starts, q, k, v)


def attend_back_kernel(
    ends, aug_ref, k_ref, v_ref, g_ref, o_ref, scale_ref, d_ref, gaug_ref, dq_ref, dk_ref, dv_ref, *, heads, head_dim
):
    step = pl.program_id(0)
    tile = k_ref.shape[0]
    length = aug_ref.shape[0]
    lane = lax.broadcasted_iota(jnp.int32, (1, LANES), 1)

    def cols(h):
        return pl.ds(h * LANES, LANES)

    @pl.when(step == 0)
    def _():
        @pl.loop(0, length // tile)
        def _(n):
            rows = pl.ds(pl.multiple_of(n * tile, tile), tile)
            g = g_ref[rows, :]
            product = g.astype(F32) * o_ref[rows, :].astype(F32)
            for h in range(heads):
                own = slice(h * head_dim, (h + 1) * head_dim)
                delta = -jnp.sum(product[:, own], axis=-1, keepdims=True)
                mine = jnp.concatenate(
                    [g[:, own].astype(F32), jnp.zeros((tile, LANES - head_dim), F32)], axis=1
                )
                marks = (lane >= head_dim) & (lane < head_dim + PARTS)
                gaug_ref[rows, cols(h)] = jnp.where(
                    marks, spread(delta, lane, head_dim), mine
                ).astype(BF16)
            dq_ref[rows, :] = jnp.zeros((tile, heads * LANES), F32)

    dk_ref[...] = jnp.zeros_like(dk_ref)
    dv_ref[...] = jnp.zeros_like(dv_ref)

    def one(block, masked):
        rows = pl.ds(pl.multiple_of(block * tile, tile), tile)
        for h in range(heads):
            q = aug_ref[rows, cols(h)]
            g = gaug_ref[rows, cols(h)]
            k = k_ref[:, cols(h)]
            s = dot_nt(k, q)
            if masked:
                s = jnp.where(
                    lax.broadcasted_iota(jnp.int32, (tile, tile), 0)
                    <= lax.broadcasted_iota(jnp.int32, (tile, tile), 1),
                    s,
                    -BIG,
                )
            p = jnp.exp(s)
            d = dot_nt(v_ref[:, cols(h)], g)
            dv_ref[:, cols(h)] += dot_nn(p.astype(BF16), g)
            ds = (p * d).astype(BF16)
            dk_ref[:, cols(h)] += dot_nn(ds, q)
            dq_ref[rows, cols(h)] += dot_tn(ds, k)

    one(step, True)

    @pl.loop(step + 1, ends[step])
    def _(block):
        one(block, False)

    own = pl.ds(pl.multiple_of(step * tile, tile), tile)
    pieces = []
    for h in range(heads):
        dq = dq_ref[own, cols(h)].astype(BF16).astype(F32) * scale_ref[...]
        pieces.append(dq[:, :head_dim])
    for ref in (dk_ref, dv_ref):
        for h in range(heads):
            pieces.append(ref[:, h * LANES : h * LANES + head_dim])
    d_ref[...] = jnp.concatenate(pieces, axis=1).astype(BF16)


def attend_back(ends, aug, k, v, grad, attended, scale, heads, head_dim):
    length, width = aug.shape
    blocks = length // TILE
    row = lambda w: pl.BlockSpec((TILE, w), lambda n, st: (n, 0))
    whole = lambda w: pl.BlockSpec((length, w), lambda n, st: (0, 0))
    return pl.pallas_call(
        functools.partial(attend_back_kernel, heads=heads, head_dim=head_dim),
        out_shape=jax.ShapeDtypeStruct((length, 3 * heads * head_dim), BF16),
        grid_spec=pltpu.PrefetchScalarGridSpec(
            num_scalar_prefetch=1,
            grid=(blocks,),
            in_specs=[
                whole(width),
                row(width),
                row(width),
                whole(heads * head_dim),
                whole(heads * head_dim),
                pl.BlockSpec((1, LANES), lambda n, st: (0, 0)),
            ],
            out_specs=row(3 * heads * head_dim),
            scratch_shapes=[
                pltpu.VMEM((length, width), BF16),
                pltpu.VMEM((length, width), F32),
                pltpu.VMEM((TILE, width), F32),
                pltpu.VMEM((TILE, width), F32),
            ],
        ),
        compiler_params=pltpu.CompilerParams(vmem_limit_bytes=VMEM_LIMIT),
        cost_estimate=pl.CostEstimate(
            flops=60 * heads * length * 1024 * LANES, bytes_accessed=14 * length * width, transcendentals=0
        ),
        name="attend_back",
    )(ends, aug, k, v, grad, attended, scale)


def rms_scale(values):
    return lax.rsqrt(jnp.mean(values * values, axis=-1, keepdims=True) + EPSILON)


def rms_back(values, scale_rows, grad_normed):
    cubed = scale_rows * scale_rows * scale_rows
    return scale_rows * grad_normed - values * cubed * jnp.mean(
        grad_normed * values, axis=-1, keepdims=True
    )


def after(value, *others):
    return lax.optimization_barrier((value, others))[0]


def together(*values):
    return lax.optimization_barrier(values)


def own_and_sent(value, own, masks):
    return [
        piece_of(value, own) if m == 0 else xor_permute(piece_of(value, own ^ m), "sp", m) for m in masks
    ]


def in_order(pieces, own):
    stacked = jnp.stack(pieces)
    return jnp.stack([piece_of(stacked, n ^ own) for n in range(len(pieces))], axis=0)


def direct_shares(part, n_fs):
    fs = lax.axis_index("fs")
    split = part.reshape(n_fs, part.shape[0] // n_fs, part.shape[1])
    return [
        piece_of(split, fs) if m == 0 else xor_permute(piece_of(split, fs ^ m), "fs", m) for m in range(n_fs)
    ]


def over_sequences(part, groups, n_sp):
    mask = groups
    while mask < n_sp:
        part = part + xor_permute(part, "sp", mask)
        mask <<= 1
    return [part] + [xor_permute(part, "sp", m) for m in range(1, groups)]


def fold(pieces, adapter_index, adapters, own):
    by_seq = in_order(pieces, own)
    tables = []
    for a in range(adapters):
        table = jnp.zeros_like(pieces[0])
        for s in range(len(pieces)):
            table = table + jnp.where(adapter_index[s, 0] == a, by_seq[s], 0.0)
        tables.append(table)
    return jnp.stack(tables)


def joined_rows(every):
    n, adapters, rows, model = every.shape
    return jnp.swapaxes(every, 0, 1).reshape(adapters, n * rows, model)


def local(
    layer_input,
    output_grad,
    segment_ids,
    adapter_index,
    gain_attention,
    gain_feedforward,
    query_scale,
    weight_qkv,
    weight_mixer,
    weight_expand,
    weight_contract,
    qkv_down,
    qkv_up,
    mixer_down,
    mixer_up,
    expand_down,
    expand_up,
    contract_down,
    contract_up,
):
    sequences, tokens, model = layer_input.shape
    head_dim = query_scale.shape[0]
    n_fs, n_sp = lax.axis_size("fs"), lax.axis_size("sp")
    adapters, rank = qkv_down.shape[0], qkv_down.shape[2]
    length = segment_ids.shape[1]
    folds = n_sp // sequences
    heads = model // head_dim // n_fs
    unit = heads * head_dim
    width = heads * LANES
    rows = sequences * tokens
    fs = lax.axis_index("fs")
    sp = lax.axis_index("sp")
    own = sp % sequences
    fold_of = sp // sequences

    pick = piece_of(adapter_index, own)[0]
    downs = [piece_of(t, pick) for t in (qkv_down, mixer_down, expand_down, contract_down)]
    ups = [piece_of(t, pick) for t in (qkv_up, mixer_up, expand_up, contract_up)]

    def merged(weight, down, up):
        cols = weight.shape[1]
        own_up = lax.dynamic_slice_in_dim(up, fs * cols, cols, 1)
        return (weight.astype(F32) + dot_nn(down, own_up)).astype(BF16)

    shard = merged(weight_qkv, downs[0], ups[0])
    inverse = pow(3, -1, n_fs)
    received = [
        lax.ppermute(
            shard[:, t * unit : (t + 1) * unit], "fs", [(d, (3 * d + t) % n_fs) for d in range(n_fs)]
        )
        for t in range(3)
    ]
    places = [(3 * ((inverse * (fs - t)) % n_fs) + t) // n_fs for t in range(3)]
    w_parts = []
    for b in range(3):
        part = jnp.zeros_like(received[0])
        for t in range(3):
            part = jnp.where(places[t] == b, received[t], part)
        w_parts.append(part)
    w_own = jnp.concatenate(w_parts, axis=1)
    w_padded = jnp.pad(
        w_own.reshape(model, 3 * heads, head_dim), ((0, 0), (0, 0), (0, LANES - head_dim))
    ).reshape(model, 3 * width)

    segs = piece_of(segment_ids, own)
    scale = query_scale * (1.0 / math.sqrt(head_dim))
    scale_pad = jnp.pad(scale, (0, LANES - head_dim))[None]
    col_scale = jnp.concatenate([jnp.tile(scale_pad, (1, heads)), jnp.ones((1, 2 * width), F32)], axis=1)
    lane = jnp.arange(LANES)[None, :]
    marks = lane >= head_dim + PARTS
    same = lane == segs[:, None] + (head_dim + PARTS)
    qpad = same.astype(BF16)
    kpad = jnp.where(
        marks, jnp.where(same, 0.0, -BIG), jnp.where(lane >= head_dim, 1.0, 0.0)
    ).astype(BF16)

    project_args = (gain_attention[None], w_padded, col_scale, qpad, kpad)
    as_table = lambda *s: jnp.stack(s).astype(jnp.int32)
    if n_fs == 8 and folds == 1 and sequences == 4 and 2 * tokens == TILE:
        pieces = own_and_sent(layer_input, own, (0, 1))
        pieces += own_and_sent(after(layer_input, pieces[1]), own, (2, 3))
        odd = own % 2 == 1
        upper = own // 2

        def pair(low, high):
            return jnp.where(odd, jnp.concatenate([high, low], 0), jnp.concatenate([low, high], 0))

        def to(value, mask):
            return xor_permute(value, "fs", mask)

        def fill(blocks, place, earlier):
            sources = [block for _, block in blocks]
            tiles = as_table(*[(fs ^ mask) * 2 + place for mask, _ in blocks])
            return project(sources, tiles, *project_args, earlier, heads, head_dim, length)

        other = 1 - upper
        first = pair(pieces[0], pieces[1])
        half = TILE // 2
        y1, x1, c1 = to(first, 4), to(first, 2), to(first, 1)
        y1, x1, c1 = together(y1, x1, c1)
        top1, bottom1, cy1, cx1 = to(y1[:half], 2), to(x1[half:], 4), to(y1, 1), to(x1, 1)
        qkv = fill([(0, first), (1, c1), (4, y1), (2, x1)], upper, None)
        *qkv, top1, bottom1, cy1, cx1, p2, p3 = together(*qkv, top1, bottom1, cy1, cx1, pieces[2], pieces[3])
        both1 = jnp.concatenate([top1, bottom1], axis=0)
        second = pair(p2, p3)
        y2, x2, c2, cb1 = to(second, 4), to(second, 2), to(second, 1), to(both1, 1)
        qkv = fill([(5, cy1), (3, cx1)], upper, qkv)
        *qkv, y2, x2, c2, cb1 = together(*qkv, y2, x2, c2, cb1)
        top2, bottom2, cy2, cx2 = to(y2[:half], 2), to(x2[half:], 4), to(y2, 1), to(x2, 1)
        qkv = fill([(6, both1), (7, cb1)], upper, qkv)
        qkv = fill([(0, second), (1, c2)], other, qkv)
        *qkv, top2, bottom2, cy2, cx2 = together(*qkv, top2, bottom2, cy2, cx2)
        both2 = jnp.concatenate([top2, bottom2], axis=0)
        cb2 = to(both2, 1)
        qkv = fill([(4, y2), (2, x2), (5, cy2), (3, cx2)], other, qkv)
        *qkv, cb2 = together(*qkv, cb2)
        qkv = fill([(6, both2), (7, cb2)], other, qkv)
        x_own = jnp.where(
            upper == 0, jnp.concatenate([first, second], 0), jnp.concatenate([second, first], 0)
        )
        x_sent, x_here = (p2, p3), (both2,)
    else:
        pieces = own_and_sent(layer_input, own, range(sequences))
        x_own = in_order(pieces, own).reshape(rows, model)
        gathered = lax.all_gather(x_own, ("fs", "sp"), axis=0)
        gathered = gathered.reshape(n_fs, folds, sequences, rows, model)
        gathered = lax.dynamic_index_in_dim(gathered, own, 2, keepdims=False)
        blocks = gathered.reshape(n_fs * folds, rows, model)
        tiles = jnp.arange(length // TILE, dtype=jnp.int32)
        qkv = project([blocks], tiles, *project_args, None, heads, head_dim, length)
        x_sent, x_here = (x_own,), (blocks,)
    q, k, v = qkv

    three = jnp.stack(
        [
            merged(w, d, u).T
            for w, d, u in zip((weight_mixer, weight_expand, weight_contract), downs[1:], ups[1:])
        ]
    )
    w_mixer, w_expand, w_contract = lax.all_gather(after(three, *x_here), "fs", axis=1, tiled=True)
    g_pieces = own_and_sent(after(output_grad, *x_sent), own, range(sequences))

    firsts, lasts = segs[::TILE], segs[TILE - 1 :: TILE]
    starts = jnp.sum(segs[None, :] < firsts[:, None], axis=1, dtype=jnp.int32) // TILE
    ends = (jnp.sum(segs[None, :] <= lasts[:, None], axis=1, dtype=jnp.int32) + TILE - 1) // TILE

    attended_heads, aug = attend(starts, q, k, v, heads, head_dim)
    attended_heads, *g_pieces = together(attended_heads, *g_pieces)

    def sections_out(value):
        if folds == 1:
            mine = value.reshape(n_fs, rows, value.shape[1])
        else:
            cut = value.reshape(n_fs, folds, rows, value.shape[1])
            mine = lax.dynamic_index_in_dim(cut, fold_of, 1, keepdims=False)
        return lax.all_to_all(mine, "fs", split_axis=0, concat_axis=0, tiled=True)

    attended = jnp.swapaxes(sections_out(attended_heads), 0, 1).reshape(rows, model)
    g_own = in_order(g_pieces, own).reshape(rows, model)

    x_f = x_own.astype(F32)
    scale_one = rms_scale(x_f)
    normed_one = (x_f * scale_one * gain_attention).astype(BF16)
    narrow = lambda u, down: dot_nn(u, down).astype(BF16)
    mixer = dot_nt(attended, w_mixer)
    middle = x_f + mixer
    scale_two = rms_scale(middle)
    normed_two = (middle * scale_two * gain_feedforward).astype(BF16)
    expanded = dot_nt(normed_two, w_expand)
    gate = jax.nn.sigmoid(expanded)
    hidden = (expanded * gate).astype(BF16)
    contracted = dot_nt(hidden, w_contract)
    layer_output = (middle + contracted).astype(BF16).reshape(sequences, tokens, model)

    def adapter_back(u, grad, down, up):
        grad_up = dot_tn(narrow(u, down), grad)
        grad_narrow = dot_nt(grad, up).astype(BF16)
        return [dot_tn(grad_narrow, u), grad_up]

    grad_hidden = dot_nn(g_own, w_contract)
    grad_expanded = (grad_hidden * gate * (1.0 + expanded * (1.0 - gate))).astype(BF16)
    grad_normed_two = dot_nn(grad_expanded, w_expand)
    grad_middle = g_own.astype(F32) + rms_back(middle, scale_two, grad_normed_two * gain_feedforward)
    grad_mixer = grad_middle.astype(BF16)
    grad_attended = dot_nn(grad_mixer, w_mixer).astype(BF16)

    to_heads = jnp.swapaxes(grad_attended.reshape(rows, n_fs, unit), 0, 1)
    grad_heads = lax.all_to_all(to_heads, "fs", split_axis=0, concat_axis=0, tiled=True)
    if folds > 1:
        every = lax.all_gather(grad_heads, "sp", axis=0)
        every = every.reshape(folds, sequences, n_fs, rows, unit)
        every = lax.dynamic_index_in_dim(every, own, 1, keepdims=False)
        grad_heads = jnp.swapaxes(every, 0, 1)
    grad_heads = grad_heads.reshape(length, unit)

    early = jnp.concatenate(
        adapter_back(attended, grad_mixer, downs[1], ups[1])
        + adapter_back(normed_two, grad_expanded, downs[2], ups[2])
        + adapter_back(hidden, g_own, downs[3], ups[3]),
        axis=0,
    )
    grad_heads, early = together(grad_heads, early)
    w_all = lax.all_gather(after(w_own.T, grad_heads), "fs", axis=0)
    early = lax.all_to_all(
        early.reshape(n_fs, early.shape[0] // n_fs, model), "fs", split_axis=0, concat_axis=0, tiled=True
    )
    out_pieces = own_and_sent(after(layer_output, grad_heads), own, range(sequences))

    grad_qkv = attend_back(ends, aug, k, v, grad_heads, attended_heads, scale_pad, heads, head_dim)
    grad_qkv, w_all, early, *out_pieces = together(grad_qkv, w_all, early, *out_pieces)
    grad_joined = sections_out(grad_qkv)
    early = over_sequences(jnp.sum(early, axis=0), sequences, n_sp)
    grad_joined, *early = together(grad_joined, *early)
    early = fold(early, adapter_index, adapters, own)
    layer_output = in_order(out_pieces, own)

    up_all = (
        ups[0].reshape(rank, 3, n_fs, unit).transpose(2, 0, 1, 3).reshape(n_fs, rank, 3 * unit)
    )
    narrow_one = narrow(normed_one, downs[0])
    grad_up = jnp.einsum("tr,htc->rhc", narrow_one, grad_joined, preferred_element_type=F32)
    grad_up = grad_up.reshape(rank, n_fs, 3, unit).transpose(0, 2, 1, 3).reshape(3 * rank, model)
    grad_narrow = jnp.einsum("htc,hrc->tr", grad_joined, up_all, preferred_element_type=F32).astype(BF16)
    late = jnp.concatenate([dot_tn(grad_narrow, normed_one), grad_up], axis=0)
    grad_joined, late = together(grad_joined, late)
    late = direct_shares(late, n_fs)
    early = [early] + [xor_permute(early, "fs", m) for m in range(1, n_fs)]
    grad_normed_one = jnp.einsum("htc,hcd->td", grad_joined, w_all, preferred_element_type=F32)
    input_grad = grad_middle + rms_back(x_f, scale_one, grad_normed_one * gain_attention)
    input_grad = input_grad.astype(BF16).reshape(sequences, tokens, model)
    input_grad, late, early = together(input_grad, late, early)
    early = in_order(early, fs)
    late = over_sequences(sum(late[1:], late[0]), sequences, n_sp)
    in_pieces = own_and_sent(input_grad, own, range(sequences))
    in_pieces[1], *late = together(in_pieces[1], *late)
    late = fold(late, adapter_index, adapters, own)
    late = in_order([late] + [xor_permute(late, "fs", m) for m in range(1, n_fs)], fs)
    input_grad = in_order(in_pieces, own)

    factor = 1.0 / math.sqrt(length)
    outs = []
    late, early = joined_rows(late) * factor, joined_rows(early) * factor
    for tables, wides in ((late, (3,)), (early, (1, 1, 1))):
        first = 0
        for wide in wides:
            outs.append(jnp.swapaxes(tables[:, first : first + rank], 1, 2))
            first += rank
            outs.append(tables[:, first : first + rank * wide].reshape(adapters, rank, wide * model))
            first += rank * wide
    return (layer_output, input_grad, *outs)


def solution(mesh):
    tokens = P(None, ("fs", "sp"), None)
    in_specs = (tokens, tokens) + (P(),) * 5 + (P(None, "fs"),) * 4 + (P(),) * 8
    out_specs = (tokens, tokens) + (P(),) * 8
    return jax.shard_map(local, mesh=mesh, in_specs=in_specs, out_specs=out_specs, check_vma=False)
```

```python
import functools
import math

import jax
import jax.numpy as jnp
from jax import lax
from jax.experimental import pallas as pl
from jax.experimental.pallas import tpu as pltpu
from jax.sharding import PartitionSpec as P

EPSILON = 1e-06
BIG = 1e30
LANES = 128
PARTS = 3
TILE = 256
VMEM_LIMIT = 64000000
F32 = jnp.float32
BF16 = jnp.bfloat16
NT = (((1,), (1,)), ((), ()))
TN = (((0,), (0,)), ((), ()))


def dot_nn(a, b):
    return jnp.dot(a, b, preferred_element_type=F32)


def dot_nt(a, b):
    return lax.dot_general(a, b, NT, preferred_element_type=F32)


def dot_tn(a, b):
    return lax.dot_general(a, b, TN, preferred_element_type=F32)


def xor_permute(value, axis, mask):
    count = lax.axis_size(axis)
    return lax.ppermute(value, axis, [(a, a ^ mask) for a in range(count)])


def piece_of(stacked, index):
    return lax.dynamic_index_in_dim(stacked, index, 0, keepdims=False)


def project_kernel(tiles, *refs, count, heads, head_dim):
    x_refs, (gain_ref, w_ref, scale_ref, qpad_ref, kpad_ref) = refs[:count], refs[count : count + 5]
    q_ref, k_ref, v_ref, x_ref = refs[-4:]
    if count > 1:
        for n in range(count):

            @pl.when(pl.program_id(0) == n)
            def _():
                x_ref[...] = x_refs[n][...]

        x = x_ref[...].astype(F32)
    else:
        x = x_refs[0][0].astype(F32)
    mean = jnp.mean(x * x, axis=-1, keepdims=True)
    normed = (x * lax.rsqrt(mean + EPSILON) * gain_ref[...]).astype(BF16)
    rows = dot_nn(normed, w_ref[...]) * scale_ref[...]
    width = heads * LANES
    lane = lax.broadcasted_iota(jnp.int32, (1, width), 1) % LANES
    q_ref[...] = (rows[:, :width] + jnp.tile(qpad_ref[...].astype(F32), (1, heads))).astype(BF16)
    k_ref[...] = (rows[:, width : 2 * width] + jnp.tile(kpad_ref[...].astype(F32), (1, heads))).astype(BF16)
    ones = jnp.where((lane >= head_dim) & (lane < head_dim + PARTS), 1.0, 0.0)
    v_ref[...] = (rows[:, 2 * width :] + ones).astype(BF16)


def project(sources, tiles, gain, weight, scale, qpad, kpad, earlier, heads, head_dim, length):
    model = weight.shape[0]
    step = TILE
    count = len(sources)
    steps = tiles.shape[0]
    width = heads * LANES
    out = pl.BlockSpec((step, width), lambda n, t: (t[n], 0))
    pad = pl.BlockSpec((step, LANES), lambda n, t: (t[n], 0))
    fixed = lambda shape: pl.BlockSpec(shape, lambda n, t: (0,) * len(shape))
    if count > 1:
        in_specs = [fixed((step, model))] * count
    else:
        per = sources[0].shape[1] // step
        in_specs = [pl.BlockSpec((1, step, model), lambda n, t: (n // per, n % per, 0))]
    in_specs += [fixed((1, model)), fixed((model, 3 * width)), fixed((1, 3 * width)), pad, pad]
    operands = [*sources, gain, weight, scale, qpad, kpad]
    aliases = {}
    if earlier is not None:
        in_specs += [pl.BlockSpec(memory_space=pl.ANY)] * 3
        aliases = {1 + len(operands) + n: n for n in range(3)}
        operands += list(earlier)
    return pl.pallas_call(
        functools.partial(project_kernel, count=count, heads=heads, head_dim=head_dim),
        out_shape=[jax.ShapeDtypeStruct((length, width), BF16)] * 3,
        grid_spec=pltpu.PrefetchScalarGridSpec(
            num_scalar_prefetch=1,
            grid=(steps,),
            in_specs=in_specs,
            out_specs=[out] * 3,
            scratch_shapes=[pltpu.VMEM((step, model), BF16)],
        ),
        input_output_aliases=aliases,
        compiler_params=pltpu.CompilerParams(vmem_limit_bytes=VMEM_LIMIT),
        cost_estimate=pl.CostEstimate(
            flops=6 * steps * step * model * 3 * width,
            bytes_accessed=2 * (steps * step * (model + 3 * width) + model * 3 * width),
            transcendentals=0,
        ),
        name="project",
    )(tiles, *operands)


def spread(column, lane, first):
    high = column.astype(BF16).astype(F32)
    middle = (column - high).astype(BF16).astype(F32)
    last = column - high - middle
    return jnp.where(lane == first, high, jnp.where(lane == first + 1, middle, last))


def attend_kernel(starts, q_ref, k_ref, v_ref, o_ref, aug_ref, s_ref, *, heads, head_dim):
    step = pl.program_id(0)
    first = starts[step]
    tile = q_ref.shape[0]
    lane = lax.broadcasted_iota(jnp.int32, (1, LANES), 1)

    def cols(h):
        return pl.ds(h * LANES, LANES)

    def scores(block, masked):
        out = []
        rows = pl.ds(pl.multiple_of(block * tile, tile), tile)
        for h in range(heads):
            s = dot_nt(q_ref[:, cols(h)], k_ref[rows, cols(h)])
            if masked:
                s = jnp.where(
                    lax.broadcasted_iota(jnp.int32, (tile, tile), 1)
                    <= lax.broadcasted_iota(jnp.int32, (tile, tile), 0),
                    s,
                    -BIG,
                )
            s_ref[h, block - first] = s
            top = s[:, :LANES]
            for c in range(LANES, tile, LANES):
                top = jnp.maximum(top, s[:, c : c + LANES])
            out.append(top)
        return tuple(out)

    def first_pass(block, tops):
        return tuple(jnp.maximum(a, b) for a, b in zip(tops, scores(block, False)))

    tops = lax.fori_loop(first, step, first_pass, scores(step, True))
    peaks = [jnp.max(top, axis=-1, keepdims=True) for top in tops]

    def second_pass(block, totals):
        rows = pl.ds(pl.multiple_of(block * tile, tile), tile)
        out = []
        for h in range(heads):
            p = jnp.exp(s_ref[h, block - first] - peaks[h]).astype(BF16)
            out.append(totals[h] + dot_nn(p, v_ref[rows, cols(h)]))
        return tuple(out)

    zero = jnp.zeros((tile, LANES), F32)
    totals = lax.fori_loop(first, step + 1, second_pass, (zero,) * heads)
    parts = []
    for h in range(heads):
        total = totals[h][:, head_dim : head_dim + 1]
        parts.append((totals[h] / total)[:, :head_dim].astype(BF16))
        lse = -(peaks[h] + jnp.log(total))
        marks = (lane >= head_dim) & (lane < head_dim + PARTS)
        aug_ref[:, cols(h)] = jnp.where(
            marks, spread(lse, lane, head_dim), q_ref[:, cols(h)].astype(F32)
        ).astype(BF16)
    o_ref[...] = jnp.concatenate(parts, axis=1)


def attend(starts, q, k, v, heads, head_dim):
    length, width = q.shape
    blocks = length // TILE
    span = min(blocks, -(-2048 // TILE) + 1)
    row = lambda w: pl.BlockSpec((TILE, w), lambda n, st: (n, 0))
    whole = pl.BlockSpec((length, width), lambda n, st: (0, 0))
    return pl.pallas_call(
        functools.partial(attend_kernel, heads=heads, head_dim=head_dim),
        out_shape=[
            jax.ShapeDtypeStruct((length, heads * head_dim), BF16),
            jax.ShapeDtypeStruct((length, width), BF16),
        ],
        grid_spec=pltpu.PrefetchScalarGridSpec(
            num_scalar_prefetch=1,
            grid=(blocks,),
            in_specs=[row(width), whole, whole],
            out_specs=[row(heads * head_dim), row(width)],
            scratch_shapes=[pltpu.VMEM((heads, span, TILE, TILE), F32)],
        ),
        compiler_params=pltpu.CompilerParams(vmem_limit_bytes=VMEM_LIMIT),
        cost_estimate=pl.CostEstimate(
            flops=40 * heads * length * 1024 * LANES, bytes_accessed=10 * length * width, transcendentals=0
        ),
        name="attend",
    )(starts, q, k, v)


def attend_back_kernel(
    ends, aug_ref, k_ref, v_ref, g_ref, o_ref, scale_ref, d_ref, gaug_ref, dq_ref, dk_ref, dv_ref, *, heads, head_dim
):
    step = pl.program_id(0)
    tile = k_ref.shape[0]
    length = aug_ref.shape[0]
    lane = lax.broadcasted_iota(jnp.int32, (1, LANES), 1)

    def cols(h):
        return pl.ds(h * LANES, LANES)

    @pl.when(step == 0)
    def _():
        @pl.loop(0, length // tile)
        def _(n):
            rows = pl.ds(pl.multiple_of(n * tile, tile), tile)
            g = g_ref[rows, :]
            product = g.astype(F32) * o_ref[rows, :].astype(F32)
            for h in range(heads):
                own = slice(h * head_dim, (h + 1) * head_dim)
                delta = -jnp.sum(product[:, own], axis=-1, keepdims=True)
                mine = jnp.concatenate(
                    [g[:, own].astype(F32), jnp.zeros((tile, LANES - head_dim), F32)], axis=1
                )
                marks = (lane >= head_dim) & (lane < head_dim + PARTS)
                gaug_ref[rows, cols(h)] = jnp.where(
                    marks, spread(delta, lane, head_dim), mine
                ).astype(BF16)
            dq_ref[rows, :] = jnp.zeros((tile, heads * LANES), F32)

    dk_ref[...] = jnp.zeros_like(dk_ref)
    dv_ref[...] = jnp.zeros_like(dv_ref)

    def one(block, masked):
        rows = pl.ds(pl.multiple_of(block * tile, tile), tile)
        for h in range(heads):
            q = aug_ref[rows, cols(h)]
            g = gaug_ref[rows, cols(h)]
            k = k_ref[:, cols(h)]
            s = dot_nt(k, q)
            if masked:
                s = jnp.where(
                    lax.broadcasted_iota(jnp.int32, (tile, tile), 0)
                    <= lax.broadcasted_iota(jnp.int32, (tile, tile), 1),
                    s,
                    -BIG,
                )
            p = jnp.exp(s)
            d = dot_nt(v_ref[:, cols(h)], g)
            dv_ref[:, cols(h)] += dot_nn(p.astype(BF16), g)
            ds = (p * d).astype(BF16)
            dk_ref[:, cols(h)] += dot_nn(ds, q)
            dq_ref[rows, cols(h)] += dot_tn(ds, k)

    one(step, True)

    @pl.loop(step + 1, ends[step])
    def _(block):
        one(block, False)

    own = pl.ds(pl.multiple_of(step * tile, tile), tile)
    pieces = []
    for h in range(heads):
        dq = dq_ref[own, cols(h)].astype(BF16).astype(F32) * scale_ref[...]
        pieces.append(dq[:, :head_dim])
    for ref in (dk_ref, dv_ref):
        for h in range(heads):
            pieces.append(ref[:, h * LANES : h * LANES + head_dim])
    d_ref[...] = jnp.concatenate(pieces, axis=1).astype(BF16)


def attend_back(ends, aug, k, v, grad, attended, scale, heads, head_dim):
    length, width = aug.shape
    blocks = length // TILE
    row = lambda w: pl.BlockSpec((TILE, w), lambda n, st: (n, 0))
    whole = lambda w: pl.BlockSpec((length, w), lambda n, st: (0, 0))
    return pl.pallas_call(
        functools.partial(attend_back_kernel, heads=heads, head_dim=head_dim),
        out_shape=jax.ShapeDtypeStruct((length, 3 * heads * head_dim), BF16),
        grid_spec=pltpu.PrefetchScalarGridSpec(
            num_scalar_prefetch=1,
            grid=(blocks,),
            in_specs=[
                whole(width),
                row(width),
                row(width),
                whole(heads * head_dim),
                whole(heads * head_dim),
                pl.BlockSpec((1, LANES), lambda n, st: (0, 0)),
            ],
            out_specs=row(3 * heads * head_dim),
            scratch_shapes=[
                pltpu.VMEM((length, width), BF16),
                pltpu.VMEM((length, width), F32),
                pltpu.VMEM((TILE, width), F32),
                pltpu.VMEM((TILE, width), F32),
            ],
        ),
        compiler_params=pltpu.CompilerParams(vmem_limit_bytes=VMEM_LIMIT),
        cost_estimate=pl.CostEstimate(
            flops=60 * heads * length * 1024 * LANES, bytes_accessed=14 * length * width, transcendentals=0
        ),
        name="attend_back",
    )(ends, aug, k, v, grad, attended, scale)


def rms_scale(values):
    return lax.rsqrt(jnp.mean(values * values, axis=-1, keepdims=True) + EPSILON)


def rms_back(values, scale_rows, grad_normed):
    cubed = scale_rows * scale_rows * scale_rows
    return scale_rows * grad_normed - values * cubed * jnp.mean(
        grad_normed * values, axis=-1, keepdims=True
    )


def after(value, *others):
    return lax.optimization_barrier((value, others))[0]


def together(*values):
    return lax.optimization_barrier(values)


def own_and_sent(value, own, masks):
    return [
        piece_of(value, own) if m == 0 else xor_permute(piece_of(value, own ^ m), "sp", m) for m in masks
    ]


def in_order(pieces, own):
    stacked = jnp.stack(pieces)
    return jnp.stack([piece_of(stacked, n ^ own) for n in range(len(pieces))], axis=0)


def direct_shares(part, n_fs):
    fs = lax.axis_index("fs")
    split = part.reshape(n_fs, part.shape[0] // n_fs, part.shape[1])
    return [
        piece_of(split, fs) if m == 0 else xor_permute(piece_of(split, fs ^ m), "fs", m) for m in range(n_fs)
    ]


def over_sequences(part, groups, n_sp):
    mask = groups
    while mask < n_sp:
        part = part + xor_permute(part, "sp", mask)
        mask <<= 1
    return [part] + [xor_permute(part, "sp", m) for m in range(1, groups)]


def fold(pieces, adapter_index, adapters, own):
    by_seq = in_order(pieces, own)
    tables = []
    for a in range(adapters):
        table = jnp.zeros_like(pieces[0])
        for s in range(len(pieces)):
            table = table + jnp.where(adapter_index[s, 0] == a, by_seq[s], 0.0)
        tables.append(table)
    return jnp.stack(tables)


def joined_rows(every):
    n, adapters, rows, model = every.shape
    return jnp.swapaxes(every, 0, 1).reshape(adapters, n * rows, model)


def local(
    layer_input,
    output_grad,
    segment_ids,
    adapter_index,
    gain_attention,
    gain_feedforward,
    query_scale,
    weight_qkv,
    weight_mixer,
    weight_expand,
    weight_contract,
    qkv_down,
    qkv_up,
    mixer_down,
    mixer_up,
    expand_down,
    expand_up,
    contract_down,
    contract_up,
):
    sequences, tokens, model = layer_input.shape
    head_dim = query_scale.shape[0]
    n_fs, n_sp = lax.axis_size("fs"), lax.axis_size("sp")
    adapters, rank = qkv_down.shape[0], qkv_down.shape[2]
    length = segment_ids.shape[1]
    folds = n_sp // sequences
    heads = model // head_dim // n_fs
    unit = heads * head_dim
    width = heads * LANES
    rows = sequences * tokens
    fs = lax.axis_index("fs")
    sp = lax.axis_index("sp")
    own = sp % sequences
    fold_of = sp // sequences

    pick = piece_of(adapter_index, own)[0]
    downs = [piece_of(t, pick) for t in (qkv_down, mixer_down, expand_down, contract_down)]
    ups = [piece_of(t, pick) for t in (qkv_up, mixer_up, expand_up, contract_up)]

    def merged(weight, down, up):
        cols = weight.shape[1]
        own_up = lax.dynamic_slice_in_dim(up, fs * cols, cols, 1)
        return (weight.astype(F32) + dot_nn(down, own_up)).astype(BF16)

    shard = merged(weight_qkv, downs[0], ups[0])
    inverse = pow(3, -1, n_fs)
    received = [
        lax.ppermute(
            shard[:, t * unit : (t + 1) * unit], "fs", [(d, (3 * d + t) % n_fs) for d in range(n_fs)]
        )
        for t in range(3)
    ]
    places = [(3 * ((inverse * (fs - t)) % n_fs) + t) // n_fs for t in range(3)]
    w_parts = []
    for b in range(3):
        part = jnp.zeros_like(received[0])
        for t in range(3):
            part = jnp.where(places[t] == b, received[t], part)
        w_parts.append(part)
    w_own = jnp.concatenate(w_parts, axis=1)
    w_padded = jnp.pad(
        w_own.reshape(model, 3 * heads, head_dim), ((0, 0), (0, 0), (0, LANES - head_dim))
    ).reshape(model, 3 * width)

    segs = piece_of(segment_ids, own)
    scale = query_scale * (1.0 / math.sqrt(head_dim))
    scale_pad = jnp.pad(scale, (0, LANES - head_dim))[None]
    col_scale = jnp.concatenate([jnp.tile(scale_pad, (1, heads)), jnp.ones((1, 2 * width), F32)], axis=1)
    lane = jnp.arange(LANES)[None, :]
    marks = lane >= head_dim + PARTS
    same = lane == segs[:, None] + (head_dim + PARTS)
    qpad = same.astype(BF16)
    kpad = jnp.where(
        marks, jnp.where(same, 0.0, -BIG), jnp.where(lane >= head_dim, 1.0, 0.0)
    ).astype(BF16)

    project_args = (gain_attention[None], w_padded, col_scale, qpad, kpad)
    as_table = lambda *s: jnp.stack(s).astype(jnp.int32)
    if n_fs == 8 and folds == 1 and sequences == 4 and 2 * tokens == TILE:
        pieces = own_and_sent(layer_input, own, (0, 1))
        pieces += own_and_sent(after(layer_input, pieces[1]), own, (2, 3))
        odd = own % 2 == 1
        upper = own // 2

        def pair(low, high):
            return jnp.where(odd, jnp.concatenate([high, low], 0), jnp.concatenate([low, high], 0))

        def to(value, mask):
            return xor_permute(value, "fs", mask)

        def fill(blocks, place, earlier):
            sources = [block for _, block in blocks]
            tiles = as_table(*[(fs ^ mask) * 2 + place for mask, _ in blocks])
            return project(sources, tiles, *project_args, earlier, heads, head_dim, length)

        other = 1 - upper
        first = pair(pieces[0], pieces[1])
        half = TILE // 2
        y1, x1, c1 = to(first, 4), to(first, 2), to(first, 1)
        y1, x1, c1 = together(y1, x1, c1)
        top1, bottom1, cy1, cx1 = to(y1[:half], 2), to(x1[half:], 4), to(y1, 1), to(x1, 1)
        qkv = fill([(0, first), (1, c1), (4, y1), (2, x1)], upper, None)
        *qkv, top1, bottom1, cy1, cx1, p2, p3 = together(*qkv, top1, bottom1, cy1, cx1, pieces[2], pieces[3])
        both1 = jnp.concatenate([top1, bottom1], axis=0)
        second = pair(p2, p3)
        y2, x2, c2, cb1 = to(second, 4), to(second, 2), to(second, 1), to(both1, 1)
        qkv = fill([(5, cy1), (3, cx1)], upper, qkv)
        *qkv, y2, x2, c2, cb1 = together(*qkv, y2, x2, c2, cb1)
        top2, bottom2, cy2, cx2 = to(y2[:half], 2), to(x2[half:], 4), to(y2, 1), to(x2, 1)
        qkv = fill([(6, both1), (7, cb1)], upper, qkv)
        qkv = fill([(0, second), (1, c2)], other, qkv)
        *qkv, top2, bottom2, cy2, cx2 = together(*qkv, top2, bottom2, cy2, cx2)
        both2 = jnp.concatenate([top2, bottom2], axis=0)
        cb2 = to(both2, 1)
        qkv = fill([(4, y2), (2, x2), (5, cy2), (3, cx2)], other, qkv)
        *qkv, cb2 = together(*qkv, cb2)
        qkv = fill([(6, both2), (7, cb2)], other, qkv)
        x_own = jnp.where(
            upper == 0, jnp.concatenate([first, second], 0), jnp.concatenate([second, first], 0)
        )
        x_sent, x_here = (p2, p3), (both2,)
    else:
        pieces = own_and_sent(layer_input, own, range(sequences))
        x_own = in_order(pieces, own).reshape(rows, model)
        gathered = lax.all_gather(x_own, ("fs", "sp"), axis=0)
        gathered = gathered.reshape(n_fs, folds, sequences, rows, model)
        gathered = lax.dynamic_index_in_dim(gathered, own, 2, keepdims=False)
        blocks = gathered.reshape(n_fs * folds, rows, model)
        tiles = jnp.arange(length // TILE, dtype=jnp.int32)
        qkv = project([blocks], tiles, *project_args, None, heads, head_dim, length)
        x_sent, x_here = (x_own,), (blocks,)
    q, k, v = qkv

    three = jnp.stack(
        [
            merged(w, d, u).T
            for w, d, u in zip((weight_mixer, weight_expand, weight_contract), downs[1:], ups[1:])
        ]
    )
    w_mixer, w_expand, w_contract = lax.all_gather(after(three, *x_here), "fs", axis=1, tiled=True)
    g_pieces = own_and_sent(after(output_grad, *x_sent), own, range(sequences))

    firsts, lasts = segs[::TILE], segs[TILE - 1 :: TILE]
    starts = jnp.sum(segs[None, :] < firsts[:, None], axis=1, dtype=jnp.int32) // TILE
    ends = (jnp.sum(segs[None, :] <= lasts[:, None], axis=1, dtype=jnp.int32) + TILE - 1) // TILE

    attended_heads, aug = attend(starts, q, k, v, heads, head_dim)
    attended_heads, *g_pieces = together(attended_heads, *g_pieces)

    def sections_out(value):
        if folds == 1:
            mine = value.reshape(n_fs, rows, value.shape[1])
        else:
            cut = value.reshape(n_fs, folds, rows, value.shape[1])
            mine = lax.dynamic_index_in_dim(cut, fold_of, 1, keepdims=False)
        return lax.all_to_all(mine, "fs", split_axis=0, concat_axis=0, tiled=True)

    attended = jnp.swapaxes(sections_out(attended_heads), 0, 1).reshape(rows, model)
    g_own = in_order(g_pieces, own).reshape(rows, model)

    x_f = x_own.astype(F32)
    scale_one = rms_scale(x_f)
    normed_one = (x_f * scale_one * gain_attention).astype(BF16)
    narrow = lambda u, down: dot_nn(u, down).astype(BF16)
    mixer = dot_nt(attended, w_mixer)
    middle = x_f + mixer
    scale_two = rms_scale(middle)
    normed_two = (middle * scale_two * gain_feedforward).astype(BF16)
    expanded = dot_nt(normed_two, w_expand)
    gate = jax.nn.sigmoid(expanded)
    hidden = (expanded * gate).astype(BF16)
    contracted = dot_nt(hidden, w_contract)
    layer_output = (middle + contracted).astype(BF16).reshape(sequences, tokens, model)

    def adapter_back(u, grad, down, up):
        grad_up = dot_tn(narrow(u, down), grad)
        grad_narrow = dot_nt(grad, up).astype(BF16)
        return [dot_tn(grad_narrow, u), grad_up]

    grad_hidden = dot_nn(g_own, w_contract)
    grad_expanded = (grad_hidden * gate * (1.0 + expanded * (1.0 - gate))).astype(BF16)
    grad_normed_two = dot_nn(grad_expanded, w_expand)
    grad_middle = g_own.astype(F32) + rms_back(middle, scale_two, grad_normed_two * gain_feedforward)
    grad_mixer = grad_middle.astype(BF16)
    grad_attended = dot_nn(grad_mixer, w_mixer).astype(BF16)

    to_heads = jnp.swapaxes(grad_attended.reshape(rows, n_fs, unit), 0, 1)
    grad_heads = lax.all_to_all(to_heads, "fs", split_axis=0, concat_axis=0, tiled=True)
    if folds > 1:
        every = lax.all_gather(grad_heads, "sp", axis=0)
        every = every.reshape(folds, sequences, n_fs, rows, unit)
        every = lax.dynamic_index_in_dim(every, own, 1, keepdims=False)
        grad_heads = jnp.swapaxes(every, 0, 1)
    grad_heads = grad_heads.reshape(length, unit)

    early = jnp.concatenate(
        adapter_back(attended, grad_mixer, downs[1], ups[1])
        + adapter_back(normed_two, grad_expanded, downs[2], ups[2])
        + adapter_back(hidden, g_own, downs[3], ups[3]),
        axis=0,
    )
    grad_heads, early = together(grad_heads, early)
    w_all = lax.all_gather(after(w_own.T, grad_heads), "fs", axis=0)
    early = lax.all_to_all(
        early.reshape(n_fs, early.shape[0] // n_fs, model), "fs", split_axis=0, concat_axis=0, tiled=True
    )
    out_pieces = own_and_sent(after(layer_output, grad_heads), own, range(sequences))

    grad_qkv = attend_back(ends, aug, k, v, grad_heads, attended_heads, scale_pad, heads, head_dim)
    grad_qkv, w_all, early, *out_pieces = together(grad_qkv, w_all, early, *out_pieces)
    grad_joined = sections_out(grad_qkv)
    early = over_sequences(jnp.sum(early, axis=0), sequences, n_sp)
    grad_joined, *early = together(grad_joined, *early)
    early = fold(early, adapter_index, adapters, own)
    layer_output = in_order(out_pieces, own)

    up_all = (
        ups[0].reshape(rank, 3, n_fs, unit).transpose(2, 0, 1, 3).reshape(n_fs, rank, 3 * unit)
    )
    narrow_one = narrow(normed_one, downs[0])
    grad_up = jnp.einsum("tr,htc->rhc", narrow_one, grad_joined, preferred_element_type=F32)
    grad_up = grad_up.reshape(rank, n_fs, 3, unit).transpose(0, 2, 1, 3).reshape(3 * rank, model)
    grad_narrow = jnp.einsum("htc,hrc->tr", grad_joined, up_all, preferred_element_type=F32).astype(BF16)
    late = jnp.concatenate([dot_tn(grad_narrow, normed_one), grad_up], axis=0)
    grad_joined, late = together(grad_joined, late)
    late = direct_shares(late, n_fs)
    early = [early] + [xor_permute(early, "fs", m) for m in range(1, n_fs)]
    grad_normed_one = jnp.einsum("htc,hcd->td", grad_joined, w_all, preferred_element_type=F32)
    input_grad = grad_middle + rms_back(x_f, scale_one, grad_normed_one * gain_attention)
    input_grad = input_grad.astype(BF16).reshape(sequences, tokens, model)
    input_grad, late = together(input_grad, late)
    late = over_sequences(sum(late[1:], late[0]), sequences, n_sp)
    in_pieces = own_and_sent(input_grad, own, range(sequences))
    in_pieces[-1], late, early = together(in_pieces[-1], late, early)
    early = in_order(early, fs)
    late = fold(late, adapter_index, adapters, own)
    late = in_order([late] + [xor_permute(late, "fs", m) for m in range(1, n_fs)], fs)
    input_grad = in_order(in_pieces, own)

    factor = 1.0 / math.sqrt(length)
    outs = []
    late, early = joined_rows(late) * factor, joined_rows(early) * factor
    for tables, wides in ((late, (3,)), (early, (1, 1, 1))):
        first = 0
        for wide in wides:
            outs.append(jnp.swapaxes(tables[:, first : first + rank], 1, 2))
            first += rank
            outs.append(tables[:, first : first + rank * wide].reshape(adapters, rank, wide * model))
            first += rank * wide
    return (layer_output, input_grad, *outs)


def solution(mesh):
    tokens = P(None, ("fs", "sp"), None)
    in_specs = (tokens, tokens) + (P(),) * 5 + (P(None, "fs"),) * 4 + (P(),) * 8
    out_specs = (tokens, tokens) + (P(),) * 8
    return jax.shard_map(local, mesh=mesh, in_specs=in_specs, out_specs=out_specs, check_vma=False)
```

```python
import functools
import math

import jax
import jax.numpy as jnp
from jax import lax
from jax.experimental import pallas as pl
from jax.experimental.pallas import tpu as pltpu
from jax.sharding import PartitionSpec as P

EPSILON = 1e-06
BIG = 1e30
LANES = 128
PARTS = 3
TILE = 256
VMEM_LIMIT = 64000000
F32 = jnp.float32
BF16 = jnp.bfloat16
NT = (((1,), (1,)), ((), ()))
TN = (((0,), (0,)), ((), ()))


def dot_nn(a, b):
    return jnp.dot(a, b, preferred_element_type=F32)


def dot_nt(a, b):
    return lax.dot_general(a, b, NT, preferred_element_type=F32)


def dot_tn(a, b):
    return lax.dot_general(a, b, TN, preferred_element_type=F32)


def xor_permute(value, axis, mask):
    count = lax.axis_size(axis)
    return lax.ppermute(value, axis, [(a, a ^ mask) for a in range(count)])


def piece_of(stacked, index):
    return lax.dynamic_index_in_dim(stacked, index, 0, keepdims=False)


def project_kernel(tiles, *refs, count, heads, head_dim):
    x_refs, (gain_ref, w_ref, scale_ref, qpad_ref, kpad_ref) = refs[:count], refs[count : count + 5]
    q_ref, k_ref, v_ref, x_ref = refs[-4:]
    if count > 1:
        for n in range(count):

            @pl.when(pl.program_id(0) == n)
            def _():
                x_ref[...] = x_refs[n][...]

        x = x_ref[...].astype(F32)
    else:
        x = x_refs[0][0].astype(F32)
    mean = jnp.mean(x * x, axis=-1, keepdims=True)
    normed = (x * lax.rsqrt(mean + EPSILON) * gain_ref[...]).astype(BF16)
    rows = dot_nn(normed, w_ref[...]) * scale_ref[...]
    width = heads * LANES
    lane = lax.broadcasted_iota(jnp.int32, (1, width), 1) % LANES
    q_ref[...] = (rows[:, :width] + jnp.tile(qpad_ref[...].astype(F32), (1, heads))).astype(BF16)
    k_ref[...] = (rows[:, width : 2 * width] + jnp.tile(kpad_ref[...].astype(F32), (1, heads))).astype(BF16)
    ones = jnp.where((lane >= head_dim) & (lane < head_dim + PARTS), 1.0, 0.0)
    v_ref[...] = (rows[:, 2 * width :] + ones).astype(BF16)


def project(sources, tiles, gain, weight, scale, qpad, kpad, earlier, heads, head_dim, length):
    model = weight.shape[0]
    step = TILE
    count = len(sources)
    steps = tiles.shape[0]
    width = heads * LANES
    out = pl.BlockSpec((step, width), lambda n, t: (t[n], 0))
    pad = pl.BlockSpec((step, LANES), lambda n, t: (t[n], 0))
    fixed = lambda shape: pl.BlockSpec(shape, lambda n, t: (0,) * len(shape))
    if count > 1:
        in_specs = [fixed((step, model))] * count
    else:
        per = sources[0].shape[1] // step
        in_specs = [pl.BlockSpec((1, step, model), lambda n, t: (n // per, n % per, 0))]
    in_specs += [fixed((1, model)), fixed((model, 3 * width)), fixed((1, 3 * width)), pad, pad]
    operands = [*sources, gain, weight, scale, qpad, kpad]
    aliases = {}
    if earlier is not None:
        in_specs += [pl.BlockSpec(memory_space=pl.ANY)] * 3
        aliases = {1 + len(operands) + n: n for n in range(3)}
        operands += list(earlier)
    return pl.pallas_call(
        functools.partial(project_kernel, count=count, heads=heads, head_dim=head_dim),
        out_shape=[jax.ShapeDtypeStruct((length, width), BF16)] * 3,
        grid_spec=pltpu.PrefetchScalarGridSpec(
            num_scalar_prefetch=1,
            grid=(steps,),
            in_specs=in_specs,
            out_specs=[out] * 3,
            scratch_shapes=[pltpu.VMEM((step, model), BF16)],
        ),
        input_output_aliases=aliases,
        compiler_params=pltpu.CompilerParams(vmem_limit_bytes=VMEM_LIMIT),
        cost_estimate=pl.CostEstimate(
            flops=6 * steps * step * model * 3 * width,
            bytes_accessed=2 * (steps * step * (model + 3 * width) + model * 3 * width),
            transcendentals=0,
        ),
        name="project",
    )(tiles, *operands)


def spread(row, index, first):
    high = row.astype(BF16).astype(F32)
    middle = (row - high).astype(BF16).astype(F32)
    last = row - high - middle
    return jnp.where(index == first, high, jnp.where(index == first + 1, middle, last))


def at(block):
    return pl.ds(pl.multiple_of(block * TILE, TILE), TILE)


def attend_kernel(starts, q_ref, k_ref, v_ref, *refs, heads, head_dim, parity):
    o_ref, aug_ref = refs[-2:]
    step = 2 * pl.program_id(0) + parity
    first = starts[step]
    index = lax.broadcasted_iota(jnp.int32, (LANES, 1), 0)
    marks = (index >= head_dim) & (index < head_dim + PARTS)

    def cols(h):
        return pl.ds(h * LANES, LANES)

    turned = [jnp.transpose(q_ref[:, cols(h)].astype(F32)) for h in range(heads)]
    queries = [t.astype(BF16) for t in turned]

    def one(block, carry, masked):
        scores = [dot_nn(k_ref[at(block), cols(h)], queries[h]) for h in range(heads)]
        out = []
        for h, s in enumerate(scores):
            if masked:
                key = lax.broadcasted_iota(jnp.int32, (TILE, TILE), 0)
                query = lax.broadcasted_iota(jnp.int32, (TILE, TILE), 1)
                s = jnp.where(key <= query, s, -BIG)
            peak = jnp.max(s, axis=0, keepdims=True)
            if not masked:
                peak = jnp.maximum(carry[h][0], peak)
            p = jnp.exp(s - peak).astype(BF16)
            total = dot_tn(v_ref[at(block), cols(h)], p)
            if not masked:
                total = carry[h][1] * jnp.exp(carry[h][0] - peak) + total
            out.append((peak, total))
        return tuple(out)

    carry = one(step, None, True)
    carry = lax.fori_loop(first, step, lambda block, c: one(block, c, False), carry)
    for h in range(heads):
        peak, total = carry[h]
        weight = total[head_dim : head_dim + 1]
        o_ref[0, h * head_dim : (h + 1) * head_dim, :] = (total / weight)[:head_dim].astype(BF16)
        lse = -(peak + jnp.log(weight))
        aug_ref[cols(h), :] = jnp.where(marks, spread(lse, index, head_dim), turned[h]).astype(BF16)


def attend(starts, q, k, v, earlier, parity, heads, head_dim):
    length, width = q.shape
    steps = length // TILE // 2
    whole = pl.BlockSpec((length, width), lambda n, st: (0, 0))
    in_specs = [pl.BlockSpec((TILE, width), lambda n, st: (2 * n + parity, 0)), whole, whole]
    operands = [q, k, v]
    aliases = {}
    if earlier is not None:
        in_specs.append(pl.BlockSpec(memory_space=pl.ANY))
        operands.append(earlier)
        aliases = {4: 1}
    return pl.pallas_call(
        functools.partial(attend_kernel, heads=heads, head_dim=head_dim, parity=parity),
        out_shape=[
            jax.ShapeDtypeStruct((steps, heads * head_dim, TILE), BF16),
            jax.ShapeDtypeStruct((width, length), BF16),
        ],
        grid_spec=pltpu.PrefetchScalarGridSpec(
            num_scalar_prefetch=1,
            grid=(steps,),
            in_specs=in_specs,
            out_specs=[
                pl.BlockSpec((1, heads * head_dim, TILE), lambda n, st: (n, 0, 0)),
                pl.BlockSpec((width, TILE), lambda n, st: (0, 2 * n + parity)),
            ],
        ),
        input_output_aliases=aliases,
        compiler_params=pltpu.CompilerParams(vmem_limit_bytes=VMEM_LIMIT),
        cost_estimate=pl.CostEstimate(
            flops=20 * heads * length * 1024 * LANES, bytes_accessed=6 * length * width, transcendentals=0
        ),
        name="attend",
    )(starts, *operands)


def attend_back_kernel(ends, aug_ref, k_ref, v_ref, *refs, heads, head_dim, parity):
    step = 2 * pl.program_id(0) + parity
    length = aug_ref.shape[1]
    unit = heads * head_dim
    if parity == 0:
        g_ref, even_ref, odd_ref, kv_ref, g_out_ref, dq_ref, dk_ref, dv_ref = refs
        gaug_ref = g_out_ref
    else:
        gaug_ref, dq_in_ref, scale_ref, all_ref, dq_ref, dk_ref, dv_ref = refs

    def cols(h):
        return pl.ds(h * LANES, LANES)

    def own(h):
        return slice(h * head_dim, (h + 1) * head_dim)

    @pl.when(step == parity)
    def _():
        dq_ref[...] = jnp.zeros_like(dq_ref)
        if parity == 0:
            index = lax.broadcasted_iota(jnp.int32, (LANES - head_dim, 1), 0)

            @pl.loop(0, length // TILE // 2)
            def _(n):
                for part, o_ref in enumerate((even_ref, odd_ref)):
                    rows = at(2 * n + part)
                    g = g_ref[n, :, part * TILE : (part + 1) * TILE]
                    product = g.astype(F32) * o_ref[n].astype(F32)
                    for h in range(heads):
                        delta = -jnp.sum(product[own(h)], axis=0, keepdims=True)
                        gaug_ref[h * LANES : h * LANES + head_dim, rows] = g[own(h)]
                        gaug_ref[h * LANES + head_dim : (h + 1) * LANES, rows] = jnp.where(
                            index < PARTS, spread(delta, index, 0), 0.0
                        ).astype(BF16)

    dk_ref[...] = jnp.zeros_like(dk_ref)
    dv_ref[...] = jnp.zeros_like(dv_ref)
    keys = [k_ref[:, cols(h)] for h in range(heads)]
    turned = [jnp.transpose(k.astype(F32)).astype(BF16) for k in keys]

    def one(block, masked):
        for h in range(heads):
            q = aug_ref[cols(h), at(block)]
            g = gaug_ref[cols(h), at(block)]
            s = dot_nn(keys[h], q)
            if masked:
                key = lax.broadcasted_iota(jnp.int32, (TILE, TILE), 0)
                query = lax.broadcasted_iota(jnp.int32, (TILE, TILE), 1)
                s = jnp.where(key <= query, s, -BIG)
            p = jnp.exp(s)
            d = dot_nn(v_ref[:, cols(h)], g)
            dv_ref[:, cols(h)] += dot_nt(p.astype(BF16), g)
            ds = (p * d).astype(BF16)
            dk_ref[:, cols(h)] += dot_nt(ds, q)
            dq_ref[cols(h), at(block)] += dot_nn(turned[h], ds)

    one(step, True)

    @pl.loop(step + 1, ends[step])
    def _(block):
        one(block, False)

    pieces = []
    for ref in (dk_ref, dv_ref):
        for h in range(heads):
            pieces.append(jnp.transpose(ref[:, cols(h)])[:head_dim].astype(BF16))
    if parity == 0:
        for n, piece in enumerate(pieces):
            kv_ref[0, n * head_dim : (n + 1) * head_dim, :] = piece
    else:
        for n, piece in enumerate(pieces):
            all_ref[0, 2 * unit + n * head_dim : 2 * unit + (n + 1) * head_dim, :] = piece
        for part in range(2):
            rows = at(step - 1 + part)
            for h in range(heads):
                dq = (dq_in_ref[cols(h), rows] + dq_ref[cols(h), rows]).astype(BF16).astype(F32)
                all_ref[0, part * unit + h * head_dim : part * unit + (h + 1) * head_dim, :] = (
                    dq * scale_ref[...]
                )[:head_dim].astype(BF16)


def attend_back(ends, aug, k, v, others, parity, heads, head_dim):
    width, length = aug.shape
    steps = length // TILE // 2
    unit = heads * head_dim
    whole = lambda *shape: pl.BlockSpec(shape, lambda n, st: (0,) * len(shape))
    row = pl.BlockSpec((TILE, width), lambda n, st: (2 * n + parity, 0))
    out = lambda rows: pl.BlockSpec((1, rows, TILE), lambda n, st: (n, 0, 0))
    scratch = [pltpu.VMEM((TILE, width), F32)] * 2
    if parity == 0:
        in_specs = [whole(*value.shape) for value in others]
        out_shape = [
            jax.ShapeDtypeStruct((steps, 2 * unit, TILE), BF16),
            jax.ShapeDtypeStruct((width, length), BF16),
            jax.ShapeDtypeStruct((width, length), F32),
        ]
        out_specs = [out(2 * unit), whole(width, length), whole(width, length)]
    else:
        in_specs = [whole(*value.shape) for value in others]
        out_shape = jax.ShapeDtypeStruct((steps, 4 * unit, TILE), BF16)
        out_specs = out(4 * unit)
        scratch = [pltpu.VMEM((width, length), F32)] + scratch
    return pl.pallas_call(
        functools.partial(attend_back_kernel, heads=heads, head_dim=head_dim, parity=parity),
        out_shape=out_shape,
        grid_spec=pltpu.PrefetchScalarGridSpec(
            num_scalar_prefetch=1,
            grid=(steps,),
            in_specs=[whole(width, length), row, row, *in_specs],
            out_specs=out_specs,
            scratch_shapes=scratch,
        ),
        compiler_params=pltpu.CompilerParams(vmem_limit_bytes=VMEM_LIMIT),
        cost_estimate=pl.CostEstimate(
            flops=30 * heads * length * 1024 * LANES, bytes_accessed=10 * length * width, transcendentals=0
        ),
        name="attend_back",
    )(ends, aug, k, v, *others)


def rms_scale(values):
    return lax.rsqrt(jnp.mean(values * values, axis=-1, keepdims=True) + EPSILON)


def rms_back(values, scale_rows, grad_normed):
    cubed = scale_rows * scale_rows * scale_rows
    return scale_rows * grad_normed - values * cubed * jnp.mean(
        grad_normed * values, axis=-1, keepdims=True
    )


def after(value, *others):
    return lax.optimization_barrier((value, others))[0]


def together(*values):
    return lax.optimization_barrier(values)


def own_and_sent(value, own, masks):
    return [
        piece_of(value, own) if m == 0 else xor_permute(piece_of(value, own ^ m), "sp", m) for m in masks
    ]


def in_order(pieces, own):
    stacked = jnp.stack(pieces)
    return jnp.stack([piece_of(stacked, n ^ own) for n in range(len(pieces))], axis=0)


def direct_shares(part, n_fs):
    fs = lax.axis_index("fs")
    split = part.reshape(n_fs, part.shape[0] // n_fs, part.shape[1])
    return [
        piece_of(split, fs) if m == 0 else xor_permute(piece_of(split, fs ^ m), "fs", m) for m in range(n_fs)
    ]


def over_sequences(part, groups, n_sp):
    mask = groups
    while mask < n_sp:
        part = part + xor_permute(part, "sp", mask)
        mask <<= 1
    return [part] + [xor_permute(part, "sp", m) for m in range(1, groups)]


def fold(pieces, adapter_index, adapters, own):
    by_seq = in_order(pieces, own)
    tables = []
    for a in range(adapters):
        table = jnp.zeros_like(pieces[0])
        for s in range(len(pieces)):
            table = table + jnp.where(adapter_index[s, 0] == a, by_seq[s], 0.0)
        tables.append(table)
    return jnp.stack(tables)


def joined_rows(every):
    n, adapters, rows, model = every.shape
    return jnp.swapaxes(every, 0, 1).reshape(adapters, n * rows, model)


def local(
    layer_input,
    output_grad,
    segment_ids,
    adapter_index,
    gain_attention,
    gain_feedforward,
    query_scale,
    weight_qkv,
    weight_mixer,
    weight_expand,
    weight_contract,
    qkv_down,
    qkv_up,
    mixer_down,
    mixer_up,
    expand_down,
    expand_up,
    contract_down,
    contract_up,
):
    sequences, tokens, model = layer_input.shape
    head_dim = query_scale.shape[0]
    n_fs, n_sp = lax.axis_size("fs"), lax.axis_size("sp")
    adapters, rank = qkv_down.shape[0], qkv_down.shape[2]
    length = segment_ids.shape[1]
    folds = n_sp // sequences
    heads = model // head_dim // n_fs
    unit = heads * head_dim
    width = heads * LANES
    rows = sequences * tokens
    fs = lax.axis_index("fs")
    sp = lax.axis_index("sp")
    own = sp % sequences
    fold_of = sp // sequences

    pick = piece_of(adapter_index, own)[0]
    downs = [piece_of(t, pick) for t in (qkv_down, mixer_down, expand_down, contract_down)]
    ups = [piece_of(t, pick) for t in (qkv_up, mixer_up, expand_up, contract_up)]

    def merged(weight, down, up):
        cols = weight.shape[1]
        own_up = lax.dynamic_slice_in_dim(up, fs * cols, cols, 1)
        return (weight.astype(F32) + dot_nn(down, own_up)).astype(BF16)

    shard = merged(weight_qkv, downs[0], ups[0])
    inverse = pow(3, -1, n_fs)
    received = [
        lax.ppermute(
            shard[:, t * unit : (t + 1) * unit], "fs", [(d, (3 * d + t) % n_fs) for d in range(n_fs)]
        )
        for t in range(3)
    ]
    places = [(3 * ((inverse * (fs - t)) % n_fs) + t) // n_fs for t in range(3)]
    w_parts = []
    for b in range(3):
        part = jnp.zeros_like(received[0])
        for t in range(3):
            part = jnp.where(places[t] == b, received[t], part)
        w_parts.append(part)
    w_own = jnp.concatenate(w_parts, axis=1)
    w_padded = jnp.pad(
        w_own.reshape(model, 3 * heads, head_dim), ((0, 0), (0, 0), (0, LANES - head_dim))
    ).reshape(model, 3 * width)

    segs = piece_of(segment_ids, own)
    scale = query_scale * (1.0 / math.sqrt(head_dim))
    scale_pad = jnp.pad(scale, (0, LANES - head_dim))[None]
    col_scale = jnp.concatenate([jnp.tile(scale_pad, (1, heads)), jnp.ones((1, 2 * width), F32)], axis=1)
    lane = jnp.arange(LANES)[None, :]
    marks = lane >= head_dim + PARTS
    same = lane == segs[:, None] + (head_dim + PARTS)
    qpad = same.astype(BF16)
    kpad = jnp.where(
        marks, jnp.where(same, 0.0, -BIG), jnp.where(lane >= head_dim, 1.0, 0.0)
    ).astype(BF16)

    project_args = (gain_attention[None], w_padded, col_scale, qpad, kpad)
    as_table = lambda *s: jnp.stack(s).astype(jnp.int32)
    if n_fs == 8 and folds == 1 and sequences == 4 and 2 * tokens == TILE:
        pieces = own_and_sent(layer_input, own, (0, 1))
        pieces += own_and_sent(after(layer_input, pieces[1]), own, (2, 3))
        odd = own % 2 == 1
        upper = own // 2

        def pair(low, high):
            return jnp.where(odd, jnp.concatenate([high, low], 0), jnp.concatenate([low, high], 0))

        def to(value, mask):
            return xor_permute(value, "fs", mask)

        def fill(blocks, place, earlier):
            sources = [block for _, block in blocks]
            tiles = as_table(*[(fs ^ mask) * 2 + place for mask, _ in blocks])
            return project(sources, tiles, *project_args, earlier, heads, head_dim, length)

        other = 1 - upper
        first = pair(pieces[0], pieces[1])
        half = TILE // 2
        y1, x1, c1 = to(first, 4), to(first, 2), to(first, 1)
        y1, x1, c1 = together(y1, x1, c1)
        top1, bottom1, cy1, cx1 = to(y1[:half], 2), to(x1[half:], 4), to(y1, 1), to(x1, 1)
        qkv = fill([(0, first), (1, c1), (4, y1), (2, x1)], upper, None)
        *qkv, top1, bottom1, cy1, cx1, p2, p3 = together(*qkv, top1, bottom1, cy1, cx1, pieces[2], pieces[3])
        both1 = jnp.concatenate([top1, bottom1], axis=0)
        second = pair(p2, p3)
        y2, x2, c2, cb1 = to(second, 4), to(second, 2), to(second, 1), to(both1, 1)
        qkv = fill([(5, cy1), (3, cx1)], upper, qkv)
        *qkv, y2, x2, c2, cb1 = together(*qkv, y2, x2, c2, cb1)
        top2, bottom2, cy2, cx2 = to(y2[:half], 2), to(x2[half:], 4), to(y2, 1), to(x2, 1)
        qkv = fill([(6, both1), (7, cb1)], upper, qkv)
        qkv = fill([(0, second), (1, c2)], other, qkv)
        *qkv, top2, bottom2, cy2, cx2 = together(*qkv, top2, bottom2, cy2, cx2)
        both2 = jnp.concatenate([top2, bottom2], axis=0)
        cb2 = to(both2, 1)
        qkv = fill([(4, y2), (2, x2), (5, cy2), (3, cx2)], other, qkv)
        *qkv, cb2 = together(*qkv, cb2)
        qkv = fill([(6, both2), (7, cb2)], other, qkv)
        x_own = jnp.where(
            upper == 0, jnp.concatenate([first, second], 0), jnp.concatenate([second, first], 0)
        )
        x_sent, x_here = (p2, p3), (both2,)
    else:
        pieces = own_and_sent(layer_input, own, range(sequences))
        x_own = in_order(pieces, own).reshape(rows, model)
        gathered = lax.all_gather(x_own, ("fs", "sp"), axis=0)
        gathered = gathered.reshape(n_fs, folds, sequences, rows, model)
        gathered = lax.dynamic_index_in_dim(gathered, own, 2, keepdims=False)
        blocks = gathered.reshape(n_fs * folds, rows, model)
        tiles = jnp.arange(length // TILE, dtype=jnp.int32)
        qkv = project([blocks], tiles, *project_args, None, heads, head_dim, length)
        x_sent, x_here = (x_own,), (blocks,)
    q, k, v = qkv

    three = jnp.stack(
        [
            merged(w, d, u).T
            for w, d, u in zip((weight_mixer, weight_expand, weight_contract), downs[1:], ups[1:])
        ]
    )
    w_mixer, w_expand, w_contract = lax.all_gather(after(three, *x_here), "fs", axis=1, tiled=True)
    g_pieces = own_and_sent(after(output_grad, *x_sent), own, range(sequences))

    firsts, lasts = segs[::TILE], segs[TILE - 1 :: TILE]
    starts = jnp.sum(segs[None, :] < firsts[:, None], axis=1, dtype=jnp.int32) // TILE
    ends = (jnp.sum(segs[None, :] <= lasts[:, None], axis=1, dtype=jnp.int32) + TILE - 1) // TILE

    def sections_out(value):
        if folds > 1:
            cut = value.reshape(n_fs, folds, *value.shape[1:])
            value = lax.dynamic_index_in_dim(cut, fold_of, 1, keepdims=False)
        return lax.all_to_all(value, "fs", split_axis=0, concat_axis=0, tiled=True)

    o_even, aug = attend(starts, q, k, v, None, 0, heads, head_dim)
    a_even = sections_out(o_even)
    o_odd, aug = attend(starts, q, k, v, aug, 1, heads, head_dim)
    o_odd, a_even, g_pieces = together(o_odd, a_even, g_pieces)
    a_odd = sections_out(o_odd)
    attended = jnp.concatenate([a_even, a_odd], axis=2).reshape(model, rows)
    g_own = in_order(g_pieces, own).reshape(rows, model)

    x_f = x_own.astype(F32)
    scale_one = rms_scale(x_f)
    normed_one = (x_f * scale_one * gain_attention).astype(BF16)
    narrow = lambda u, down: dot_nn(u, down).astype(BF16)
    mixer = lax.dot_general(attended, w_mixer, (((0,), (1,)), ((), ())), preferred_element_type=F32)
    middle = x_f + mixer
    scale_two = rms_scale(middle)
    normed_two = (middle * scale_two * gain_feedforward).astype(BF16)
    expanded = dot_nt(normed_two, w_expand)
    gate = jax.nn.sigmoid(expanded)
    hidden = (expanded * gate).astype(BF16)
    contracted = dot_nt(hidden, w_contract)
    layer_output = (middle + contracted).astype(BF16).reshape(sequences, tokens, model)

    def adapter_back(u, grad, down, up):
        grad_up = dot_tn(narrow(u, down), grad)
        grad_narrow = dot_nt(grad, up).astype(BF16)
        return [dot_tn(grad_narrow, u), grad_up]

    grad_hidden = dot_nn(g_own, w_contract)
    grad_expanded = (grad_hidden * gate * (1.0 + expanded * (1.0 - gate))).astype(BF16)
    grad_normed_two = dot_nn(grad_expanded, w_expand)
    grad_middle = g_own.astype(F32) + rms_back(middle, scale_two, grad_normed_two * gain_feedforward)
    grad_mixer = grad_middle.astype(BF16)
    grad_attended = lax.dot_general(w_mixer, grad_mixer, (((0,), (1,)), ((), ())), preferred_element_type=F32)
    grad_heads = lax.all_to_all(
        grad_attended.astype(BF16).reshape(n_fs, unit, rows), "fs", split_axis=0, concat_axis=0, tiled=True
    )
    if folds > 1:
        every = lax.all_gather(grad_heads, "sp", axis=0)
        every = every.reshape(folds, sequences, n_fs, unit, rows)
        every = lax.dynamic_index_in_dim(every, own, 1, keepdims=False)
        grad_heads = jnp.swapaxes(every, 0, 1).reshape(n_fs * folds, unit, rows)

    narrow_mixer = dot_tn(attended, downs[1]).astype(BF16)
    early = jnp.concatenate(
        [
            lax.dot_general(
                dot_nt(grad_mixer, ups[1]).astype(BF16), attended, (((0,), (1,)), ((), ())), preferred_element_type=F32
            ),
            dot_tn(narrow_mixer, grad_mixer),
            *adapter_back(normed_two, grad_expanded, downs[2], ups[2]),
            *adapter_back(hidden, g_own, downs[3], ups[3]),
        ],
        axis=0,
    )
    grad_heads, early, layer_output = together(grad_heads, early, layer_output)
    w_all = lax.all_gather(after(w_own.T, grad_heads), "fs", axis=0)
    early = lax.all_to_all(
        early.reshape(n_fs, early.shape[0] // n_fs, model), "fs", split_axis=0, concat_axis=0, tiled=True
    )
    out_pieces = own_and_sent(layer_output, own, range(sequences))

    kv_even, g_aug, dq = attend_back(ends, aug, k, v, (grad_heads, o_even, o_odd), 0, heads, head_dim)
    kv_even, g_aug, dq, early, out_pieces = together(kv_even, g_aug, dq, early, out_pieces)
    kv_even = sections_out(kv_even)
    early = over_sequences(jnp.sum(early, axis=0), sequences, n_sp)
    grads_odd = attend_back(ends, aug, k, v, (g_aug, dq, scale_pad.T), 1, heads, head_dim)
    grads_odd, kv_even, early, w_all = together(grads_odd, kv_even, early, w_all)
    grads_odd = sections_out(grads_odd)
    early = fold(early, adapter_index, adapters, own)
    grad_joined = jnp.concatenate(
        [
            jnp.concatenate([grads_odd[:, :unit], kv_even], axis=1),
            jnp.concatenate([grads_odd[:, unit : 2 * unit], grads_odd[:, 2 * unit :]], axis=1),
        ],
        axis=2,
    )
    layer_output = in_order(out_pieces, own)

    up_all = (
        ups[0].reshape(rank, 3, n_fs, unit).transpose(2, 0, 1, 3).reshape(n_fs, rank, 3 * unit)
    )
    narrow_one = narrow(normed_one, downs[0])
    grad_up = jnp.einsum("tr,hct->rhc", narrow_one, grad_joined, preferred_element_type=F32)
    grad_up = grad_up.reshape(rank, n_fs, 3, unit).transpose(0, 2, 1, 3).reshape(3 * rank, model)
    grad_narrow = jnp.einsum("hct,hrc->tr", grad_joined, up_all, preferred_element_type=F32).astype(BF16)
    late = jnp.concatenate([dot_tn(grad_narrow, normed_one), grad_up], axis=0)
    grad_joined, late = together(grad_joined, late)
    late = direct_shares(late, n_fs)
    early = [early] + [xor_permute(early, "fs", m) for m in range(1, n_fs)]
    grad_normed_one = jnp.einsum("hct,hcd->td", grad_joined, w_all, preferred_element_type=F32)
    input_grad = grad_middle + rms_back(x_f, scale_one, grad_normed_one * gain_attention)
    input_grad = input_grad.astype(BF16).reshape(sequences, tokens, model)
    input_grad, late, early[0] = together(input_grad, late, early[0])
    late = over_sequences(sum(late[1:], late[0]), sequences, n_sp)
    in_pieces = own_and_sent(input_grad, own, range(sequences))
    in_pieces[-1], late, early = together(in_pieces[-1], late, early)
    early = in_order(early, fs)
    late = fold(late, adapter_index, adapters, own)
    late = in_order([late] + [xor_permute(late, "fs", m) for m in range(1, n_fs)], fs)
    input_grad = in_order(in_pieces, own)

    factor = 1.0 / math.sqrt(length)
    outs = []
    late, early = joined_rows(late) * factor, joined_rows(early) * factor
    for tables, wides in ((late, (3,)), (early, (1, 1, 1))):
        first = 0
        for wide in wides:
            outs.append(jnp.swapaxes(tables[:, first : first + rank], 1, 2))
            first += rank
            outs.append(tables[:, first : first + rank * wide].reshape(adapters, rank, wide * model))
            first += rank * wide
    return (layer_output, input_grad, *outs)


def solution(mesh):
    tokens = P(None, ("fs", "sp"), None)
    in_specs = (tokens, tokens) + (P(),) * 5 + (P(None, "fs"),) * 4 + (P(),) * 8
    out_specs = (tokens, tokens) + (P(),) * 8
    return jax.shard_map(local, mesh=mesh, in_specs=in_specs, out_specs=out_specs, check_vma=False)
```

```python
import functools
import math

import jax
import jax.numpy as jnp
from jax import lax
from jax.experimental import pallas as pl
from jax.experimental.pallas import tpu as pltpu
from jax.sharding import PartitionSpec as P

EPSILON = 1e-06
BIG = 1e30
LANES = 128
PARTS = 3
TILE = 256
VMEM_LIMIT = 64000000
F32 = jnp.float32
BF16 = jnp.bfloat16
NT = (((1,), (1,)), ((), ()))
TN = (((0,), (0,)), ((), ()))


def dot_nn(a, b):
    return jnp.dot(a, b, preferred_element_type=F32)


def dot_nt(a, b):
    return lax.dot_general(a, b, NT, preferred_element_type=F32)


def dot_tn(a, b):
    return lax.dot_general(a, b, TN, preferred_element_type=F32)


def xor_permute(value, axis, mask):
    count = lax.axis_size(axis)
    return lax.ppermute(value, axis, [(a, a ^ mask) for a in range(count)])


def piece_of(stacked, index):
    return lax.dynamic_index_in_dim(stacked, index, 0, keepdims=False)


def project_kernel(tiles, *refs, count, heads, head_dim):
    x_refs, (gain_ref, w_ref, scale_ref, qpad_ref, kpad_ref) = refs[:count], refs[count : count + 5]
    q_ref, k_ref, v_ref, x_ref = refs[-4:]
    if count > 1:
        for n in range(count):

            @pl.when(pl.program_id(0) == n)
            def _():
                x_ref[...] = x_refs[n][...]

        x = x_ref[...].astype(F32)
    else:
        x = x_refs[0][0].astype(F32)
    mean = jnp.mean(x * x, axis=-1, keepdims=True)
    normed = (x * lax.rsqrt(mean + EPSILON) * gain_ref[...]).astype(BF16)
    rows = dot_nn(normed, w_ref[...]) * scale_ref[...]
    width = heads * LANES
    lane = lax.broadcasted_iota(jnp.int32, (1, width), 1) % LANES
    q_ref[...] = (rows[:, :width] + jnp.tile(qpad_ref[...].astype(F32), (1, heads))).astype(BF16)
    k_ref[...] = (rows[:, width : 2 * width] + jnp.tile(kpad_ref[...].astype(F32), (1, heads))).astype(BF16)
    ones = jnp.where((lane >= head_dim) & (lane < head_dim + PARTS), 1.0, 0.0)
    v_ref[...] = (rows[:, 2 * width :] + ones).astype(BF16)


def project(sources, tiles, gain, weight, scale, qpad, kpad, earlier, heads, head_dim, length):
    model = weight.shape[0]
    step = TILE
    count = len(sources)
    steps = tiles.shape[0]
    width = heads * LANES
    out = pl.BlockSpec((step, width), lambda n, t: (t[n], 0))
    pad = pl.BlockSpec((step, LANES), lambda n, t: (t[n], 0))
    fixed = lambda shape: pl.BlockSpec(shape, lambda n, t: (0,) * len(shape))
    if count > 1:
        in_specs = [fixed((step, model))] * count
    else:
        per = sources[0].shape[1] // step
        in_specs = [pl.BlockSpec((1, step, model), lambda n, t: (n // per, n % per, 0))]
    in_specs += [fixed((1, model)), fixed((model, 3 * width)), fixed((1, 3 * width)), pad, pad]
    operands = [*sources, gain, weight, scale, qpad, kpad]
    aliases = {}
    if earlier is not None:
        in_specs += [pl.BlockSpec(memory_space=pl.ANY)] * 3
        aliases = {1 + len(operands) + n: n for n in range(3)}
        operands += list(earlier)
    return pl.pallas_call(
        functools.partial(project_kernel, count=count, heads=heads, head_dim=head_dim),
        out_shape=[jax.ShapeDtypeStruct((length, width), BF16)] * 3,
        grid_spec=pltpu.PrefetchScalarGridSpec(
            num_scalar_prefetch=1,
            grid=(steps,),
            in_specs=in_specs,
            out_specs=[out] * 3,
            scratch_shapes=[pltpu.VMEM((step, model), BF16)],
        ),
        input_output_aliases=aliases,
        compiler_params=pltpu.CompilerParams(vmem_limit_bytes=VMEM_LIMIT),
        cost_estimate=pl.CostEstimate(
            flops=1,
            bytes_accessed=1,
            transcendentals=0,
        ),
        name="project",
    )(tiles, *operands)


def spread(row, index, first):
    high = row.astype(BF16).astype(F32)
    middle = (row - high).astype(BF16).astype(F32)
    last = row - high - middle
    return jnp.where(index == first, high, jnp.where(index == first + 1, middle, last))


def at(block):
    return pl.ds(pl.multiple_of(block * TILE, TILE), TILE)


def attend_kernel(starts, q_ref, k_ref, v_ref, *refs, heads, head_dim, parity):
    o_ref, aug_ref = refs[-2:]
    step = 2 * pl.program_id(0) + parity
    first = starts[step]
    index = lax.broadcasted_iota(jnp.int32, (LANES, 1), 0)
    marks = (index >= head_dim) & (index < head_dim + PARTS)

    def cols(h):
        return pl.ds(h * LANES, LANES)

    turned = [jnp.transpose(q_ref[:, cols(h)].astype(F32)) for h in range(heads)]
    queries = [t.astype(BF16) for t in turned]

    def one(block, carry, masked):
        scores = [dot_nn(k_ref[at(block), cols(h)], queries[h]) for h in range(heads)]
        out = []
        for h, s in enumerate(scores):
            if masked:
                key = lax.broadcasted_iota(jnp.int32, (TILE, TILE), 0)
                query = lax.broadcasted_iota(jnp.int32, (TILE, TILE), 1)
                s = jnp.where(key <= query, s, -BIG)
            peak = jnp.max(s, axis=0, keepdims=True)
            if not masked:
                peak = jnp.maximum(carry[h][0], peak)
            p = jnp.exp(s - peak).astype(BF16)
            total = dot_tn(v_ref[at(block), cols(h)], p)
            if not masked:
                total = carry[h][1] * jnp.exp(carry[h][0] - peak) + total
            out.append((peak, total))
        return tuple(out)

    carry = one(step, None, True)
    carry = lax.fori_loop(first, step, lambda block, c: one(block, c, False), carry)
    for h in range(heads):
        peak, total = carry[h]
        weight = total[head_dim : head_dim + 1]
        o_ref[0, h * head_dim : (h + 1) * head_dim, :] = (total / weight)[:head_dim].astype(BF16)
        lse = -(peak + jnp.log(weight))
        aug_ref[cols(h), :] = jnp.where(marks, spread(lse, index, head_dim), turned[h]).astype(BF16)


def attend(starts, q, k, v, earlier, parity, heads, head_dim):
    length, width = q.shape
    steps = length // TILE // 2
    whole = pl.BlockSpec((length, width), lambda n, st: (0, 0))
    in_specs = [pl.BlockSpec((TILE, width), lambda n, st: (2 * n + parity, 0)), whole, whole]
    operands = [q, k, v]
    aliases = {}
    if earlier is not None:
        in_specs.append(pl.BlockSpec(memory_space=pl.ANY))
        operands.append(earlier)
        aliases = {4: 1}
    return pl.pallas_call(
        functools.partial(attend_kernel, heads=heads, head_dim=head_dim, parity=parity),
        out_shape=[
            jax.ShapeDtypeStruct((steps, heads * head_dim, TILE), BF16),
            jax.ShapeDtypeStruct((width, length), BF16),
        ],
        grid_spec=pltpu.PrefetchScalarGridSpec(
            num_scalar_prefetch=1,
            grid=(steps,),
            in_specs=in_specs,
            out_specs=[
                pl.BlockSpec((1, heads * head_dim, TILE), lambda n, st: (n, 0, 0)),
                pl.BlockSpec((width, TILE), lambda n, st: (0, 2 * n + parity)),
            ],
        ),
        input_output_aliases=aliases,
        compiler_params=pltpu.CompilerParams(vmem_limit_bytes=VMEM_LIMIT),
        cost_estimate=pl.CostEstimate(
            flops=1, bytes_accessed=1, transcendentals=0
        ),
        name="attend",
    )(starts, *operands)


def attend_back_kernel(ends, aug_ref, k_ref, v_ref, *refs, heads, head_dim, parity):
    step = 2 * pl.program_id(0) + parity
    length = aug_ref.shape[1]
    unit = heads * head_dim
    if parity == 0:
        g_ref, even_ref, odd_ref, kv_ref, g_out_ref, dq_ref, dk_ref, dv_ref = refs
        gaug_ref = g_out_ref
    else:
        gaug_ref, dq_in_ref, scale_ref, all_ref, dq_ref, dk_ref, dv_ref = refs

    def cols(h):
        return pl.ds(h * LANES, LANES)

    def own(h):
        return slice(h * head_dim, (h + 1) * head_dim)

    @pl.when(step == parity)
    def _():
        dq_ref[...] = jnp.zeros_like(dq_ref)
        if parity == 0:
            index = lax.broadcasted_iota(jnp.int32, (LANES - head_dim, 1), 0)

            @pl.loop(0, length // TILE // 2)
            def _(n):
                for part, o_ref in enumerate((even_ref, odd_ref)):
                    rows = at(2 * n + part)
                    g = g_ref[n, :, part * TILE : (part + 1) * TILE]
                    product = g.astype(F32) * o_ref[n].astype(F32)
                    for h in range(heads):
                        delta = -jnp.sum(product[own(h)], axis=0, keepdims=True)
                        gaug_ref[h * LANES : h * LANES + head_dim, rows] = g[own(h)]
                        gaug_ref[h * LANES + head_dim : (h + 1) * LANES, rows] = jnp.where(
                            index < PARTS, spread(delta, index, 0), 0.0
                        ).astype(BF16)

    dk_ref[...] = jnp.zeros_like(dk_ref)
    dv_ref[...] = jnp.zeros_like(dv_ref)
    keys = [k_ref[:, cols(h)] for h in range(heads)]
    turned = [jnp.transpose(k.astype(F32)).astype(BF16) for k in keys]

    def one(block, masked):
        for h in range(heads):
            q = aug_ref[cols(h), at(block)]
            g = gaug_ref[cols(h), at(block)]
            s = dot_nn(keys[h], q)
            if masked:
                key = lax.broadcasted_iota(jnp.int32, (TILE, TILE), 0)
                query = lax.broadcasted_iota(jnp.int32, (TILE, TILE), 1)
                s = jnp.where(key <= query, s, -BIG)
            p = jnp.exp(s)
            d = dot_nn(v_ref[:, cols(h)], g)
            dv_ref[:, cols(h)] += dot_nt(p.astype(BF16), g)
            ds = (p * d).astype(BF16)
            dk_ref[:, cols(h)] += dot_nt(ds, q)
            dq_ref[cols(h), at(block)] += dot_nn(turned[h], ds)

    one(step, True)

    @pl.loop(step + 1, ends[step])
    def _(block):
        one(block, False)

    pieces = []
    for ref in (dk_ref, dv_ref):
        for h in range(heads):
            pieces.append(jnp.transpose(ref[:, cols(h)])[:head_dim].astype(BF16))
    if parity == 0:
        for n, piece in enumerate(pieces):
            kv_ref[0, n * head_dim : (n + 1) * head_dim, :] = piece
    else:
        for n, piece in enumerate(pieces):
            all_ref[0, 2 * unit + n * head_dim : 2 * unit + (n + 1) * head_dim, :] = piece
        for part in range(2):
            rows = at(step - 1 + part)
            for h in range(heads):
                dq = (dq_in_ref[cols(h), rows] + dq_ref[cols(h), rows]).astype(BF16).astype(F32)
                all_ref[0, part * unit + h * head_dim : part * unit + (h + 1) * head_dim, :] = (
                    dq * scale_ref[...]
                )[:head_dim].astype(BF16)


def attend_back(ends, aug, k, v, others, parity, heads, head_dim):
    width, length = aug.shape
    steps = length // TILE // 2
    unit = heads * head_dim
    whole = lambda *shape: pl.BlockSpec(shape, lambda n, st: (0,) * len(shape))
    row = pl.BlockSpec((TILE, width), lambda n, st: (2 * n + parity, 0))
    out = lambda rows: pl.BlockSpec((1, rows, TILE), lambda n, st: (n, 0, 0))
    scratch = [pltpu.VMEM((TILE, width), F32)] * 2
    if parity == 0:
        in_specs = [whole(*value.shape) for value in others]
        out_shape = [
            jax.ShapeDtypeStruct((steps, 2 * unit, TILE), BF16),
            jax.ShapeDtypeStruct((width, length), BF16),
            jax.ShapeDtypeStruct((width, length), F32),
        ]
        out_specs = [out(2 * unit), whole(width, length), whole(width, length)]
    else:
        in_specs = [whole(*value.shape) for value in others]
        out_shape = jax.ShapeDtypeStruct((steps, 4 * unit, TILE), BF16)
        out_specs = out(4 * unit)
        scratch = [pltpu.VMEM((width, length), F32)] + scratch
    return pl.pallas_call(
        functools.partial(attend_back_kernel, heads=heads, head_dim=head_dim, parity=parity),
        out_shape=out_shape,
        grid_spec=pltpu.PrefetchScalarGridSpec(
            num_scalar_prefetch=1,
            grid=(steps,),
            in_specs=[whole(width, length), row, row, *in_specs],
            out_specs=out_specs,
            scratch_shapes=scratch,
        ),
        compiler_params=pltpu.CompilerParams(vmem_limit_bytes=VMEM_LIMIT),
        cost_estimate=pl.CostEstimate(
            flops=1, bytes_accessed=1, transcendentals=0
        ),
        name="attend_back",
    )(ends, aug, k, v, *others)


def rms_scale(values):
    return lax.rsqrt(jnp.mean(values * values, axis=-1, keepdims=True) + EPSILON)


def rms_back(values, scale_rows, grad_normed):
    cubed = scale_rows * scale_rows * scale_rows
    return scale_rows * grad_normed - values * cubed * jnp.mean(
        grad_normed * values, axis=-1, keepdims=True
    )


def after(value, *others):
    return lax.optimization_barrier((value, others))[0]


def together(*values):
    return lax.optimization_barrier(values)


def own_and_sent(value, own, masks):
    return [
        piece_of(value, own) if m == 0 else xor_permute(piece_of(value, own ^ m), "sp", m) for m in masks
    ]


def in_order(pieces, own):
    stacked = jnp.stack(pieces)
    return jnp.stack([piece_of(stacked, n ^ own) for n in range(len(pieces))], axis=0)


def shares_of_all(table, n_fs, pieces):
    to = lambda value, mask: xor_permute(value, "fs", mask)
    if n_fs != 8 or table.shape[0] % 2:
        return [table] + [to(table, m) for m in range(1, n_fs)]
    half = table.shape[0] // 2
    y, x, core, pieces[2] = together(to(table, 4), to(table, 2), to(table, 1), pieces[2])
    top, bottom, core_y, core_x = to(y[:half], 2), to(x[half:], 4), to(y, 1), to(x, 1)
    top, bottom, core_y, core_x, pieces[3] = together(top, bottom, core_y, core_x, pieces[3])
    both = jnp.concatenate([top, bottom], axis=0)
    return [table, core, x, core_x, y, core_y, both, to(both, 1)]


def over_sequences(part, groups, n_sp):
    mask = groups
    while mask < n_sp:
        part = part + xor_permute(part, "sp", mask)
        mask <<= 1
    return [part] + [xor_permute(part, "sp", m) for m in range(1, groups)]


def fold(pieces, adapter_index, adapters, own):
    by_seq = in_order(pieces, own)
    tables = []
    for a in range(adapters):
        table = jnp.zeros_like(pieces[0])
        for s in range(len(pieces)):
            table = table + jnp.where(adapter_index[s, 0] == a, by_seq[s], 0.0)
        tables.append(table)
    return jnp.stack(tables)


def joined_rows(every):
    n, adapters, rows, model = every.shape
    return jnp.swapaxes(every, 0, 1).reshape(adapters, n * rows, model)


def local(
    layer_input,
    output_grad,
    segment_ids,
    adapter_index,
    gain_attention,
    gain_feedforward,
    query_scale,
    weight_qkv,
    weight_mixer,
    weight_expand,
    weight_contract,
    qkv_down,
    qkv_up,
    mixer_down,
    mixer_up,
    expand_down,
    expand_up,
    contract_down,
    contract_up,
):
    sequences, tokens, model = layer_input.shape
    head_dim = query_scale.shape[0]
    n_fs, n_sp = lax.axis_size("fs"), lax.axis_size("sp")
    adapters, rank = qkv_down.shape[0], qkv_down.shape[2]
    length = segment_ids.shape[1]
    folds = n_sp // sequences
    heads = model // head_dim // n_fs
    unit = heads * head_dim
    width = heads * LANES
    rows = sequences * tokens
    fs = lax.axis_index("fs")
    sp = lax.axis_index("sp")
    own = sp % sequences
    fold_of = sp // sequences

    pick = piece_of(adapter_index, own)[0]
    downs = [piece_of(t, pick) for t in (qkv_down, mixer_down, expand_down, contract_down)]
    ups = [piece_of(t, pick) for t in (qkv_up, mixer_up, expand_up, contract_up)]

    def merged(weight, down, up):
        cols = weight.shape[1]
        own_up = lax.dynamic_slice_in_dim(up, fs * cols, cols, 1)
        return (weight.astype(F32) + dot_nn(down, own_up)).astype(BF16)

    shard = merged(weight_qkv, downs[0], ups[0])
    inverse = pow(3, -1, n_fs)
    received = [
        lax.ppermute(
            shard[:, t * unit : (t + 1) * unit], "fs", [(d, (3 * d + t) % n_fs) for d in range(n_fs)]
        )
        for t in range(3)
    ]
    places = [(3 * ((inverse * (fs - t)) % n_fs) + t) // n_fs for t in range(3)]
    w_parts = []
    for b in range(3):
        part = jnp.zeros_like(received[0])
        for t in range(3):
            part = jnp.where(places[t] == b, received[t], part)
        w_parts.append(part)
    w_own = jnp.concatenate(w_parts, axis=1)
    w_padded = jnp.pad(
        w_own.reshape(model, 3 * heads, head_dim), ((0, 0), (0, 0), (0, LANES - head_dim))
    ).reshape(model, 3 * width)

    segs = piece_of(segment_ids, own)
    scale = query_scale * (1.0 / math.sqrt(head_dim))
    scale_pad = jnp.pad(scale, (0, LANES - head_dim))[None]
    col_scale = jnp.concatenate([jnp.tile(scale_pad, (1, heads)), jnp.ones((1, 2 * width), F32)], axis=1)
    lane = jnp.arange(LANES)[None, :]
    marks = lane >= head_dim + PARTS
    same = lane == segs[:, None] + (head_dim + PARTS)
    qpad = same.astype(BF16)
    kpad = jnp.where(
        marks, jnp.where(same, 0.0, -BIG), jnp.where(lane >= head_dim, 1.0, 0.0)
    ).astype(BF16)

    project_args = (gain_attention[None], w_padded, col_scale, qpad, kpad)
    as_table = lambda *s: jnp.stack(s).astype(jnp.int32)
    if n_fs == 8 and folds == 1 and sequences == 4 and 2 * tokens == TILE:
        pieces = own_and_sent(layer_input, own, (0, 1))
        pieces += own_and_sent(layer_input, own, (2, 3))
        odd = own % 2 == 1
        upper = own // 2

        def pair(low, high):
            return jnp.where(odd, jnp.concatenate([high, low], 0), jnp.concatenate([low, high], 0))

        def to(value, mask):
            return xor_permute(value, "fs", mask)

        def fill(blocks, place, earlier):
            sources = [block for _, block in blocks]
            tiles = as_table(*[(fs ^ mask) * 2 + place for mask, _ in blocks])
            return project(sources, tiles, *project_args, earlier, heads, head_dim, length)

        other = 1 - upper
        first = pair(pieces[0], pieces[1])
        half = TILE // 2
        y1, x1, c1 = to(first, 4), to(first, 2), to(first, 1)
        y1, x1, c1 = together(y1, x1, c1)
        top1, bottom1, cy1, cx1 = to(y1[:half], 2), to(x1[half:], 4), to(y1, 1), to(x1, 1)
        qkv = fill([(0, first), (1, c1), (4, y1), (2, x1)], upper, None)
        *qkv, top1, bottom1, cy1, cx1, p2, p3 = together(*qkv, top1, bottom1, cy1, cx1, pieces[2], pieces[3])
        both1 = jnp.concatenate([top1, bottom1], axis=0)
        second = pair(p2, p3)
        y2, x2, c2, cb1 = to(second, 4), to(second, 2), to(second, 1), to(both1, 1)
        qkv = fill([(5, cy1), (3, cx1)], upper, qkv)
        *qkv, y2, x2, c2, cb1 = together(*qkv, y2, x2, c2, cb1)
        top2, bottom2, cy2, cx2 = to(y2[:half], 2), to(x2[half:], 4), to(y2, 1), to(x2, 1)
        qkv = fill([(6, both1), (7, cb1)], upper, qkv)
        qkv = fill([(0, second), (1, c2)], other, qkv)
        *qkv, top2, bottom2, cy2, cx2 = together(*qkv, top2, bottom2, cy2, cx2)
        both2 = jnp.concatenate([top2, bottom2], axis=0)
        cb2 = to(both2, 1)
        qkv = fill([(4, y2), (2, x2), (5, cy2), (3, cx2)], other, qkv)
        *qkv, cb2 = together(*qkv, cb2)
        qkv = fill([(6, both2), (7, cb2)], other, qkv)
        x_own = jnp.where(
            upper == 0, jnp.concatenate([first, second], 0), jnp.concatenate([second, first], 0)
        )
        x_sent, x_here = (p2, p3), (both2,)
    else:
        pieces = own_and_sent(layer_input, own, range(sequences))
        x_own = in_order(pieces, own).reshape(rows, model)
        gathered = lax.all_gather(x_own, ("fs", "sp"), axis=0)
        gathered = gathered.reshape(n_fs, folds, sequences, rows, model)
        gathered = lax.dynamic_index_in_dim(gathered, own, 2, keepdims=False)
        blocks = gathered.reshape(n_fs * folds, rows, model)
        tiles = jnp.arange(length // TILE, dtype=jnp.int32)
        qkv = project([blocks], tiles, *project_args, None, heads, head_dim, length)
        x_sent, x_here = (x_own,), (blocks,)
    q, k, v = qkv

    three = jnp.stack(
        [
            merged(w, d, u).T
            for w, d, u in zip((weight_mixer, weight_expand, weight_contract), downs[1:], ups[1:])
        ]
    )
    w_mixer, w_expand, w_contract = lax.all_gather(after(three, *x_here), "fs", axis=1, tiled=True)
    g_pieces = own_and_sent(after(output_grad, *x_sent), own, range(sequences))

    firsts, lasts = segs[::TILE], segs[TILE - 1 :: TILE]
    starts = jnp.sum(segs[None, :] < firsts[:, None], axis=1, dtype=jnp.int32) // TILE
    ends = (jnp.sum(segs[None, :] <= lasts[:, None], axis=1, dtype=jnp.int32) + TILE - 1) // TILE

    def sections_out(value):
        if folds > 1:
            cut = value.reshape(n_fs, folds, *value.shape[1:])
            value = lax.dynamic_index_in_dim(cut, fold_of, 1, keepdims=False)
        return lax.all_to_all(value, "fs", split_axis=0, concat_axis=0, tiled=True)

    o_even, aug = attend(starts, q, k, v, None, 0, heads, head_dim)
    a_even = sections_out(o_even)
    o_odd, aug = attend(starts, q, k, v, aug, 1, heads, head_dim)
    o_odd, a_even, g_pieces = together(o_odd, a_even, g_pieces)
    a_odd = sections_out(o_odd)
    attended = jnp.concatenate([a_even, a_odd], axis=2).reshape(model, rows)
    g_own = in_order(g_pieces, own).reshape(rows, model)

    x_f = x_own.astype(F32)
    scale_one = rms_scale(x_f)
    normed_one = (x_f * scale_one * gain_attention).astype(BF16)
    narrow = lambda u, down: dot_nn(u, down).astype(BF16)
    mixer = lax.dot_general(attended, w_mixer, (((0,), (1,)), ((), ())), preferred_element_type=F32)
    middle = x_f + mixer
    scale_two = rms_scale(middle)
    normed_two = (middle * scale_two * gain_feedforward).astype(BF16)
    expanded = dot_nt(normed_two, w_expand)
    gate = jax.nn.sigmoid(expanded)
    hidden = (expanded * gate).astype(BF16)
    contracted = dot_nt(hidden, w_contract)
    layer_output = (middle + contracted).astype(BF16).reshape(sequences, tokens, model)

    def adapter_back(u, grad, down, up):
        grad_up = dot_tn(narrow(u, down), grad)
        grad_narrow = dot_nt(grad, up).astype(BF16)
        return [dot_tn(grad_narrow, u), grad_up]

    grad_hidden = dot_nn(g_own, w_contract)
    grad_expanded = (grad_hidden * gate * (1.0 + expanded * (1.0 - gate))).astype(BF16)
    grad_normed_two = dot_nn(grad_expanded, w_expand)
    grad_middle = g_own.astype(F32) + rms_back(middle, scale_two, grad_normed_two * gain_feedforward)
    grad_mixer = grad_middle.astype(BF16)
    grad_attended = lax.dot_general(w_mixer, grad_mixer, (((0,), (1,)), ((), ())), preferred_element_type=F32)
    grad_heads = lax.all_to_all(
        grad_attended.astype(BF16).reshape(n_fs, unit, rows), "fs", split_axis=0, concat_axis=0, tiled=True
    )
    if folds > 1:
        every = lax.all_gather(grad_heads, "sp", axis=0)
        every = every.reshape(folds, sequences, n_fs, unit, rows)
        every = lax.dynamic_index_in_dim(every, own, 1, keepdims=False)
        grad_heads = jnp.swapaxes(every, 0, 1).reshape(n_fs * folds, unit, rows)

    narrow_mixer = dot_tn(attended, downs[1]).astype(BF16)
    early = jnp.concatenate(
        [
            lax.dot_general(
                dot_nt(grad_mixer, ups[1]).astype(BF16), attended, (((0,), (1,)), ((), ())), preferred_element_type=F32
            ),
            dot_tn(narrow_mixer, grad_mixer),
            *adapter_back(normed_two, grad_expanded, downs[2], ups[2]),
            *adapter_back(hidden, g_own, downs[3], ups[3]),
        ],
        axis=0,
    )
    grad_heads, early, layer_output = together(grad_heads, early, layer_output)
    w_all = lax.all_gather(after(w_own.T, grad_heads), "fs", axis=0)
    early = lax.all_to_all(
        early.reshape(n_fs, early.shape[0] // n_fs, model), "fs", split_axis=0, concat_axis=0, tiled=True
    )
    out_pieces = own_and_sent(layer_output, own, range(sequences))

    kv_even, g_aug, dq = attend_back(ends, aug, k, v, (grad_heads, o_even, o_odd), 0, heads, head_dim)
    kv_even, g_aug, dq, early, out_pieces = together(kv_even, g_aug, dq, early, out_pieces)
    kv_even = sections_out(kv_even)
    early = jnp.sum(early, axis=0)
    grads_odd = attend_back(ends, aug, k, v, (g_aug, dq, scale_pad.T), 1, heads, head_dim)
    grads_odd, kv_even, early, w_all = together(grads_odd, kv_even, early, w_all)
    grads_odd = sections_out(grads_odd)
    grad_joined = jnp.concatenate(
        [
            jnp.concatenate([grads_odd[:, :unit], kv_even], axis=1),
            jnp.concatenate([grads_odd[:, unit : 2 * unit], grads_odd[:, 2 * unit :]], axis=1),
        ],
        axis=2,
    )
    layer_output = in_order(out_pieces, own)

    up_all = (
        ups[0].reshape(rank, 3, n_fs, unit).transpose(2, 0, 1, 3).reshape(n_fs, rank, 3 * unit)
    )
    narrow_one = narrow(normed_one, downs[0])
    grad_up = jnp.einsum("tr,hct->rhc", narrow_one, grad_joined, preferred_element_type=F32)
    grad_up = grad_up.reshape(rank, n_fs, 3, unit).transpose(0, 2, 1, 3).reshape(3 * rank, model)
    grad_narrow = jnp.einsum("hct,hrc->tr", grad_joined, up_all, preferred_element_type=F32).astype(BF16)
    late = jnp.concatenate([dot_tn(grad_narrow, normed_one), grad_up], axis=0)
    grad_joined, late = together(grad_joined, late)
    late = lax.all_to_all(
        late.reshape(n_fs, late.shape[0] // n_fs, model), "fs", split_axis=0, concat_axis=0, tiled=True
    )
    grad_normed_one = jnp.einsum("hct,hcd->td", grad_joined, w_all, preferred_element_type=F32)
    input_grad = grad_middle + rms_back(x_f, scale_one, grad_normed_one * gain_attention)
    input_grad = input_grad.astype(BF16).reshape(sequences, tokens, model)
    input_grad, late = together(input_grad, late)
    in_pieces = own_and_sent(input_grad, own, range(sequences))
    part = jnp.concatenate([jnp.sum(late, axis=0), early], axis=0)
    part = over_sequences(part, sequences, n_sp)
    in_pieces[1], part = together(in_pieces[1], part)
    table = shares_of_all(fold(part, adapter_index, adapters, own), n_fs, in_pieces)
    table = in_order(table, fs)
    input_grad = in_order(in_pieces, own)

    factor = 1.0 / math.sqrt(length)
    outs = []
    late_rows = late.shape[1]
    late = joined_rows(table[:, :, :late_rows]) * factor
    early = joined_rows(table[:, :, late_rows:]) * factor
    for tables, wides in ((late, (3,)), (early, (1, 1, 1))):
        first = 0
        for wide in wides:
            outs.append(jnp.swapaxes(tables[:, first : first + rank], 1, 2))
            first += rank
            outs.append(tables[:, first : first + rank * wide].reshape(adapters, rank, wide * model))
            first += rank * wide
    return (layer_output, input_grad, *outs)


def solution(mesh):
    tokens = P(None, ("fs", "sp"), None)
    in_specs = (tokens, tokens) + (P(),) * 5 + (P(None, "fs"),) * 4 + (P(),) * 8
    out_specs = (tokens, tokens) + (P(),) * 8
    return jax.shard_map(local, mesh=mesh, in_specs=in_specs, out_specs=out_specs, check_vma=False)
```

```python
import functools
import math

import jax
import jax.numpy as jnp
from jax import lax
from jax.experimental import pallas as pl
from jax.experimental.pallas import tpu as pltpu
from jax.sharding import PartitionSpec as P

EPSILON = 1e-06
BIG = 1e30
LANES = 128
PARTS = 3
TILE = 256
VMEM_LIMIT = 64000000
F32 = jnp.float32
BF16 = jnp.bfloat16
NT = (((1,), (1,)), ((), ()))
TN = (((0,), (0,)), ((), ()))


def dot_nn(a, b):
    return jnp.dot(a, b, preferred_element_type=F32)


def dot_nt(a, b):
    return lax.dot_general(a, b, NT, preferred_element_type=F32)


def dot_tn(a, b):
    return lax.dot_general(a, b, TN, preferred_element_type=F32)


def xor_permute(value, axis, mask):
    count = lax.axis_size(axis)
    return lax.ppermute(value, axis, [(a, a ^ mask) for a in range(count)])


def piece_of(stacked, index):
    return lax.dynamic_index_in_dim(stacked, index, 0, keepdims=False)


def project_kernel(tiles, *refs, count, heads, head_dim):
    x_refs, (gain_ref, w_ref, scale_ref, qpad_ref, kpad_ref) = refs[:count], refs[count : count + 5]
    q_ref, k_ref, v_ref, x_ref = refs[-4:]
    if count > 1:
        for n in range(count):

            @pl.when(pl.program_id(0) == n)
            def _():
                x_ref[...] = x_refs[n][...]

        x = x_ref[...].astype(F32)
    else:
        x = x_refs[0][0].astype(F32)
    mean = jnp.mean(x * x, axis=-1, keepdims=True)
    normed = (x * lax.rsqrt(mean + EPSILON) * gain_ref[...]).astype(BF16)
    rows = dot_nn(normed, w_ref[...]) * scale_ref[...]
    width = heads * LANES
    lane = lax.broadcasted_iota(jnp.int32, (1, width), 1) % LANES
    q_ref[...] = (rows[:, :width] + jnp.tile(qpad_ref[...].astype(F32), (1, heads))).astype(BF16)
    k_ref[...] = (rows[:, width : 2 * width] + jnp.tile(kpad_ref[...].astype(F32), (1, heads))).astype(BF16)
    ones = jnp.where((lane >= head_dim) & (lane < head_dim + PARTS), 1.0, 0.0)
    v_ref[...] = (rows[:, 2 * width :] + ones).astype(BF16)


def project(sources, tiles, gain, weight, scale, qpad, kpad, earlier, heads, head_dim, length):
    model = weight.shape[0]
    step = TILE
    count = len(sources)
    steps = tiles.shape[0]
    width = heads * LANES
    out = pl.BlockSpec((step, width), lambda n, t: (t[n], 0))
    pad = pl.BlockSpec((step, LANES), lambda n, t: (t[n], 0))
    fixed = lambda shape: pl.BlockSpec(shape, lambda n, t: (0,) * len(shape))
    if count > 1:
        in_specs = [fixed((step, model))] * count
    else:
        per = sources[0].shape[1] // step
        in_specs = [pl.BlockSpec((1, step, model), lambda n, t: (n // per, n % per, 0))]
    in_specs += [fixed((1, model)), fixed((model, 3 * width)), fixed((1, 3 * width)), pad, pad]
    operands = [*sources, gain, weight, scale, qpad, kpad]
    aliases = {}
    if earlier is not None:
        in_specs += [pl.BlockSpec(memory_space=pl.ANY)] * 3
        aliases = {1 + len(operands) + n: n for n in range(3)}
        operands += list(earlier)
    return pl.pallas_call(
        functools.partial(project_kernel, count=count, heads=heads, head_dim=head_dim),
        out_shape=[jax.ShapeDtypeStruct((length, width), BF16)] * 3,
        grid_spec=pltpu.PrefetchScalarGridSpec(
            num_scalar_prefetch=1,
            grid=(steps,),
            in_specs=in_specs,
            out_specs=[out] * 3,
            scratch_shapes=[pltpu.VMEM((step, model), BF16)],
        ),
        input_output_aliases=aliases,
        compiler_params=pltpu.CompilerParams(vmem_limit_bytes=VMEM_LIMIT),
        cost_estimate=pl.CostEstimate(
            flops=1,
            bytes_accessed=1,
            transcendentals=0,
        ),
        name="project",
    )(tiles, *operands)


def spread(row, index, first):
    high = row.astype(BF16).astype(F32)
    middle = (row - high).astype(BF16).astype(F32)
    last = row - high - middle
    return jnp.where(index == first, high, jnp.where(index == first + 1, middle, last))


def at(block):
    return pl.ds(pl.multiple_of(block * TILE, TILE), TILE)


def attend_kernel(starts, q_ref, k_ref, v_ref, *refs, heads, head_dim, tiles):
    o_ref, aug_ref = refs[-2:]
    step = 2 * pl.program_id(0) + starts[tiles]
    first = starts[step]
    index = lax.broadcasted_iota(jnp.int32, (LANES, 1), 0)
    marks = (index >= head_dim) & (index < head_dim + PARTS)

    def cols(h):
        return pl.ds(h * LANES, LANES)

    turned = [jnp.transpose(q_ref[:, cols(h)].astype(F32)) for h in range(heads)]
    queries = [t.astype(BF16) for t in turned]

    def one(block, carry, masked):
        scores = [dot_nn(k_ref[at(block), cols(h)], queries[h]) for h in range(heads)]
        out = []
        for h, s in enumerate(scores):
            if masked:
                key = lax.broadcasted_iota(jnp.int32, (TILE, TILE), 0)
                query = lax.broadcasted_iota(jnp.int32, (TILE, TILE), 1)
                s = jnp.where(key <= query, s, -BIG)
            peak = jnp.max(s, axis=0, keepdims=True)
            if not masked:
                peak = jnp.maximum(carry[h][0], peak)
            p = jnp.exp(s - peak).astype(BF16)
            total = dot_tn(v_ref[at(block), cols(h)], p)
            if not masked:
                total = carry[h][1] * jnp.exp(carry[h][0] - peak) + total
            out.append((peak, total))
        return tuple(out)

    carry = one(step, None, True)
    carry = lax.fori_loop(first, step, lambda block, c: one(block, c, False), carry)
    for h in range(heads):
        peak, total = carry[h]
        weight = total[head_dim : head_dim + 1]
        o_ref[0, h * head_dim : (h + 1) * head_dim, :] = (total / weight)[:head_dim].astype(BF16)
        lse = -(peak + jnp.log(weight))
        aug_ref[cols(h), :] = jnp.where(marks, spread(lse, index, head_dim), turned[h]).astype(BF16)


def attend(starts, q, k, v, earlier, parity, heads, head_dim):
    length, width = q.shape
    tiles = length // TILE
    steps = tiles // 2
    whole = pl.BlockSpec((length, width), lambda n, st: (0, 0))
    in_specs = [pl.BlockSpec((TILE, width), lambda n, st: (2 * n + st[tiles], 0)), whole, whole]
    operands = [q, k, v]
    aliases = {}
    if earlier is not None:
        in_specs.append(pl.BlockSpec(memory_space=pl.ANY))
        operands.append(earlier)
        aliases = {4: 1}
    return pl.pallas_call(
        functools.partial(attend_kernel, heads=heads, head_dim=head_dim, tiles=tiles),
        out_shape=[
            jax.ShapeDtypeStruct((steps, heads * head_dim, TILE), BF16),
            jax.ShapeDtypeStruct((width, length), BF16),
        ],
        grid_spec=pltpu.PrefetchScalarGridSpec(
            num_scalar_prefetch=1,
            grid=(steps,),
            in_specs=in_specs,
            out_specs=[
                pl.BlockSpec((1, heads * head_dim, TILE), lambda n, st: (n, 0, 0)),
                pl.BlockSpec((width, TILE), lambda n, st: (0, 2 * n + st[tiles])),
            ],
        ),
        input_output_aliases=aliases,
        compiler_params=pltpu.CompilerParams(vmem_limit_bytes=VMEM_LIMIT),
        cost_estimate=pl.CostEstimate(
            flops=1, bytes_accessed=1, transcendentals=0
        ),
        name="attend",
    )(jnp.append(starts, parity), *operands)


def attend_back_kernel(ends, aug_ref, k_ref, v_ref, *refs, heads, head_dim, tiles, second):
    parity = ends[tiles]
    step = 2 * pl.program_id(0) + parity
    unit = heads * head_dim
    if second:
        gaug_ref, dq_in_ref, scale_ref, all_ref, dq_ref, dk_ref, dv_ref = refs
    else:
        *g_refs, kv_ref, gaug_ref, dq_ref, dk_ref, dv_ref = refs
        g_refs, o_refs = g_refs[:2], g_refs[2:]

    def cols(h):
        return pl.ds(h * LANES, LANES)

    def own(h):
        return slice(h * head_dim, (h + 1) * head_dim)

    @pl.when(pl.program_id(0) == 0)
    def _():
        dq_ref[...] = jnp.zeros_like(dq_ref)
        if not second:
            index = lax.broadcasted_iota(jnp.int32, (LANES - head_dim, 1), 0)

            @pl.loop(0, tiles // 2)
            def _(n):
                for part, g_ref, o_ref in zip((parity, 1 - parity), g_refs, o_refs):
                    rows = at(2 * n + part)
                    g = g_ref[n]
                    product = g.astype(F32) * o_ref[n].astype(F32)
                    for h in range(heads):
                        delta = -jnp.sum(product[own(h)], axis=0, keepdims=True)
                        gaug_ref[h * LANES : h * LANES + head_dim, rows] = g[own(h)]
                        gaug_ref[h * LANES + head_dim : (h + 1) * LANES, rows] = jnp.where(
                            index < PARTS, spread(delta, index, 0), 0.0
                        ).astype(BF16)

    dk_ref[...] = jnp.zeros_like(dk_ref)
    dv_ref[...] = jnp.zeros_like(dv_ref)
    keys = [k_ref[:, cols(h)] for h in range(heads)]
    turned = [jnp.transpose(k.astype(F32)).astype(BF16) for k in keys]

    def one(block, masked):
        for h in range(heads):
            q = aug_ref[cols(h), at(block)]
            g = gaug_ref[cols(h), at(block)]
            s = dot_nn(keys[h], q)
            if masked:
                key = lax.broadcasted_iota(jnp.int32, (TILE, TILE), 0)
                query = lax.broadcasted_iota(jnp.int32, (TILE, TILE), 1)
                s = jnp.where(key <= query, s, -BIG)
            p = jnp.exp(s)
            d = dot_nn(v_ref[:, cols(h)], g)
            dv_ref[:, cols(h)] += dot_nt(p.astype(BF16), g)
            ds = (p * d).astype(BF16)
            dk_ref[:, cols(h)] += dot_nt(ds, q)
            dq_ref[cols(h), at(block)] += dot_nn(turned[h], ds)

    one(step, True)

    @pl.loop(step + 1, ends[step])
    def _(block):
        one(block, False)

    pieces = []
    for ref in (dk_ref, dv_ref):
        for h in range(heads):
            pieces.append(jnp.transpose(ref[:, cols(h)])[:head_dim].astype(BF16))
    if not second:
        for n, piece in enumerate(pieces):
            kv_ref[0, n * head_dim : (n + 1) * head_dim, :] = piece
    else:
        for n, piece in enumerate(pieces):
            all_ref[0, 2 * unit + n * head_dim : 2 * unit + (n + 1) * head_dim, :] = piece
        for slot, part in enumerate((1 - parity, parity)):
            rows = at(2 * pl.program_id(0) + part)
            for h in range(heads):
                dq = (dq_in_ref[cols(h), rows] + dq_ref[cols(h), rows]).astype(BF16).astype(F32)
                all_ref[0, slot * unit + h * head_dim : slot * unit + (h + 1) * head_dim, :] = (
                    dq * scale_ref[...]
                )[:head_dim].astype(BF16)


def attend_back(ends, aug, k, v, others, parity, second, heads, head_dim):
    width, length = aug.shape
    tiles = length // TILE
    steps = tiles // 2
    unit = heads * head_dim
    whole = lambda *shape: pl.BlockSpec(shape, lambda n, st: (0,) * len(shape))
    row = pl.BlockSpec((TILE, width), lambda n, st: (2 * n + st[tiles], 0))
    out = lambda rows: pl.BlockSpec((1, rows, TILE), lambda n, st: (n, 0, 0))
    scratch = [pltpu.VMEM((TILE, width), F32)] * 2
    in_specs = [whole(*value.shape) for value in others]
    if not second:
        out_shape = [
            jax.ShapeDtypeStruct((steps, 2 * unit, TILE), BF16),
            jax.ShapeDtypeStruct((width, length), BF16),
            jax.ShapeDtypeStruct((width, length), F32),
        ]
        out_specs = [out(2 * unit), whole(width, length), whole(width, length)]
    else:
        out_shape = jax.ShapeDtypeStruct((steps, 4 * unit, TILE), BF16)
        out_specs = out(4 * unit)
        scratch = [pltpu.VMEM((width, length), F32)] + scratch
    return pl.pallas_call(
        functools.partial(attend_back_kernel, heads=heads, head_dim=head_dim, tiles=tiles, second=second),
        out_shape=out_shape,
        grid_spec=pltpu.PrefetchScalarGridSpec(
            num_scalar_prefetch=1,
            grid=(steps,),
            in_specs=[whole(width, length), row, row, *in_specs],
            out_specs=out_specs,
            scratch_shapes=scratch,
        ),
        compiler_params=pltpu.CompilerParams(vmem_limit_bytes=VMEM_LIMIT),
        cost_estimate=pl.CostEstimate(
            flops=1, bytes_accessed=1, transcendentals=0
        ),
        name="attend_back",
    )(jnp.append(ends, parity), aug, k, v, *others)


def rms_scale(values):
    return lax.rsqrt(jnp.mean(values * values, axis=-1, keepdims=True) + EPSILON)


def rms_back(values, scale_rows, grad_normed):
    cubed = scale_rows * scale_rows * scale_rows
    return scale_rows * grad_normed - values * cubed * jnp.mean(
        grad_normed * values, axis=-1, keepdims=True
    )


def after(value, *others):
    return lax.optimization_barrier((value, others))[0]


def together(*values):
    return lax.optimization_barrier(values)


def own_and_sent(value, own, masks):
    return [
        piece_of(value, own) if m == 0 else xor_permute(piece_of(value, own ^ m), "sp", m) for m in masks
    ]


def in_order(pieces, own):
    stacked = jnp.stack(pieces)
    return jnp.stack([piece_of(stacked, n ^ own) for n in range(len(pieces))], axis=0)


def shares_of_all(table, n_fs, pieces):
    to = lambda value, mask: xor_permute(value, "fs", mask)
    if n_fs != 8 or table.shape[0] % 2:
        return [table] + [to(table, m) for m in range(1, n_fs)]
    half = table.shape[0] // 2
    y, x, core, pieces[2] = together(to(table, 4), to(table, 2), to(table, 1), pieces[2])
    top, bottom, core_y, core_x = to(y[:half], 2), to(x[half:], 4), to(y, 1), to(x, 1)
    top, bottom, core_y, core_x, pieces[3] = together(top, bottom, core_y, core_x, pieces[3])
    both = jnp.concatenate([top, bottom], axis=0)
    return [table, core, x, core_x, y, core_y, both, to(both, 1)]


def over_sequences(part, groups, n_sp):
    mask = groups
    while mask < n_sp:
        part = part + xor_permute(part, "sp", mask)
        mask <<= 1
    return [part] + [xor_permute(part, "sp", m) for m in range(1, groups)]


def fold(pieces, adapter_index, adapters, own):
    by_seq = in_order(pieces, own)
    tables = []
    for a in range(adapters):
        table = jnp.zeros_like(pieces[0])
        for s in range(len(pieces)):
            table = table + jnp.where(adapter_index[s, 0] == a, by_seq[s], 0.0)
        tables.append(table)
    return jnp.stack(tables)


def joined_rows(every):
    n, adapters, rows, model = every.shape
    return jnp.swapaxes(every, 0, 1).reshape(adapters, n * rows, model)


def local(
    layer_input,
    output_grad,
    segment_ids,
    adapter_index,
    gain_attention,
    gain_feedforward,
    query_scale,
    weight_qkv,
    weight_mixer,
    weight_expand,
    weight_contract,
    qkv_down,
    qkv_up,
    mixer_down,
    mixer_up,
    expand_down,
    expand_up,
    contract_down,
    contract_up,
):
    sequences, tokens, model = layer_input.shape
    head_dim = query_scale.shape[0]
    n_fs, n_sp = lax.axis_size("fs"), lax.axis_size("sp")
    adapters, rank = qkv_down.shape[0], qkv_down.shape[2]
    length = segment_ids.shape[1]
    folds = n_sp // sequences
    heads = model // head_dim // n_fs
    unit = heads * head_dim
    width = heads * LANES
    rows = sequences * tokens
    fs = lax.axis_index("fs")
    sp = lax.axis_index("sp")
    own = sp % sequences
    fold_of = sp // sequences

    pick = piece_of(adapter_index, own)[0]
    downs = [piece_of(t, pick) for t in (qkv_down, mixer_down, expand_down, contract_down)]
    ups = [piece_of(t, pick) for t in (qkv_up, mixer_up, expand_up, contract_up)]

    def merged(weight, down, up):
        cols = weight.shape[1]
        own_up = lax.dynamic_slice_in_dim(up, fs * cols, cols, 1)
        return (weight.astype(F32) + dot_nn(down, own_up)).astype(BF16)

    shard = merged(weight_qkv, downs[0], ups[0])
    inverse = pow(3, -1, n_fs)
    received = [
        lax.ppermute(
            shard[:, t * unit : (t + 1) * unit], "fs", [(d, (3 * d + t) % n_fs) for d in range(n_fs)]
        )
        for t in range(3)
    ]
    places = [(3 * ((inverse * (fs - t)) % n_fs) + t) // n_fs for t in range(3)]
    w_parts = []
    for b in range(3):
        part = jnp.zeros_like(received[0])
        for t in range(3):
            part = jnp.where(places[t] == b, received[t], part)
        w_parts.append(part)
    w_own = jnp.concatenate(w_parts, axis=1)
    w_padded = jnp.pad(
        w_own.reshape(model, 3 * heads, head_dim), ((0, 0), (0, 0), (0, LANES - head_dim))
    ).reshape(model, 3 * width)

    segs = piece_of(segment_ids, own)
    scale = query_scale * (1.0 / math.sqrt(head_dim))
    scale_pad = jnp.pad(scale, (0, LANES - head_dim))[None]
    col_scale = jnp.concatenate([jnp.tile(scale_pad, (1, heads)), jnp.ones((1, 2 * width), F32)], axis=1)
    lane = jnp.arange(LANES)[None, :]
    marks = lane >= head_dim + PARTS
    same = lane == segs[:, None] + (head_dim + PARTS)
    qpad = same.astype(BF16)
    kpad = jnp.where(
        marks, jnp.where(same, 0.0, -BIG), jnp.where(lane >= head_dim, 1.0, 0.0)
    ).astype(BF16)

    odd = own % 2
    upper = own // 2
    other = 1 - upper

    def pair(low, high):
        return jnp.where(odd == 1, jnp.concatenate([high, low], 0), jnp.concatenate([low, high], 0))

    def far_pieces(half):
        cut = half.reshape(2, tokens, -1)
        return [xor_permute(piece_of(cut, odd ^ (m & 1)), "sp", m) for m in (2, 3)]

    def near_pieces(half):
        cut = half.reshape(2, tokens, -1)
        return [piece_of(cut, odd), xor_permute(piece_of(cut, 1 - odd), "sp", 1)]

    project_args = (gain_attention[None], w_padded, col_scale, qpad, kpad)
    as_table = lambda *s: jnp.stack(s).astype(jnp.int32)
    if n_fs == 8 and folds == 1 and sequences == 4 and 2 * tokens == TILE:
        pieces = own_and_sent(layer_input, own, range(4))

        def to(value, mask):
            return xor_permute(value, "fs", mask)

        def fill(blocks, place, earlier):
            sources = [block for _, block in blocks]
            tiles = as_table(*[(fs ^ mask) * 2 + place for mask, _ in blocks])
            return project(sources, tiles, *project_args, earlier, heads, head_dim, length)

        first = pair(pieces[0], pieces[1])
        half = TILE // 2
        sent = after(first, *received)
        y1, x1, c1 = to(sent, 4), to(sent, 2), to(sent, 1)
        y1, x1, c1 = together(y1, x1, c1)
        top1, bottom1, cy1, cx1 = to(y1[:half], 2), to(x1[half:], 4), to(y1, 1), to(x1, 1)
        qkv = fill([(0, first), (1, c1), (4, y1), (2, x1)], upper, None)
        *qkv, top1, bottom1, cy1, cx1, p2, p3 = together(*qkv, top1, bottom1, cy1, cx1, pieces[2], pieces[3])
        both1 = jnp.concatenate([top1, bottom1], axis=0)
        second = pair(p2, p3)
        y2, x2, c2, cb1 = to(second, 4), to(second, 2), to(second, 1), to(both1, 1)
        qkv = fill([(5, cy1), (3, cx1)], upper, qkv)
        *qkv, y2, x2, c2, cb1 = together(*qkv, y2, x2, c2, cb1)
        top2, bottom2, cy2, cx2 = to(y2[:half], 2), to(x2[half:], 4), to(y2, 1), to(x2, 1)
        qkv = fill([(6, both1), (7, cb1)], upper, qkv)
        qkv = fill([(0, second), (1, c2)], other, qkv)
        *qkv, top2, bottom2, cy2, cx2 = together(*qkv, top2, bottom2, cy2, cx2)
        both2 = jnp.concatenate([top2, bottom2], axis=0)
        cb2 = to(both2, 1)
        qkv = fill([(4, y2), (2, x2), (5, cy2), (3, cx2)], other, qkv)
        *qkv, cb2 = together(*qkv, cb2)
        qkv = fill([(6, both2), (7, cb2)], other, qkv)
        x_halves = (second, first)
        x_sent, x_here = (p2, p3), (both2,)
    else:
        pieces = own_and_sent(layer_input, own, range(sequences))
        x_own = in_order(pieces, own).reshape(rows, model)
        gathered = lax.all_gather(x_own, ("fs", "sp"), axis=0)
        gathered = gathered.reshape(n_fs, folds, sequences, rows, model)
        gathered = lax.dynamic_index_in_dim(gathered, own, 2, keepdims=False)
        blocks = gathered.reshape(n_fs * folds, rows, model)
        tiles = jnp.arange(length // TILE, dtype=jnp.int32)
        qkv = project([blocks], tiles, *project_args, None, heads, head_dim, length)
        x_halves = (pair(pieces[2], pieces[3]), pair(pieces[0], pieces[1]))
        x_sent, x_here = (x_own,), (blocks,)
    q, k, v = qkv

    three = jnp.stack(
        [
            merged(w, d, u).T
            for w, d, u in zip((weight_mixer, weight_expand, weight_contract), downs[1:], ups[1:])
        ]
    )
    w_mixer, w_expand, w_contract = lax.all_gather(after(three, *x_here), "fs", axis=1, tiled=True)
    g_pieces = own_and_sent(after(output_grad, *x_sent), own, range(sequences))

    firsts, lasts = segs[::TILE], segs[TILE - 1 :: TILE]
    starts = jnp.sum(segs[None, :] < firsts[:, None], axis=1, dtype=jnp.int32) // TILE
    ends = (jnp.sum(segs[None, :] <= lasts[:, None], axis=1, dtype=jnp.int32) + TILE - 1) // TILE

    def sections_out(value):
        if folds > 1:
            cut = value.reshape(n_fs, folds, *value.shape[1:])
            value = lax.dynamic_index_in_dim(cut, fold_of, 1, keepdims=False)
        return lax.all_to_all(value, "fs", split_axis=0, concat_axis=0, tiled=True)

    def halves_in(value):
        value = lax.all_to_all(value, "fs", split_axis=0, concat_axis=0, tiled=True)
        if folds > 1:
            every = lax.all_gather(value, "sp", axis=0)
            every = every.reshape(folds, sequences, *value.shape)
            every = lax.dynamic_index_in_dim(every, own, 1, keepdims=False)
            value = jnp.swapaxes(every, 0, 1).reshape(n_fs * folds, *value.shape[1:])
        return value

    narrow = lambda u, down: dot_nn(u, down).astype(BF16)
    first_of = lambda a, b: lax.dot_general(a, b, (((0,), (1,)), ((), ())), preferred_element_type=F32)

    def feed(x, attended, g):
        x = x.astype(F32)
        middle = x + first_of(attended, w_mixer)
        scale_two = rms_scale(middle)
        normed_two = (middle * scale_two * gain_feedforward).astype(BF16)
        expanded = dot_nt(normed_two, w_expand)
        gate = jax.nn.sigmoid(expanded)
        hidden = (expanded * gate).astype(BF16)
        grad_hidden = dot_nn(g, w_contract)
        grad_expanded = (grad_hidden * gate * (1.0 + expanded * (1.0 - gate))).astype(BF16)
        grad_normed_two = dot_nn(grad_expanded, w_expand)
        grad_middle = g.astype(F32) + rms_back(middle, scale_two, grad_normed_two * gain_feedforward)
        grad_mixer = grad_middle.astype(BF16)
        grad_attended = first_of(w_mixer, grad_mixer).astype(BF16).reshape(n_fs, unit, TILE)
        return grad_attended, (middle, grad_middle), (normed_two, hidden, grad_expanded, grad_mixer)

    o_far, aug = attend(starts, q, k, v, None, other, heads, head_dim)
    a_far = sections_out(o_far)
    o_near, aug = attend(starts, q, k, v, aug, upper, heads, head_dim)
    o_near, a_far, g_pieces = together(o_near, a_far, g_pieces)
    a_near = sections_out(o_near)
    g_far, g_near = pair(g_pieces[2], g_pieces[3]), pair(g_pieces[0], g_pieces[1])
    a_far, a_near = a_far.reshape(model, TILE), a_near.reshape(model, TILE)
    d_far, keep_far, low_far = feed(x_halves[0], a_far, g_far)
    d_far, keep_far, low_far, a_near = together(d_far, keep_far, low_far, a_near)
    d_far = halves_in(d_far)
    d_near, keep_near, low_near = feed(x_halves[1], a_near, g_near)
    d_near, keep_near, low_near, d_far = together(d_near, keep_near, low_near, d_far)
    d_near = halves_in(d_near)

    attended = jnp.concatenate([a_far, a_near], axis=1)
    normed_two, hidden, grad_expanded, grad_mixer, g_own = (
        jnp.concatenate(pair_of, axis=0) for pair_of in zip((*low_far, g_far), (*low_near, g_near))
    )

    def adapter_back(u, grad, down, up):
        grad_up = dot_tn(narrow(u, down), grad)
        grad_narrow = dot_nt(grad, up).astype(BF16)
        return [dot_tn(grad_narrow, u), grad_up]

    early = jnp.concatenate(
        [
            first_of(dot_nt(grad_mixer, ups[1]).astype(BF16), attended),
            dot_tn(dot_tn(attended, downs[1]).astype(BF16), grad_mixer),
            *adapter_back(normed_two, grad_expanded, downs[2], ups[2]),
            *adapter_back(hidden, g_own, downs[3], ups[3]),
        ],
        axis=0,
    )
    contracted = dot_nt(hidden, w_contract)
    out_far = (keep_far[0] + contracted[:TILE]).astype(BF16)
    out_near = (keep_near[0] + contracted[TILE:]).astype(BF16)
    d_near, early, out_far, out_near = together(d_near, early, out_far, out_near)
    w_all = lax.all_gather(after(w_own.T, d_near), "fs", axis=0)
    early = lax.all_to_all(
        early.reshape(n_fs, early.shape[0] // n_fs, model), "fs", split_axis=0, concat_axis=0, tiled=True
    )
    out_pieces = near_pieces(out_near) + far_pieces(out_far)

    kv_far, g_aug, dq = attend_back(
        ends, aug, k, v, (d_far, d_near, o_far, o_near), other, False, heads, head_dim
    )
    kv_far, g_aug, dq, early, out_pieces = together(kv_far, g_aug, dq, early, out_pieces)
    kv_far = sections_out(kv_far)
    early = jnp.sum(early, axis=0)
    rest = attend_back(ends, aug, k, v, (g_aug, dq, scale_pad.T), upper, True, heads, head_dim)
    rest, kv_far, early, w_all = together(rest, kv_far, early, w_all)
    rest = sections_out(rest)
    layer_output = in_order(out_pieces, own)

    joined_far = jnp.concatenate([rest[:, :unit], kv_far], axis=1)
    joined_near = rest[:, unit:]

    def start_of(x):
        x = x.astype(F32)
        scale_one = rms_scale(x)
        return x, scale_one, (x * scale_one * gain_attention).astype(BF16)

    x_far, scale_far, normed_far = start_of(x_halves[0])
    x_near, scale_near, normed_near = start_of(x_halves[1])
    up_all = (
        ups[0].reshape(rank, 3, n_fs, unit).transpose(2, 0, 1, 3).reshape(n_fs, rank, 3 * unit)
    )
    grad_up = jnp.einsum("tr,hct->rhc", narrow(normed_far, downs[0]), joined_far, preferred_element_type=F32)
    grad_up += jnp.einsum("tr,hct->rhc", narrow(normed_near, downs[0]), joined_near, preferred_element_type=F32)
    grad_up = grad_up.reshape(rank, n_fs, 3, unit).transpose(0, 2, 1, 3).reshape(3 * rank, model)
    grad_down = sum(
        dot_tn(jnp.einsum("hct,hrc->tr", joined, up_all, preferred_element_type=F32).astype(BF16), normed)
        for joined, normed in ((joined_far, normed_far), (joined_near, normed_near))
    )
    late = jnp.concatenate([grad_down, grad_up], axis=0)
    joined_far, joined_near, late = together(joined_far, joined_near, late)
    late = lax.all_to_all(
        late.reshape(n_fs, late.shape[0] // n_fs, model), "fs", split_axis=0, concat_axis=0, tiled=True
    )

    def back_to_input(joined, x, scale_one, grad_middle):
        grad_normed_one = jnp.einsum("hct,hcd->td", joined, w_all, preferred_element_type=F32)
        return (grad_middle + rms_back(x, scale_one, grad_normed_one * gain_attention)).astype(BF16)

    grad_far = back_to_input(joined_far, x_far, scale_far, keep_far[1])
    grad_far, late, joined_near = together(grad_far, late, joined_near)
    in_far = far_pieces(grad_far)
    part = jnp.concatenate([jnp.sum(late, axis=0), early], axis=0)
    part = over_sequences(part, sequences, n_sp)
    grad_near = back_to_input(joined_near, x_near, scale_near, keep_near[1])
    grad_near, part = together(grad_near, part)
    in_pieces = near_pieces(grad_near) + in_far
    table = shares_of_all(fold(part, adapter_index, adapters, own), n_fs, in_pieces)
    table = in_order(table, fs)
    input_grad = in_order(in_pieces, own)

    factor = 1.0 / math.sqrt(length)
    outs = []
    late_rows = late.shape[1]
    late = joined_rows(table[:, :, :late_rows]) * factor
    early = joined_rows(table[:, :, late_rows:]) * factor
    for tables, wides in ((late, (3,)), (early, (1, 1, 1))):
        first = 0
        for wide in wides:
            outs.append(jnp.swapaxes(tables[:, first : first + rank], 1, 2))
            first += rank
            outs.append(tables[:, first : first + rank * wide].reshape(adapters, rank, wide * model))
            first += rank * wide
    return (layer_output, input_grad, *outs)


def solution(mesh):
    tokens = P(None, ("fs", "sp"), None)
    in_specs = (tokens, tokens) + (P(),) * 5 + (P(None, "fs"),) * 4 + (P(),) * 8
    out_specs = (tokens, tokens) + (P(),) * 8
    return jax.shard_map(local, mesh=mesh, in_specs=in_specs, out_specs=out_specs, check_vma=False)
```

```python
import functools
import math

import jax
import jax.numpy as jnp
from jax import lax
from jax.experimental import pallas as pl
from jax.experimental.pallas import tpu as pltpu
from jax.sharding import PartitionSpec as P

EPSILON = 1e-06
BIG = 1e30
LANES = 128
PARTS = 3
TILE = 256
VMEM_LIMIT = 64000000
F32 = jnp.float32
BF16 = jnp.bfloat16
NT = (((1,), (1,)), ((), ()))
TN = (((0,), (0,)), ((), ()))


def dot_nn(a, b):
    return jnp.dot(a, b, preferred_element_type=F32)


def dot_nt(a, b):
    return lax.dot_general(a, b, NT, preferred_element_type=F32)


def dot_tn(a, b):
    return lax.dot_general(a, b, TN, preferred_element_type=F32)


def xor_permute(value, axis, mask):
    count = lax.axis_size(axis)
    return lax.ppermute(value, axis, [(a, a ^ mask) for a in range(count)])


def piece_of(stacked, index):
    return lax.dynamic_index_in_dim(stacked, index, 0, keepdims=False)


def project_kernel(tiles, *refs, count, heads, head_dim):
    x_refs, (gain_ref, w_ref, scale_ref, qpad_ref, kpad_ref) = refs[:count], refs[count : count + 5]
    q_ref, k_ref, v_ref, x_ref = refs[-4:]
    if count > 1:
        for n in range(count):

            @pl.when(pl.program_id(0) == n)
            def _():
                x_ref[...] = x_refs[n][...]

        x = x_ref[...].astype(F32)
    else:
        x = x_refs[0][0].astype(F32)
    mean = jnp.mean(x * x, axis=-1, keepdims=True)
    normed = (x * lax.rsqrt(mean + EPSILON) * gain_ref[...]).astype(BF16)
    rows = dot_nn(normed, w_ref[...]) * scale_ref[...]
    width = heads * LANES
    lane = lax.broadcasted_iota(jnp.int32, (1, width), 1) % LANES
    q_ref[...] = (rows[:, :width] + jnp.tile(qpad_ref[...].astype(F32), (1, heads))).astype(BF16)
    k_ref[...] = (rows[:, width : 2 * width] + jnp.tile(kpad_ref[...].astype(F32), (1, heads))).astype(BF16)
    ones = jnp.where((lane >= head_dim) & (lane < head_dim + PARTS), 1.0, 0.0)
    v_ref[...] = (rows[:, 2 * width :] + ones).astype(BF16)


def project(sources, tiles, gain, weight, scale, qpad, kpad, earlier, heads, head_dim, length):
    model = weight.shape[0]
    step = TILE
    count = len(sources)
    steps = tiles.shape[0]
    width = heads * LANES
    out = pl.BlockSpec((step, width), lambda n, t: (t[n], 0))
    pad = pl.BlockSpec((step, LANES), lambda n, t: (t[n], 0))
    fixed = lambda shape: pl.BlockSpec(shape, lambda n, t: (0,) * len(shape))
    if count > 1:
        in_specs = [fixed((step, model))] * count
    else:
        per = sources[0].shape[1] // step
        in_specs = [pl.BlockSpec((1, step, model), lambda n, t: (n // per, n % per, 0))]
    in_specs += [fixed((1, model)), fixed((model, 3 * width)), fixed((1, 3 * width)), pad, pad]
    operands = [*sources, gain, weight, scale, qpad, kpad]
    aliases = {}
    if earlier is not None:
        in_specs += [pl.BlockSpec(memory_space=pl.ANY)] * 3
        aliases = {1 + len(operands) + n: n for n in range(3)}
        operands += list(earlier)
    return pl.pallas_call(
        functools.partial(project_kernel, count=count, heads=heads, head_dim=head_dim),
        out_shape=[jax.ShapeDtypeStruct((length, width), BF16)] * 3,
        grid_spec=pltpu.PrefetchScalarGridSpec(
            num_scalar_prefetch=1,
            grid=(steps,),
            in_specs=in_specs,
            out_specs=[out] * 3,
            scratch_shapes=[pltpu.VMEM((step, model), BF16)],
        ),
        input_output_aliases=aliases,
        compiler_params=pltpu.CompilerParams(vmem_limit_bytes=VMEM_LIMIT),
        cost_estimate=pl.CostEstimate(
            flops=1,
            bytes_accessed=1,
            transcendentals=0,
        ),
        name="project",
    )(tiles, *operands)


def spread(row, index, first):
    high = row.astype(BF16).astype(F32)
    middle = (row - high).astype(BF16).astype(F32)
    last = row - high - middle
    return jnp.where(index == first, high, jnp.where(index == first + 1, middle, last))


def at(block):
    return pl.ds(pl.multiple_of(block * TILE, TILE), TILE)


def attend_kernel(starts, q_ref, k_ref, v_ref, *refs, heads, head_dim, parity):
    o_ref, aug_ref = refs[-2:]
    step = 2 * pl.program_id(0) + parity
    first = starts[step]
    index = lax.broadcasted_iota(jnp.int32, (LANES, 1), 0)
    marks = (index >= head_dim) & (index < head_dim + PARTS)

    def cols(h):
        return pl.ds(h * LANES, LANES)

    turned = [jnp.transpose(q_ref[:, cols(h)].astype(F32)) for h in range(heads)]
    queries = [t.astype(BF16) for t in turned]

    def one(block, carry, masked):
        scores = [dot_nn(k_ref[at(block), cols(h)], queries[h]) for h in range(heads)]
        out = []
        for h, s in enumerate(scores):
            if masked:
                key = lax.broadcasted_iota(jnp.int32, (TILE, TILE), 0)
                query = lax.broadcasted_iota(jnp.int32, (TILE, TILE), 1)
                s = jnp.where(key <= query, s, -BIG)
            peak = jnp.max(s, axis=0, keepdims=True)
            if not masked:
                peak = jnp.maximum(carry[h][0], peak)
            p = jnp.exp(s - peak).astype(BF16)
            total = dot_tn(v_ref[at(block), cols(h)], p)
            if not masked:
                total = carry[h][1] * jnp.exp(carry[h][0] - peak) + total
            out.append((peak, total))
        return tuple(out)

    carry = one(step, None, True)
    carry = lax.fori_loop(first, step, lambda block, c: one(block, c, False), carry)
    for h in range(heads):
        peak, total = carry[h]
        weight = total[head_dim : head_dim + 1]
        o_ref[0, h * head_dim : (h + 1) * head_dim, :] = (total / weight)[:head_dim].astype(BF16)
        lse = -(peak + jnp.log(weight))
        aug_ref[cols(h), :] = jnp.where(marks, spread(lse, index, head_dim), turned[h]).astype(BF16)


def attend(starts, q, k, v, earlier, parity, heads, head_dim):
    length, width = q.shape
    steps = length // TILE // 2
    whole = pl.BlockSpec((length, width), lambda n, st: (0, 0))
    in_specs = [pl.BlockSpec((TILE, width), lambda n, st: (2 * n + parity, 0)), whole, whole]
    operands = [q, k, v]
    aliases = {}
    if earlier is not None:
        in_specs.append(pl.BlockSpec(memory_space=pl.ANY))
        operands.append(earlier)
        aliases = {4: 1}
    return pl.pallas_call(
        functools.partial(attend_kernel, heads=heads, head_dim=head_dim, parity=parity),
        out_shape=[
            jax.ShapeDtypeStruct((steps, heads * head_dim, TILE), BF16),
            jax.ShapeDtypeStruct((width, length), BF16),
        ],
        grid_spec=pltpu.PrefetchScalarGridSpec(
            num_scalar_prefetch=1,
            grid=(steps,),
            in_specs=in_specs,
            out_specs=[
                pl.BlockSpec((1, heads * head_dim, TILE), lambda n, st: (n, 0, 0)),
                pl.BlockSpec((width, TILE), lambda n, st: (0, 2 * n + parity)),
            ],
        ),
        input_output_aliases=aliases,
        compiler_params=pltpu.CompilerParams(vmem_limit_bytes=VMEM_LIMIT),
        cost_estimate=pl.CostEstimate(
            flops=1, bytes_accessed=1, transcendentals=0
        ),
        name="attend",
    )(starts, *operands)


def attend_back_kernel(ends, aug_ref, k_ref, v_ref, *refs, heads, head_dim, parity):
    step = 2 * pl.program_id(0) + parity
    length = aug_ref.shape[1]
    unit = heads * head_dim
    if parity == 0:
        g_ref, even_ref, odd_ref, kv_ref, g_out_ref, dq_ref, dk_ref, dv_ref = refs
        gaug_ref = g_out_ref
    else:
        gaug_ref, dq_in_ref, scale_ref, all_ref, dq_ref, dk_ref, dv_ref = refs

    def cols(h):
        return pl.ds(h * LANES, LANES)

    def own(h):
        return slice(h * head_dim, (h + 1) * head_dim)

    @pl.when(step == parity)
    def _():
        dq_ref[...] = jnp.zeros_like(dq_ref)
        if parity == 0:
            index = lax.broadcasted_iota(jnp.int32, (LANES - head_dim, 1), 0)

            @pl.loop(0, length // TILE // 2)
            def _(n):
                for part, o_ref in enumerate((even_ref, odd_ref)):
                    rows = at(2 * n + part)
                    g = g_ref[n, :, part * TILE : (part + 1) * TILE]
                    product = g.astype(F32) * o_ref[n].astype(F32)
                    for h in range(heads):
                        delta = -jnp.sum(product[own(h)], axis=0, keepdims=True)
                        gaug_ref[h * LANES : h * LANES + head_dim, rows] = g[own(h)]
                        gaug_ref[h * LANES + head_dim : (h + 1) * LANES, rows] = jnp.where(
                            index < PARTS, spread(delta, index, 0), 0.0
                        ).astype(BF16)

    dk_ref[...] = jnp.zeros_like(dk_ref)
    dv_ref[...] = jnp.zeros_like(dv_ref)
    keys = [k_ref[:, cols(h)] for h in range(heads)]
    turned = [jnp.transpose(k.astype(F32)).astype(BF16) for k in keys]

    def one(block, masked):
        for h in range(heads):
            q = aug_ref[cols(h), at(block)]
            g = gaug_ref[cols(h), at(block)]
            s = dot_nn(keys[h], q)
            if masked:
                key = lax.broadcasted_iota(jnp.int32, (TILE, TILE), 0)
                query = lax.broadcasted_iota(jnp.int32, (TILE, TILE), 1)
                s = jnp.where(key <= query, s, -BIG)
            p = jnp.exp(s)
            d = dot_nn(v_ref[:, cols(h)], g)
            dv_ref[:, cols(h)] += dot_nt(p.astype(BF16), g)
            ds = (p * d).astype(BF16)
            dk_ref[:, cols(h)] += dot_nt(ds, q)
            dq_ref[cols(h), at(block)] += dot_nn(turned[h], ds)

    one(step, True)

    @pl.loop(step + 1, ends[step])
    def _(block):
        one(block, False)

    pieces = []
    for ref in (dk_ref, dv_ref):
        for h in range(heads):
            pieces.append(jnp.transpose(ref[:, cols(h)])[:head_dim].astype(BF16))
    if parity == 0:
        for n, piece in enumerate(pieces):
            kv_ref[0, n * head_dim : (n + 1) * head_dim, :] = piece
    else:
        for n, piece in enumerate(pieces):
            all_ref[0, 2 * unit + n * head_dim : 2 * unit + (n + 1) * head_dim, :] = piece
        for part in range(2):
            rows = at(step - 1 + part)
            for h in range(heads):
                dq = (dq_in_ref[cols(h), rows] + dq_ref[cols(h), rows]).astype(BF16).astype(F32)
                all_ref[0, part * unit + h * head_dim : part * unit + (h + 1) * head_dim, :] = (
                    dq * scale_ref[...]
                )[:head_dim].astype(BF16)


def attend_back(ends, aug, k, v, others, parity, heads, head_dim):
    width, length = aug.shape
    steps = length // TILE // 2
    unit = heads * head_dim
    whole = lambda *shape: pl.BlockSpec(shape, lambda n, st: (0,) * len(shape))
    row = pl.BlockSpec((TILE, width), lambda n, st: (2 * n + parity, 0))
    out = lambda rows: pl.BlockSpec((1, rows, TILE), lambda n, st: (n, 0, 0))
    scratch = [pltpu.VMEM((TILE, width), F32)] * 2
    if parity == 0:
        in_specs = [whole(*value.shape) for value in others]
        out_shape = [
            jax.ShapeDtypeStruct((steps, 2 * unit, TILE), BF16),
            jax.ShapeDtypeStruct((width, length), BF16),
            jax.ShapeDtypeStruct((width, length), F32),
        ]
        out_specs = [out(2 * unit), whole(width, length), whole(width, length)]
    else:
        in_specs = [whole(*value.shape) for value in others]
        out_shape = jax.ShapeDtypeStruct((steps, 4 * unit, TILE), BF16)
        out_specs = out(4 * unit)
        scratch = [pltpu.VMEM((width, length), F32)] + scratch
    return pl.pallas_call(
        functools.partial(attend_back_kernel, heads=heads, head_dim=head_dim, parity=parity),
        out_shape=out_shape,
        grid_spec=pltpu.PrefetchScalarGridSpec(
            num_scalar_prefetch=1,
            grid=(steps,),
            in_specs=[whole(width, length), row, row, *in_specs],
            out_specs=out_specs,
            scratch_shapes=scratch,
        ),
        compiler_params=pltpu.CompilerParams(vmem_limit_bytes=VMEM_LIMIT),
        cost_estimate=pl.CostEstimate(
            flops=1, bytes_accessed=1, transcendentals=0
        ),
        name="attend_back",
    )(ends, aug, k, v, *others)


def rms_scale(values):
    return lax.rsqrt(jnp.mean(values * values, axis=-1, keepdims=True) + EPSILON)


def rms_back(values, scale_rows, grad_normed):
    cubed = scale_rows * scale_rows * scale_rows
    return scale_rows * grad_normed - values * cubed * jnp.mean(
        grad_normed * values, axis=-1, keepdims=True
    )


def after(value, *others):
    return lax.optimization_barrier((value, others))[0]


def together(*values):
    return lax.optimization_barrier(values)


def own_and_sent(value, own, masks):
    return [
        piece_of(value, own) if m == 0 else xor_permute(piece_of(value, own ^ m), "sp", m) for m in masks
    ]


def in_order(pieces, own):
    stacked = jnp.stack(pieces)
    return jnp.stack([piece_of(stacked, n ^ own) for n in range(len(pieces))], axis=0)


def shares_of_all(table, n_fs, pieces):
    to = lambda value, mask: xor_permute(value, "fs", mask)
    if n_fs != 8 or table.shape[0] % 2:
        return [table] + [to(table, m) for m in range(1, n_fs)]
    half = table.shape[0] // 2
    y, x, core, pieces[2] = together(to(table, 4), to(table, 2), to(table, 1), pieces[2])
    top, bottom, core_y, core_x = to(y[:half], 2), to(x[half:], 4), to(y, 1), to(x, 1)
    top, bottom, core_y, core_x, pieces[3] = together(top, bottom, core_y, core_x, pieces[3])
    both = jnp.concatenate([top, bottom], axis=0)
    return [table, core, x, core_x, y, core_y, both, to(both, 1)]


def over_sequences(part, groups, n_sp):
    mask = groups
    while mask < n_sp:
        part = part + xor_permute(part, "sp", mask)
        mask <<= 1
    return [part] + [xor_permute(part, "sp", m) for m in range(1, groups)]


def fold(pieces, adapter_index, adapters, own):
    by_seq = in_order(pieces, own)
    tables = []
    for a in range(adapters):
        table = jnp.zeros_like(pieces[0])
        for s in range(len(pieces)):
            table = table + jnp.where(adapter_index[s, 0] == a, by_seq[s], 0.0)
        tables.append(table)
    return jnp.stack(tables)


def joined_rows(every):
    n, adapters, rows, model = every.shape
    return jnp.swapaxes(every, 0, 1).reshape(adapters, n * rows, model)


def local(
    layer_input,
    output_grad,
    segment_ids,
    adapter_index,
    gain_attention,
    gain_feedforward,
    query_scale,
    weight_qkv,
    weight_mixer,
    weight_expand,
    weight_contract,
    qkv_down,
    qkv_up,
    mixer_down,
    mixer_up,
    expand_down,
    expand_up,
    contract_down,
    contract_up,
):
    sequences, tokens, model = layer_input.shape
    head_dim = query_scale.shape[0]
    n_fs, n_sp = lax.axis_size("fs"), lax.axis_size("sp")
    adapters, rank = qkv_down.shape[0], qkv_down.shape[2]
    length = segment_ids.shape[1]
    folds = n_sp // sequences
    heads = model // head_dim // n_fs
    unit = heads * head_dim
    width = heads * LANES
    rows = sequences * tokens
    fs = lax.axis_index("fs")
    sp = lax.axis_index("sp")
    own = sp % sequences
    fold_of = sp // sequences

    pick = piece_of(adapter_index, own)[0]
    downs = [piece_of(t, pick) for t in (qkv_down, mixer_down, expand_down, contract_down)]
    ups = [piece_of(t, pick) for t in (qkv_up, mixer_up, expand_up, contract_up)]

    def merged(weight, down, up):
        cols = weight.shape[1]
        own_up = lax.dynamic_slice_in_dim(up, fs * cols, cols, 1)
        return (weight.astype(F32) + dot_nn(down, own_up)).astype(BF16)

    shard = merged(weight_qkv, downs[0], ups[0])
    inverse = pow(3, -1, n_fs)
    received = [
        lax.ppermute(
            shard[:, t * unit : (t + 1) * unit], "fs", [(d, (3 * d + t) % n_fs) for d in range(n_fs)]
        )
        for t in range(3)
    ]
    places = [(3 * ((inverse * (fs - t)) % n_fs) + t) // n_fs for t in range(3)]
    w_parts = []
    for b in range(3):
        part = jnp.zeros_like(received[0])
        for t in range(3):
            part = jnp.where(places[t] == b, received[t], part)
        w_parts.append(part)
    w_own = jnp.concatenate(w_parts, axis=1)
    w_padded = jnp.pad(
        w_own.reshape(model, 3 * heads, head_dim), ((0, 0), (0, 0), (0, LANES - head_dim))
    ).reshape(model, 3 * width)

    segs = piece_of(segment_ids, own)
    scale = query_scale * (1.0 / math.sqrt(head_dim))
    scale_pad = jnp.pad(scale, (0, LANES - head_dim))[None]
    col_scale = jnp.concatenate([jnp.tile(scale_pad, (1, heads)), jnp.ones((1, 2 * width), F32)], axis=1)
    lane = jnp.arange(LANES)[None, :]
    marks = lane >= head_dim + PARTS
    same = lane == segs[:, None] + (head_dim + PARTS)
    qpad = same.astype(BF16)
    kpad = jnp.where(
        marks, jnp.where(same, 0.0, -BIG), jnp.where(lane >= head_dim, 1.0, 0.0)
    ).astype(BF16)

    project_args = (gain_attention[None], w_padded, col_scale, qpad, kpad)
    as_table = lambda *s: jnp.stack(s).astype(jnp.int32)
    if n_fs == 8 and folds == 1 and sequences == 4 and 2 * tokens == TILE:
        pieces = own_and_sent(layer_input, own, (0, 1))
        pieces += own_and_sent(layer_input, own, (2, 3))
        odd = own % 2 == 1
        upper = own // 2

        def pair(low, high):
            return jnp.where(odd, jnp.concatenate([high, low], 0), jnp.concatenate([low, high], 0))

        def to(value, mask):
            return xor_permute(value, "fs", mask)

        def fill(blocks, place, earlier):
            sources = [block for _, block in blocks]
            tiles = as_table(*[(fs ^ mask) * 2 + place for mask, _ in blocks])
            return project(sources, tiles, *project_args, earlier, heads, head_dim, length)

        other = 1 - upper
        first = pair(pieces[0], pieces[1])
        half = TILE // 2
        sent = after(first, *received)
        y1, x1, c1 = to(sent, 4), to(sent, 2), to(sent, 1)
        y1, x1, c1 = together(y1, x1, c1)
        top1, bottom1, cy1, cx1 = to(y1[:half], 2), to(x1[half:], 4), to(y1, 1), to(x1, 1)
        qkv = fill([(0, first), (1, c1), (4, y1), (2, x1)], upper, None)
        *qkv, top1, bottom1, cy1, cx1, p2, p3 = together(*qkv, top1, bottom1, cy1, cx1, pieces[2], pieces[3])
        both1 = jnp.concatenate([top1, bottom1], axis=0)
        second = pair(p2, p3)
        y2, x2, c2, cb1 = to(second, 4), to(second, 2), to(second, 1), to(both1, 1)
        qkv = fill([(5, cy1), (3, cx1)], upper, qkv)
        *qkv, y2, x2, c2, cb1 = together(*qkv, y2, x2, c2, cb1)
        top2, bottom2, cy2, cx2 = to(y2[:half], 2), to(x2[half:], 4), to(y2, 1), to(x2, 1)
        qkv = fill([(6, both1), (7, cb1)], upper, qkv)
        qkv = fill([(0, second), (1, c2)], other, qkv)
        *qkv, top2, bottom2, cy2, cx2 = together(*qkv, top2, bottom2, cy2, cx2)
        both2 = jnp.concatenate([top2, bottom2], axis=0)
        cb2 = to(both2, 1)
        qkv = fill([(4, y2), (2, x2), (5, cy2), (3, cx2)], other, qkv)
        *qkv, cb2 = together(*qkv, cb2)
        qkv = fill([(6, both2), (7, cb2)], other, qkv)
        x_own = jnp.where(
            upper == 0, jnp.concatenate([first, second], 0), jnp.concatenate([second, first], 0)
        )
        x_sent, x_here = (p2, p3), (both2,)
    else:
        pieces = own_and_sent(layer_input, own, range(sequences))
        x_own = in_order(pieces, own).reshape(rows, model)
        gathered = lax.all_gather(x_own, ("fs", "sp"), axis=0)
        gathered = gathered.reshape(n_fs, folds, sequences, rows, model)
        gathered = lax.dynamic_index_in_dim(gathered, own, 2, keepdims=False)
        blocks = gathered.reshape(n_fs * folds, rows, model)
        tiles = jnp.arange(length // TILE, dtype=jnp.int32)
        qkv = project([blocks], tiles, *project_args, None, heads, head_dim, length)
        x_sent, x_here = (x_own,), (blocks,)
    q, k, v = qkv

    three = jnp.stack(
        [
            merged(w, d, u).T
            for w, d, u in zip((weight_mixer, weight_expand, weight_contract), downs[1:], ups[1:])
        ]
    )
    w_mixer, w_expand, w_contract = lax.all_gather(after(three, *x_here), "fs", axis=1, tiled=True)
    g_pieces = own_and_sent(after(output_grad, *x_sent), own, range(sequences))

    firsts, lasts = segs[::TILE], segs[TILE - 1 :: TILE]
    starts = jnp.sum(segs[None, :] < firsts[:, None], axis=1, dtype=jnp.int32) // TILE
    ends = (jnp.sum(segs[None, :] <= lasts[:, None], axis=1, dtype=jnp.int32) + TILE - 1) // TILE

    def sections_out(value):
        if folds > 1:
            cut = value.reshape(n_fs, folds, *value.shape[1:])
            value = lax.dynamic_index_in_dim(cut, fold_of, 1, keepdims=False)
        return lax.all_to_all(value, "fs", split_axis=0, concat_axis=0, tiled=True)

    o_even, aug = attend(starts, q, k, v, None, 0, heads, head_dim)
    a_even = sections_out(o_even)
    o_odd, aug = attend(starts, q, k, v, aug, 1, heads, head_dim)
    o_odd, a_even, g_pieces = together(o_odd, a_even, g_pieces)
    a_odd = sections_out(o_odd)
    attended = jnp.concatenate([a_even, a_odd], axis=2).reshape(model, rows)
    g_own = in_order(g_pieces, own).reshape(rows, model)

    x_f = x_own.astype(F32)
    scale_one = rms_scale(x_f)
    normed_one = (x_f * scale_one * gain_attention).astype(BF16)
    narrow = lambda u, down: dot_nn(u, down).astype(BF16)
    mixer = lax.dot_general(attended, w_mixer, (((0,), (1,)), ((), ())), preferred_element_type=F32)
    middle = x_f + mixer
    scale_two = rms_scale(middle)
    normed_two = (middle * scale_two * gain_feedforward).astype(BF16)
    expanded = dot_nt(normed_two, w_expand)
    gate = jax.nn.sigmoid(expanded)
    hidden = (expanded * gate).astype(BF16)
    contracted = dot_nt(hidden, w_contract)
    layer_output = (middle + contracted).astype(BF16).reshape(sequences, tokens, model)

    def adapter_back(u, grad, down, up):
        grad_up = dot_tn(narrow(u, down), grad)
        grad_narrow = dot_nt(grad, up).astype(BF16)
        return [dot_tn(grad_narrow, u), grad_up]

    grad_hidden = dot_nn(g_own, w_contract)
    grad_expanded = (grad_hidden * gate * (1.0 + expanded * (1.0 - gate))).astype(BF16)
    grad_normed_two = dot_nn(grad_expanded, w_expand)
    grad_middle = g_own.astype(F32) + rms_back(middle, scale_two, grad_normed_two * gain_feedforward)
    grad_mixer = grad_middle.astype(BF16)
    grad_attended = lax.dot_general(w_mixer, grad_mixer, (((0,), (1,)), ((), ())), preferred_element_type=F32)
    grad_heads = lax.all_to_all(
        grad_attended.astype(BF16).reshape(n_fs, unit, rows), "fs", split_axis=0, concat_axis=0, tiled=True
    )
    if folds > 1:
        every = lax.all_gather(grad_heads, "sp", axis=0)
        every = every.reshape(folds, sequences, n_fs, unit, rows)
        every = lax.dynamic_index_in_dim(every, own, 1, keepdims=False)
        grad_heads = jnp.swapaxes(every, 0, 1).reshape(n_fs * folds, unit, rows)

    narrow_mixer = dot_tn(attended, downs[1]).astype(BF16)
    early = jnp.concatenate(
        [
            lax.dot_general(
                dot_nt(grad_mixer, ups[1]).astype(BF16), attended, (((0,), (1,)), ((), ())), preferred_element_type=F32
            ),
            dot_tn(narrow_mixer, grad_mixer),
            *adapter_back(normed_two, grad_expanded, downs[2], ups[2]),
            *adapter_back(hidden, g_own, downs[3], ups[3]),
        ],
        axis=0,
    )
    grad_heads, early, layer_output = together(grad_heads, early, layer_output)
    w_all = lax.all_gather(
        after(w_own.T.reshape(3, unit, model), grad_heads), "fs", axis=1, tiled=True
    ).reshape(3 * model, model)
    early = lax.all_to_all(
        early.reshape(n_fs, early.shape[0] // n_fs, model), "fs", split_axis=0, concat_axis=0, tiled=True
    )

    kv_even, g_aug, dq = attend_back(ends, aug, k, v, (grad_heads, o_even, o_odd), 0, heads, head_dim)
    kv_even, g_aug, dq, early = together(kv_even, g_aug, dq, early)
    kv_even = sections_out(kv_even)
    early = jnp.sum(early, axis=0)
    grads_odd = attend_back(ends, aug, k, v, (g_aug, dq, scale_pad.T), 1, heads, head_dim)
    grads_odd, kv_even, early, w_all = together(grads_odd, kv_even, early, w_all)
    out_pieces = own_and_sent(after(layer_output, grads_odd), own, range(sequences))
    grads_odd = sections_out(grads_odd)
    grads_odd, out_pieces = together(grads_odd, out_pieces)
    layer_output = in_order(out_pieces, own)
    grad_joined = jnp.concatenate(
        [
            jnp.concatenate([a, b], axis=2).reshape(model, rows)
            for a, b in (
                (grads_odd[:, :unit], grads_odd[:, unit : 2 * unit]),
                (kv_even[:, :unit], grads_odd[:, 2 * unit : 3 * unit]),
                (kv_even[:, unit:], grads_odd[:, 3 * unit :]),
            )
        ],
        axis=0,
    )
    narrow_one = narrow(normed_one, downs[0])
    grad_up = lax.dot_general(narrow_one, grad_joined, (((0,), (1,)), ((), ())), preferred_element_type=F32)
    grad_narrow = lax.dot_general(grad_joined, ups[0], (((0,), (1,)), ((), ())), preferred_element_type=F32)
    late = jnp.concatenate([dot_tn(grad_narrow.astype(BF16), normed_one), grad_up.reshape(3 * rank, model)], axis=0)
    grad_joined, late = together(grad_joined, late)
    late = lax.all_to_all(
        late.reshape(n_fs, late.shape[0] // n_fs, model), "fs", split_axis=0, concat_axis=0, tiled=True
    )
    grad_normed_one = dot_tn(grad_joined, w_all)
    input_grad = grad_middle + rms_back(x_f, scale_one, grad_normed_one * gain_attention)
    input_grad = input_grad.astype(BF16).reshape(sequences, tokens, model)
    in_pieces = own_and_sent(input_grad, own, range(sequences))
    part = jnp.concatenate([jnp.sum(late, axis=0), early], axis=0)
    part = over_sequences(part, sequences, n_sp)
    in_pieces[1], part = together(in_pieces[1], part)
    table = shares_of_all(fold(part, adapter_index, adapters, own), n_fs, in_pieces)
    table = in_order(table, fs)
    input_grad = in_order(in_pieces, own)

    factor = 1.0 / math.sqrt(length)
    outs = []
    late_rows = late.shape[1]
    late = joined_rows(table[:, :, :late_rows]) * factor
    early = joined_rows(table[:, :, late_rows:]) * factor
    for tables, wides in ((late, (3,)), (early, (1, 1, 1))):
        first = 0
        for wide in wides:
            outs.append(jnp.swapaxes(tables[:, first : first + rank], 1, 2))
            first += rank
            outs.append(tables[:, first : first + rank * wide].reshape(adapters, rank, wide * model))
            first += rank * wide
    return (layer_output, input_grad, *outs)


def solution(mesh):
    tokens = P(None, ("fs", "sp"), None)
    in_specs = (tokens, tokens) + (P(),) * 5 + (P(None, "fs"),) * 4 + (P(),) * 8
    out_specs = (tokens, tokens) + (P(),) * 8
    return jax.shard_map(local, mesh=mesh, in_specs=in_specs, out_specs=out_specs, check_vma=False)
```

```python
import functools
import math

import jax
import jax.numpy as jnp
from jax import lax
from jax.experimental import pallas as pl
from jax.experimental.pallas import tpu as pltpu
from jax.sharding import PartitionSpec as P

EPSILON = 1e-06
BIG = 1e30
LANES = 128
PARTS = 3
TILE = 256
VMEM_LIMIT = 64000000
F32 = jnp.float32
BF16 = jnp.bfloat16
NT = (((1,), (1,)), ((), ()))
TN = (((0,), (0,)), ((), ()))


def dot_nn(a, b):
    return jnp.dot(a, b, preferred_element_type=F32)


def dot_nt(a, b):
    return lax.dot_general(a, b, NT, preferred_element_type=F32)


def dot_tn(a, b):
    return lax.dot_general(a, b, TN, preferred_element_type=F32)


def xor_permute(value, axis, mask):
    count = lax.axis_size(axis)
    return lax.ppermute(value, axis, [(a, a ^ mask) for a in range(count)])


def piece_of(stacked, index):
    return lax.dynamic_index_in_dim(stacked, index, 0, keepdims=False)


def project_kernel(tiles, *refs, count, heads, head_dim):
    x_refs, (gain_ref, w_ref, scale_ref, qpad_ref, kpad_ref) = refs[:count], refs[count : count + 5]
    q_ref, k_ref, v_ref, x_ref = refs[-4:]
    if count > 1:
        for n in range(count):

            @pl.when(pl.program_id(0) == n)
            def _():
                x_ref[...] = x_refs[n][...]

        x = x_ref[...].astype(F32)
    else:
        x = x_refs[0][0].astype(F32)
    mean = jnp.mean(x * x, axis=-1, keepdims=True)
    normed = (x * lax.rsqrt(mean + EPSILON) * gain_ref[...]).astype(BF16)
    rows = dot_nn(normed, w_ref[...]) * scale_ref[...]
    width = heads * LANES
    lane = lax.broadcasted_iota(jnp.int32, (1, width), 1) % LANES
    q_ref[...] = (rows[:, :width] + jnp.tile(qpad_ref[...].astype(F32), (1, heads))).astype(BF16)
    k_ref[...] = (rows[:, width : 2 * width] + jnp.tile(kpad_ref[...].astype(F32), (1, heads))).astype(BF16)
    ones = jnp.where((lane >= head_dim) & (lane < head_dim + PARTS), 1.0, 0.0)
    v_ref[...] = (rows[:, 2 * width :] + ones).astype(BF16)


def project(sources, tiles, gain, weight, scale, qpad, kpad, earlier, heads, head_dim, length):
    model = weight.shape[0]
    step = TILE
    count = len(sources)
    steps = tiles.shape[0]
    width = heads * LANES
    out = pl.BlockSpec((step, width), lambda n, t: (t[n], 0))
    pad = pl.BlockSpec((step, LANES), lambda n, t: (t[n], 0))
    fixed = lambda shape: pl.BlockSpec(shape, lambda n, t: (0,) * len(shape))
    if count > 1:
        in_specs = [fixed((step, model))] * count
    else:
        per = sources[0].shape[1] // step
        in_specs = [pl.BlockSpec((1, step, model), lambda n, t: (n // per, n % per, 0))]
    in_specs += [fixed((1, model)), fixed((model, 3 * width)), fixed((1, 3 * width)), pad, pad]
    operands = [*sources, gain, weight, scale, qpad, kpad]
    aliases = {}
    if earlier is not None:
        in_specs += [pl.BlockSpec(memory_space=pl.ANY)] * 3
        aliases = {1 + len(operands) + n: n for n in range(3)}
        operands += list(earlier)
    return pl.pallas_call(
        functools.partial(project_kernel, count=count, heads=heads, head_dim=head_dim),
        out_shape=[jax.ShapeDtypeStruct((length, width), BF16)] * 3,
        grid_spec=pltpu.PrefetchScalarGridSpec(
            num_scalar_prefetch=1,
            grid=(steps,),
            in_specs=in_specs,
            out_specs=[out] * 3,
            scratch_shapes=[pltpu.VMEM((step, model), BF16)],
        ),
        input_output_aliases=aliases,
        compiler_params=pltpu.CompilerParams(vmem_limit_bytes=VMEM_LIMIT),
        cost_estimate=pl.CostEstimate(
            flops=1,
            bytes_accessed=1,
            transcendentals=0,
        ),
        name="project",
    )(tiles, *operands)


def spread(row, index, first):
    high = row.astype(BF16).astype(F32)
    middle = (row - high).astype(BF16).astype(F32)
    last = row - high - middle
    return jnp.where(index == first, high, jnp.where(index == first + 1, middle, last))


def at(block):
    return pl.ds(pl.multiple_of(block * TILE, TILE), TILE)


def attend_kernel(starts, q_ref, k_ref, v_ref, *refs, heads, head_dim, parity):
    o_ref, aug_ref = refs[-2:]
    step = 2 * pl.program_id(0) + parity
    first = starts[step]
    index = lax.broadcasted_iota(jnp.int32, (LANES, 1), 0)
    marks = (index >= head_dim) & (index < head_dim + PARTS)

    def cols(h):
        return pl.ds(h * LANES, LANES)

    turned = [jnp.transpose(q_ref[:, cols(h)].astype(F32)) for h in range(heads)]
    queries = [t.astype(BF16) for t in turned]

    def one(block, carry, masked):
        scores = [dot_nn(k_ref[at(block), cols(h)], queries[h]) for h in range(heads)]
        out = []
        for h, s in enumerate(scores):
            if masked:
                key = lax.broadcasted_iota(jnp.int32, (TILE, TILE), 0)
                query = lax.broadcasted_iota(jnp.int32, (TILE, TILE), 1)
                s = jnp.where(key <= query, s, -BIG)
            peak = jnp.max(s, axis=0, keepdims=True)
            if not masked:
                peak = jnp.maximum(carry[h][0], peak)
            p = jnp.exp(s - peak).astype(BF16)
            total = dot_tn(v_ref[at(block), cols(h)], p)
            if not masked:
                total = carry[h][1] * jnp.exp(carry[h][0] - peak) + total
            out.append((peak, total))
        return tuple(out)

    carry = one(step, None, True)
    carry = lax.fori_loop(first, step, lambda block, c: one(block, c, False), carry)
    for h in range(heads):
        peak, total = carry[h]
        weight = total[head_dim : head_dim + 1]
        o_ref[0, h * head_dim : (h + 1) * head_dim, :] = (total / weight)[:head_dim].astype(BF16)
        lse = -(peak + jnp.log(weight))
        aug_ref[cols(h), :] = jnp.where(marks, spread(lse, index, head_dim), turned[h]).astype(BF16)


def attend(starts, q, k, v, earlier, parity, heads, head_dim):
    length, width = q.shape
    steps = length // TILE // 2
    whole = pl.BlockSpec((length, width), lambda n, st: (0, 0))
    in_specs = [pl.BlockSpec((TILE, width), lambda n, st: (2 * n + parity, 0)), whole, whole]
    operands = [q, k, v]
    aliases = {}
    if earlier is not None:
        in_specs.append(pl.BlockSpec(memory_space=pl.ANY))
        operands.append(earlier)
        aliases = {4: 1}
    return pl.pallas_call(
        functools.partial(attend_kernel, heads=heads, head_dim=head_dim, parity=parity),
        out_shape=[
            jax.ShapeDtypeStruct((steps, heads * head_dim, TILE), BF16),
            jax.ShapeDtypeStruct((width, length), BF16),
        ],
        grid_spec=pltpu.PrefetchScalarGridSpec(
            num_scalar_prefetch=1,
            grid=(steps,),
            in_specs=in_specs,
            out_specs=[
                pl.BlockSpec((1, heads * head_dim, TILE), lambda n, st: (n, 0, 0)),
                pl.BlockSpec((width, TILE), lambda n, st: (0, 2 * n + parity)),
            ],
        ),
        input_output_aliases=aliases,
        compiler_params=pltpu.CompilerParams(vmem_limit_bytes=VMEM_LIMIT),
        cost_estimate=pl.CostEstimate(
            flops=1, bytes_accessed=1, transcendentals=0
        ),
        name="attend",
    )(starts, *operands)


def attend_back_kernel(ends, aug_ref, k_ref, v_ref, *refs, heads, head_dim, parity):
    step = 2 * pl.program_id(0) + parity
    length = aug_ref.shape[1]
    unit = heads * head_dim
    if parity == 0:
        g_ref, even_ref, odd_ref, kv_ref, g_out_ref, dq_ref, dk_ref, dv_ref = refs
        gaug_ref = g_out_ref
    else:
        gaug_ref, dq_in_ref, scale_ref, all_ref, dq_ref, dk_ref, dv_ref = refs

    def cols(h):
        return pl.ds(h * LANES, LANES)

    def own(h):
        return slice(h * head_dim, (h + 1) * head_dim)

    @pl.when(step == parity)
    def _():
        dq_ref[...] = jnp.zeros_like(dq_ref)
        if parity == 0:
            index = lax.broadcasted_iota(jnp.int32, (LANES - head_dim, 1), 0)

            @pl.loop(0, length // TILE // 2)
            def _(n):
                for part, o_ref in enumerate((even_ref, odd_ref)):
                    rows = at(2 * n + part)
                    g = g_ref[n, :, part * TILE : (part + 1) * TILE]
                    product = g.astype(F32) * o_ref[n].astype(F32)
                    for h in range(heads):
                        delta = -jnp.sum(product[own(h)], axis=0, keepdims=True)
                        gaug_ref[h * LANES : h * LANES + head_dim, rows] = g[own(h)]
                        gaug_ref[h * LANES + head_dim : (h + 1) * LANES, rows] = jnp.where(
                            index < PARTS, spread(delta, index, 0), 0.0
                        ).astype(BF16)

    dk_ref[...] = jnp.zeros_like(dk_ref)
    dv_ref[...] = jnp.zeros_like(dv_ref)
    keys = [k_ref[:, cols(h)] for h in range(heads)]
    turned = [jnp.transpose(k.astype(F32)).astype(BF16) for k in keys]

    def one(block, masked):
        for h in range(heads):
            q = aug_ref[cols(h), at(block)]
            g = gaug_ref[cols(h), at(block)]
            s = dot_nn(keys[h], q)
            if masked:
                key = lax.broadcasted_iota(jnp.int32, (TILE, TILE), 0)
                query = lax.broadcasted_iota(jnp.int32, (TILE, TILE), 1)
                s = jnp.where(key <= query, s, -BIG)
            p = jnp.exp(s)
            d = dot_nn(v_ref[:, cols(h)], g)
            dv_ref[:, cols(h)] += dot_nt(p.astype(BF16), g)
            ds = (p * d).astype(BF16)
            dk_ref[:, cols(h)] += dot_nt(ds, q)
            dq_ref[cols(h), at(block)] += dot_nn(turned[h], ds)

    one(step, True)

    @pl.loop(step + 1, ends[step])
    def _(block):
        one(block, False)

    pieces = []
    for ref in (dk_ref, dv_ref):
        for h in range(heads):
            pieces.append(jnp.transpose(ref[:, cols(h)])[:head_dim].astype(BF16))
    if parity == 0:
        for n, piece in enumerate(pieces):
            kv_ref[0, n * head_dim : (n + 1) * head_dim, :] = piece
    else:
        for n, piece in enumerate(pieces):
            all_ref[0, 2 * unit + n * head_dim : 2 * unit + (n + 1) * head_dim, :] = piece
        for part in range(2):
            rows = at(step - 1 + part)
            for h in range(heads):
                dq = (dq_in_ref[cols(h), rows] + dq_ref[cols(h), rows]).astype(BF16).astype(F32)
                all_ref[0, part * unit + h * head_dim : part * unit + (h + 1) * head_dim, :] = (
                    dq * scale_ref[...]
                )[:head_dim].astype(BF16)


def attend_back(ends, aug, k, v, others, parity, heads, head_dim):
    width, length = aug.shape
    steps = length // TILE // 2
    unit = heads * head_dim
    whole = lambda *shape: pl.BlockSpec(shape, lambda n, st: (0,) * len(shape))
    row = pl.BlockSpec((TILE, width), lambda n, st: (2 * n + parity, 0))
    out = lambda rows: pl.BlockSpec((1, rows, TILE), lambda n, st: (n, 0, 0))
    scratch = [pltpu.VMEM((TILE, width), F32)] * 2
    if parity == 0:
        in_specs = [whole(*value.shape) for value in others]
        out_shape = [
            jax.ShapeDtypeStruct((steps, 2 * unit, TILE), BF16),
            jax.ShapeDtypeStruct((width, length), BF16),
            jax.ShapeDtypeStruct((width, length), F32),
        ]
        out_specs = [out(2 * unit), whole(width, length), whole(width, length)]
    else:
        in_specs = [whole(*value.shape) for value in others]
        out_shape = jax.ShapeDtypeStruct((steps, 4 * unit, TILE), BF16)
        out_specs = out(4 * unit)
        scratch = [pltpu.VMEM((width, length), F32)] + scratch
    return pl.pallas_call(
        functools.partial(attend_back_kernel, heads=heads, head_dim=head_dim, parity=parity),
        out_shape=out_shape,
        grid_spec=pltpu.PrefetchScalarGridSpec(
            num_scalar_prefetch=1,
            grid=(steps,),
            in_specs=[whole(width, length), row, row, *in_specs],
            out_specs=out_specs,
            scratch_shapes=scratch,
        ),
        compiler_params=pltpu.CompilerParams(vmem_limit_bytes=VMEM_LIMIT),
        cost_estimate=pl.CostEstimate(
            flops=1, bytes_accessed=1, transcendentals=0
        ),
        name="attend_back",
    )(ends, aug, k, v, *others)


def rms_scale(values):
    return lax.rsqrt(jnp.mean(values * values, axis=-1, keepdims=True) + EPSILON)


def rms_back(values, scale_rows, grad_normed):
    cubed = scale_rows * scale_rows * scale_rows
    return scale_rows * grad_normed - values * cubed * jnp.mean(
        grad_normed * values, axis=-1, keepdims=True
    )


def after(value, *others):
    return lax.optimization_barrier((value, others))[0]


def together(*values):
    return lax.optimization_barrier(values)


def own_and_sent(value, own, masks):
    return [
        piece_of(value, own) if m == 0 else xor_permute(piece_of(value, own ^ m), "sp", m) for m in masks
    ]


def in_order(pieces, own):
    stacked = jnp.stack(pieces)
    return jnp.stack([piece_of(stacked, n ^ own) for n in range(len(pieces))], axis=0)


def shares_of_all(table, n_fs):
    to = lambda value, mask: xor_permute(value, "fs", mask)
    if n_fs != 8 or table.shape[0] % 2:
        return [table] + [to(table, m) for m in range(1, n_fs)]
    half = table.shape[0] // 2
    y, x, core = to(table, 4), to(table, 2), to(table, 1)
    top, bottom, core_y, core_x = to(y[:half], 2), to(x[half:], 4), to(y, 1), to(x, 1)
    both = jnp.concatenate([top, bottom], axis=0)
    return [table, core, x, core_x, y, core_y, both, to(both, 1)]


def over_sequences(part, groups, n_sp):
    mask = groups
    while mask < n_sp:
        part = part + xor_permute(part, "sp", mask)
        mask <<= 1
    return [part] + [xor_permute(part, "sp", m) for m in range(1, groups)]


def fold(pieces, adapter_index, adapters, own):
    by_seq = in_order(pieces, own)
    tables = []
    for a in range(adapters):
        table = jnp.zeros_like(pieces[0])
        for s in range(len(pieces)):
            table = table + jnp.where(adapter_index[s, 0] == a, by_seq[s], 0.0)
        tables.append(table)
    return jnp.stack(tables)


def joined_rows(every):
    n, adapters, rows, model = every.shape
    return jnp.swapaxes(every, 0, 1).reshape(adapters, n * rows, model)


def local(
    layer_input,
    output_grad,
    segment_ids,
    adapter_index,
    gain_attention,
    gain_feedforward,
    query_scale,
    weight_qkv,
    weight_mixer,
    weight_expand,
    weight_contract,
    qkv_down,
    qkv_up,
    mixer_down,
    mixer_up,
    expand_down,
    expand_up,
    contract_down,
    contract_up,
):
    sequences, tokens, model = layer_input.shape
    head_dim = query_scale.shape[0]
    n_fs, n_sp = lax.axis_size("fs"), lax.axis_size("sp")
    adapters, rank = qkv_down.shape[0], qkv_down.shape[2]
    length = segment_ids.shape[1]
    folds = n_sp // sequences
    heads = model // head_dim // n_fs
    unit = heads * head_dim
    width = heads * LANES
    rows = sequences * tokens
    fs = lax.axis_index("fs")
    sp = lax.axis_index("sp")
    own = sp % sequences
    fold_of = sp // sequences

    pick = piece_of(adapter_index, own)[0]
    downs = [piece_of(t, pick) for t in (qkv_down, mixer_down, expand_down, contract_down)]
    ups = [piece_of(t, pick) for t in (qkv_up, mixer_up, expand_up, contract_up)]

    def merged(weight, down, up):
        cols = weight.shape[1]
        own_up = lax.dynamic_slice_in_dim(up, fs * cols, cols, 1)
        return (weight.astype(F32) + dot_nn(down, own_up)).astype(BF16)

    shard = merged(weight_qkv, downs[0], ups[0])
    inverse = pow(3, -1, n_fs)
    received = [
        lax.ppermute(
            shard[:, t * unit : (t + 1) * unit], "fs", [(d, (3 * d + t) % n_fs) for d in range(n_fs)]
        )
        for t in range(3)
    ]
    places = [(3 * ((inverse * (fs - t)) % n_fs) + t) // n_fs for t in range(3)]
    w_parts = []
    for b in range(3):
        part = jnp.zeros_like(received[0])
        for t in range(3):
            part = jnp.where(places[t] == b, received[t], part)
        w_parts.append(part)
    w_own = jnp.concatenate(w_parts, axis=1)
    w_padded = jnp.pad(
        w_own.reshape(model, 3 * heads, head_dim), ((0, 0), (0, 0), (0, LANES - head_dim))
    ).reshape(model, 3 * width)

    segs = piece_of(segment_ids, own)
    scale = query_scale * (1.0 / math.sqrt(head_dim))
    scale_pad = jnp.pad(scale, (0, LANES - head_dim))[None]
    col_scale = jnp.concatenate([jnp.tile(scale_pad, (1, heads)), jnp.ones((1, 2 * width), F32)], axis=1)
    lane = jnp.arange(LANES)[None, :]
    marks = lane >= head_dim + PARTS
    same = lane == segs[:, None] + (head_dim + PARTS)
    qpad = same.astype(BF16)
    kpad = jnp.where(
        marks, jnp.where(same, 0.0, -BIG), jnp.where(lane >= head_dim, 1.0, 0.0)
    ).astype(BF16)

    project_args = (gain_attention[None], w_padded, col_scale, qpad, kpad)
    as_table = lambda *s: jnp.stack(s).astype(jnp.int32)
    if n_fs == 8 and folds == 1 and sequences == 4 and 2 * tokens == TILE:
        pieces = own_and_sent(layer_input, own, (0, 1))
        pieces += own_and_sent(layer_input, own, (2, 3))
        odd = own % 2 == 1
        upper = own // 2

        def pair(low, high):
            return jnp.where(odd, jnp.concatenate([high, low], 0), jnp.concatenate([low, high], 0))

        def to(value, mask):
            return xor_permute(value, "fs", mask)

        def fill(blocks, place, earlier):
            sources = [block for _, block in blocks]
            tiles = as_table(*[(fs ^ mask) * 2 + place for mask, _ in blocks])
            return project(sources, tiles, *project_args, earlier, heads, head_dim, length)

        other = 1 - upper
        first = pair(pieces[0], pieces[1])
        half = TILE // 2
        sent = after(first, *received)
        y1, x1, c1 = to(sent, 4), to(sent, 2), to(sent, 1)
        y1, x1, c1 = together(y1, x1, c1)
        top1, bottom1, cy1, cx1 = to(y1[:half], 2), to(x1[half:], 4), to(y1, 1), to(x1, 1)
        qkv = fill([(0, first), (1, c1), (4, y1), (2, x1)], upper, None)
        *qkv, top1, bottom1, cy1, cx1, p2, p3 = together(*qkv, top1, bottom1, cy1, cx1, pieces[2], pieces[3])
        both1 = jnp.concatenate([top1, bottom1], axis=0)
        second = pair(p2, p3)
        y2, x2, c2, cb1 = to(second, 4), to(second, 2), to(second, 1), to(both1, 1)
        qkv = fill([(5, cy1), (3, cx1)], upper, qkv)
        *qkv, y2, x2, c2, cb1 = together(*qkv, y2, x2, c2, cb1)
        top2, bottom2, cy2, cx2 = to(y2[:half], 2), to(x2[half:], 4), to(y2, 1), to(x2, 1)
        qkv = fill([(6, both1), (7, cb1)], upper, qkv)
        qkv = fill([(0, second), (1, c2)], other, qkv)
        *qkv, top2, bottom2, cy2, cx2 = together(*qkv, top2, bottom2, cy2, cx2)
        both2 = jnp.concatenate([top2, bottom2], axis=0)
        cb2 = to(both2, 1)
        qkv = fill([(4, y2), (2, x2), (5, cy2), (3, cx2)], other, qkv)
        *qkv, cb2 = together(*qkv, cb2)
        qkv = fill([(6, both2), (7, cb2)], other, qkv)
        x_own = jnp.where(
            upper == 0, jnp.concatenate([first, second], 0), jnp.concatenate([second, first], 0)
        )
        x_sent, x_here = (p2, p3), (both2,)
    else:
        pieces = own_and_sent(layer_input, own, range(sequences))
        x_own = in_order(pieces, own).reshape(rows, model)
        gathered = lax.all_gather(x_own, ("fs", "sp"), axis=0)
        gathered = gathered.reshape(n_fs, folds, sequences, rows, model)
        gathered = lax.dynamic_index_in_dim(gathered, own, 2, keepdims=False)
        blocks = gathered.reshape(n_fs * folds, rows, model)
        tiles = jnp.arange(length // TILE, dtype=jnp.int32)
        qkv = project([blocks], tiles, *project_args, None, heads, head_dim, length)
        x_sent, x_here = (x_own,), (blocks,)
    q, k, v = qkv

    three = jnp.stack(
        [
            merged(w, d, u).T
            for w, d, u in zip((weight_mixer, weight_expand, weight_contract), downs[1:], ups[1:])
        ]
    )
    w_mixer, w_expand, w_contract = lax.all_gather(after(three, *x_here), "fs", axis=1, tiled=True)
    g_pieces = own_and_sent(after(output_grad, *x_sent), own, range(sequences))

    firsts, lasts = segs[::TILE], segs[TILE - 1 :: TILE]
    starts = jnp.sum(segs[None, :] < firsts[:, None], axis=1, dtype=jnp.int32) // TILE
    ends = (jnp.sum(segs[None, :] <= lasts[:, None], axis=1, dtype=jnp.int32) + TILE - 1) // TILE

    def sections_out(value):
        if folds > 1:
            cut = value.reshape(n_fs, folds, *value.shape[1:])
            value = lax.dynamic_index_in_dim(cut, fold_of, 1, keepdims=False)
        return lax.all_to_all(value, "fs", split_axis=0, concat_axis=0, tiled=True)

    o_even, aug = attend(starts, q, k, v, None, 0, heads, head_dim)
    a_even = sections_out(o_even)
    o_odd, aug = attend(starts, q, k, v, aug, 1, heads, head_dim)
    o_odd, a_even, g_pieces = together(o_odd, a_even, g_pieces)
    a_odd = sections_out(o_odd)
    attended = jnp.concatenate([a_even, a_odd], axis=2).reshape(model, rows)
    g_own = in_order(g_pieces, own).reshape(rows, model)

    x_f = x_own.astype(F32)
    scale_one = rms_scale(x_f)
    normed_one = (x_f * scale_one * gain_attention).astype(BF16)
    narrow = lambda u, down: dot_nn(u, down).astype(BF16)
    mixer = lax.dot_general(attended, w_mixer, (((0,), (1,)), ((), ())), preferred_element_type=F32)
    middle = x_f + mixer
    scale_two = rms_scale(middle)
    normed_two = (middle * scale_two * gain_feedforward).astype(BF16)
    expanded = dot_nt(normed_two, w_expand)
    gate = jax.nn.sigmoid(expanded)
    hidden = (expanded * gate).astype(BF16)
    contracted = dot_nt(hidden, w_contract)
    layer_output = (middle + contracted).astype(BF16).reshape(sequences, tokens, model)

    def adapter_back(u, grad, down, up):
        grad_up = dot_tn(narrow(u, down), grad)
        grad_narrow = dot_nt(grad, up).astype(BF16)
        return [dot_tn(grad_narrow, u), grad_up]

    grad_hidden = dot_nn(g_own, w_contract)
    grad_expanded = (grad_hidden * gate * (1.0 + expanded * (1.0 - gate))).astype(BF16)
    grad_normed_two = dot_nn(grad_expanded, w_expand)
    grad_middle = g_own.astype(F32) + rms_back(middle, scale_two, grad_normed_two * gain_feedforward)
    grad_mixer = grad_middle.astype(BF16)
    grad_attended = lax.dot_general(w_mixer, grad_mixer, (((0,), (1,)), ((), ())), preferred_element_type=F32)
    grad_heads = lax.all_to_all(
        grad_attended.astype(BF16).reshape(n_fs, unit, rows), "fs", split_axis=0, concat_axis=0, tiled=True
    )
    if folds > 1:
        every = lax.all_gather(grad_heads, "sp", axis=0)
        every = every.reshape(folds, sequences, n_fs, unit, rows)
        every = lax.dynamic_index_in_dim(every, own, 1, keepdims=False)
        grad_heads = jnp.swapaxes(every, 0, 1).reshape(n_fs * folds, unit, rows)

    narrow_mixer = dot_tn(attended, downs[1]).astype(BF16)
    early = jnp.concatenate(
        [
            lax.dot_general(
                dot_nt(grad_mixer, ups[1]).astype(BF16), attended, (((0,), (1,)), ((), ())), preferred_element_type=F32
            ),
            dot_tn(narrow_mixer, grad_mixer),
            *adapter_back(normed_two, grad_expanded, downs[2], ups[2]),
            *adapter_back(hidden, g_own, downs[3], ups[3]),
        ],
        axis=0,
    )
    grad_heads, early, layer_output = together(grad_heads, early, layer_output)
    w_all = lax.all_gather(after(w_own.T, grad_heads), "fs", axis=0)
    early = lax.all_to_all(
        early.reshape(n_fs, early.shape[0] // n_fs, model), "fs", split_axis=0, concat_axis=0, tiled=True
    )

    kv_even, g_aug, dq = attend_back(ends, aug, k, v, (grad_heads, o_even, o_odd), 0, heads, head_dim)
    kv_even, g_aug, dq, early = together(kv_even, g_aug, dq, early)
    kv_even = sections_out(kv_even)
    early = jnp.sum(early, axis=0)
    grads_odd = attend_back(ends, aug, k, v, (g_aug, dq, scale_pad.T), 1, heads, head_dim)
    grads_odd, kv_even, early, w_all = together(grads_odd, kv_even, early, w_all)
    out_pieces = own_and_sent(after(layer_output, grads_odd), own, range(sequences))
    grads_odd = sections_out(grads_odd)
    grads_odd, out_pieces = together(grads_odd, out_pieces)
    grad_joined = jnp.concatenate(
        [
            jnp.concatenate([grads_odd[:, :unit], kv_even], axis=1),
            jnp.concatenate([grads_odd[:, unit : 2 * unit], grads_odd[:, 2 * unit :]], axis=1),
        ],
        axis=2,
    )
    layer_output = in_order(out_pieces, own)

    up_all = (
        ups[0].reshape(rank, 3, n_fs, unit).transpose(2, 0, 1, 3).reshape(n_fs, rank, 3 * unit)
    )
    narrow_one = narrow(normed_one, downs[0])
    grad_up = jnp.einsum("tr,hct->rhc", narrow_one, grad_joined, preferred_element_type=F32)
    grad_up = grad_up.reshape(rank, n_fs, 3, unit).transpose(0, 2, 1, 3).reshape(3 * rank, model)
    grad_narrow = jnp.einsum("hct,hrc->tr", grad_joined, up_all, preferred_element_type=F32).astype(BF16)
    late = jnp.concatenate([dot_tn(grad_narrow, normed_one), grad_up], axis=0)
    grad_joined, late = together(grad_joined, late)
    split = late.reshape(n_fs, late.shape[0] // n_fs, model)
    late = [
        piece_of(split, fs) if m == 0 else xor_permute(piece_of(split, fs ^ m), "fs", m) for m in range(n_fs)
    ]
    grad_normed_one = jnp.einsum("hct,hcd->td", grad_joined, w_all, preferred_element_type=F32)
    grad_normed_one, late = together(grad_normed_one, late)
    input_grad = grad_middle + rms_back(x_f, scale_one, grad_normed_one * gain_attention)
    input_grad = input_grad.astype(BF16).reshape(sequences, tokens, model)
    if folds == 1:
        input_grad = lax.all_to_all(input_grad, "sp", split_axis=0, concat_axis=0, tiled=True)
    else:
        input_grad = in_order(own_and_sent(input_grad, own, range(sequences)), own)
    part = jnp.concatenate([sum(late[1:], late[0]), early], axis=0)
    part = over_sequences(part, sequences, n_sp)
    table = shares_of_all(fold(part, adapter_index, adapters, own), n_fs)
    table = in_order(table, fs)

    factor = 1.0 / math.sqrt(length)
    outs = []
    late_rows = late[0].shape[0]
    late = joined_rows(table[:, :, :late_rows]) * factor
    early = joined_rows(table[:, :, late_rows:]) * factor
    for tables, wides in ((late, (3,)), (early, (1, 1, 1))):
        first = 0
        for wide in wides:
            outs.append(jnp.swapaxes(tables[:, first : first + rank], 1, 2))
            first += rank
            outs.append(tables[:, first : first + rank * wide].reshape(adapters, rank, wide * model))
            first += rank * wide
    return (layer_output, input_grad, *outs)


def solution(mesh):
    tokens = P(None, ("fs", "sp"), None)
    in_specs = (tokens, tokens) + (P(),) * 5 + (P(None, "fs"),) * 4 + (P(),) * 8
    out_specs = (tokens, tokens) + (P(),) * 8
    return jax.shard_map(local, mesh=mesh, in_specs=in_specs, out_specs=out_specs, check_vma=False)
```

```python
import functools
import math

import jax
import jax.numpy as jnp
from jax import lax
from jax.experimental import pallas as pl
from jax.experimental.pallas import tpu as pltpu
from jax.sharding import PartitionSpec as P

EPSILON = 1e-06
BIG = 1e30
LANES = 128
PARTS = 3
TILE = 256
VMEM_LIMIT = 64000000
F32 = jnp.float32
BF16 = jnp.bfloat16
NT = (((1,), (1,)), ((), ()))
TN = (((0,), (0,)), ((), ()))


def dot_nn(a, b):
    return jnp.dot(a, b, preferred_element_type=F32)


def dot_nt(a, b):
    return lax.dot_general(a, b, NT, preferred_element_type=F32)


def dot_tn(a, b):
    return lax.dot_general(a, b, TN, preferred_element_type=F32)


def xor_permute(value, axis, mask):
    count = lax.axis_size(axis)
    return lax.ppermute(value, axis, [(a, a ^ mask) for a in range(count)])


def piece_of(stacked, index):
    return lax.dynamic_index_in_dim(stacked, index, 0, keepdims=False)


def project_kernel(tiles, *refs, count, heads, head_dim):
    x_refs, (gain_ref, w_ref, scale_ref, qpad_ref, kpad_ref) = refs[:count], refs[count : count + 5]
    q_ref, k_ref, v_ref, x_ref = refs[-4:]
    if count > 1:
        for n in range(count):

            @pl.when(pl.program_id(0) == n)
            def _():
                x_ref[...] = x_refs[n][...]

        x = x_ref[...].astype(F32)
    else:
        x = x_refs[0][0].astype(F32)
    mean = jnp.mean(x * x, axis=-1, keepdims=True)
    normed = (x * lax.rsqrt(mean + EPSILON) * gain_ref[...]).astype(BF16)
    rows = dot_nn(normed, w_ref[...]) * scale_ref[...]
    width = heads * LANES
    lane = lax.broadcasted_iota(jnp.int32, (1, width), 1) % LANES
    q_ref[...] = (rows[:, :width] + jnp.tile(qpad_ref[...].astype(F32), (1, heads))).astype(BF16)
    k_ref[...] = (rows[:, width : 2 * width] + jnp.tile(kpad_ref[...].astype(F32), (1, heads))).astype(BF16)
    ones = jnp.where((lane >= head_dim) & (lane < head_dim + PARTS), 1.0, 0.0)
    v_ref[...] = (rows[:, 2 * width :] + ones).astype(BF16)


def project(sources, tiles, gain, weight, scale, qpad, kpad, earlier, heads, head_dim, length):
    model = weight.shape[0]
    step = TILE
    count = len(sources)
    steps = tiles.shape[0]
    width = heads * LANES
    out = pl.BlockSpec((step, width), lambda n, t: (t[n], 0))
    pad = pl.BlockSpec((step, LANES), lambda n, t: (t[n], 0))
    fixed = lambda shape: pl.BlockSpec(shape, lambda n, t: (0,) * len(shape))
    if count > 1:
        in_specs = [fixed((step, model))] * count
    else:
        per = sources[0].shape[1] // step
        in_specs = [pl.BlockSpec((1, step, model), lambda n, t: (n // per, n % per, 0))]
    in_specs += [fixed((1, model)), fixed((model, 3 * width)), fixed((1, 3 * width)), pad, pad]
    operands = [*sources, gain, weight, scale, qpad, kpad]
    aliases = {}
    if earlier is not None:
        in_specs += [pl.BlockSpec(memory_space=pl.ANY)] * 3
        aliases = {1 + len(operands) + n: n for n in range(3)}
        operands += list(earlier)
    return pl.pallas_call(
        functools.partial(project_kernel, count=count, heads=heads, head_dim=head_dim),
        out_shape=[jax.ShapeDtypeStruct((length, width), BF16)] * 3,
        grid_spec=pltpu.PrefetchScalarGridSpec(
            num_scalar_prefetch=1,
            grid=(steps,),
            in_specs=in_specs,
            out_specs=[out] * 3,
            scratch_shapes=[pltpu.VMEM((step, model), BF16)],
        ),
        input_output_aliases=aliases,
        compiler_params=pltpu.CompilerParams(vmem_limit_bytes=VMEM_LIMIT),
        cost_estimate=pl.CostEstimate(
            flops=1,
            bytes_accessed=1,
            transcendentals=0,
        ),
        name="project",
    )(tiles, *operands)


def spread(row, index, first):
    high = row.astype(BF16).astype(F32)
    middle = (row - high).astype(BF16).astype(F32)
    last = row - high - middle
    return jnp.where(index == first, high, jnp.where(index == first + 1, middle, last))


def at(block):
    return pl.ds(pl.multiple_of(block * TILE, TILE), TILE)


def attend_kernel(starts, q_ref, k_ref, v_ref, *refs, heads, head_dim, parity):
    o_ref, aug_ref = refs[-2:]
    step = 2 * pl.program_id(0) + parity
    first = starts[step]
    index = lax.broadcasted_iota(jnp.int32, (LANES, 1), 0)
    marks = (index >= head_dim) & (index < head_dim + PARTS)

    def cols(h):
        return pl.ds(h * LANES, LANES)

    turned = [jnp.transpose(q_ref[:, cols(h)].astype(F32)) for h in range(heads)]
    queries = [t.astype(BF16) for t in turned]

    def one(block, carry, masked):
        scores = [dot_nn(k_ref[at(block), cols(h)], queries[h]) for h in range(heads)]
        out = []
        for h, s in enumerate(scores):
            if masked:
                key = lax.broadcasted_iota(jnp.int32, (TILE, TILE), 0)
                query = lax.broadcasted_iota(jnp.int32, (TILE, TILE), 1)
                s = jnp.where(key <= query, s, -BIG)
            peak = jnp.max(s, axis=0, keepdims=True)
            if not masked:
                peak = jnp.maximum(carry[h][0], peak)
            p = jnp.exp(s - peak).astype(BF16)
            total = dot_tn(v_ref[at(block), cols(h)], p)
            if not masked:
                total = carry[h][1] * jnp.exp(carry[h][0] - peak) + total
            out.append((peak, total))
        return tuple(out)

    carry = one(step, None, True)
    carry = lax.fori_loop(first, step, lambda block, c: one(block, c, False), carry)
    for h in range(heads):
        peak, total = carry[h]
        weight = total[head_dim : head_dim + 1]
        o_ref[0, h * head_dim : (h + 1) * head_dim, :] = (total / weight)[:head_dim].astype(BF16)
        lse = -(peak + jnp.log(weight))
        aug_ref[cols(h), :] = jnp.where(marks, spread(lse, index, head_dim), turned[h]).astype(BF16)


def attend(starts, q, k, v, earlier, parity, heads, head_dim):
    length, width = q.shape
    steps = length // TILE // 2
    whole = pl.BlockSpec((length, width), lambda n, st: (0, 0))
    in_specs = [pl.BlockSpec((TILE, width), lambda n, st: (2 * n + parity, 0)), whole, whole]
    operands = [q, k, v]
    aliases = {}
    if earlier is not None:
        in_specs.append(pl.BlockSpec(memory_space=pl.ANY))
        operands.append(earlier)
        aliases = {4: 1}
    return pl.pallas_call(
        functools.partial(attend_kernel, heads=heads, head_dim=head_dim, parity=parity),
        out_shape=[
            jax.ShapeDtypeStruct((steps, heads * head_dim, TILE), BF16),
            jax.ShapeDtypeStruct((width, length), BF16),
        ],
        grid_spec=pltpu.PrefetchScalarGridSpec(
            num_scalar_prefetch=1,
            grid=(steps,),
            in_specs=in_specs,
            out_specs=[
                pl.BlockSpec((1, heads * head_dim, TILE), lambda n, st: (n, 0, 0)),
                pl.BlockSpec((width, TILE), lambda n, st: (0, 2 * n + parity)),
            ],
        ),
        input_output_aliases=aliases,
        compiler_params=pltpu.CompilerParams(vmem_limit_bytes=VMEM_LIMIT),
        cost_estimate=pl.CostEstimate(
            flops=1, bytes_accessed=1, transcendentals=0
        ),
        name="attend",
    )(starts, *operands)


def attend_back_kernel(ends, aug_ref, k_ref, v_ref, *refs, heads, head_dim, parity):
    step = 2 * pl.program_id(0) + parity
    length = aug_ref.shape[1]
    unit = heads * head_dim
    if parity == 0:
        g_ref, even_ref, odd_ref, kv_ref, g_out_ref, dq_ref, dk_ref, dv_ref = refs
        gaug_ref = g_out_ref
    else:
        gaug_ref, dq_in_ref, scale_ref, all_ref, dq_ref, dk_ref, dv_ref = refs

    def cols(h):
        return pl.ds(h * LANES, LANES)

    def own(h):
        return slice(h * head_dim, (h + 1) * head_dim)

    @pl.when(step == parity)
    def _():
        dq_ref[...] = jnp.zeros_like(dq_ref)
        if parity == 0:
            index = lax.broadcasted_iota(jnp.int32, (LANES - head_dim, 1), 0)

            @pl.loop(0, length // TILE // 2)
            def _(n):
                for part, o_ref in enumerate((even_ref, odd_ref)):
                    rows = at(2 * n + part)
                    g = g_ref[n, :, part * TILE : (part + 1) * TILE]
                    product = g.astype(F32) * o_ref[n].astype(F32)
                    for h in range(heads):
                        delta = -jnp.sum(product[own(h)], axis=0, keepdims=True)
                        gaug_ref[h * LANES : h * LANES + head_dim, rows] = g[own(h)]
                        gaug_ref[h * LANES + head_dim : (h + 1) * LANES, rows] = jnp.where(
                            index < PARTS, spread(delta, index, 0), 0.0
                        ).astype(BF16)

    dk_ref[...] = jnp.zeros_like(dk_ref)
    dv_ref[...] = jnp.zeros_like(dv_ref)
    keys = [k_ref[:, cols(h)] for h in range(heads)]
    turned = [jnp.transpose(k.astype(F32)).astype(BF16) for k in keys]

    def one(block, masked):
        for h in range(heads):
            q = aug_ref[cols(h), at(block)]
            g = gaug_ref[cols(h), at(block)]
            s = dot_nn(keys[h], q)
            if masked:
                key = lax.broadcasted_iota(jnp.int32, (TILE, TILE), 0)
                query = lax.broadcasted_iota(jnp.int32, (TILE, TILE), 1)
                s = jnp.where(key <= query, s, -BIG)
            p = jnp.exp(s)
            d = dot_nn(v_ref[:, cols(h)], g)
            dv_ref[:, cols(h)] += dot_nt(p.astype(BF16), g)
            ds = (p * d).astype(BF16)
            dk_ref[:, cols(h)] += dot_nt(ds, q)
            dq_ref[cols(h), at(block)] += dot_nn(turned[h], ds)

    one(step, True)

    @pl.loop(step + 1, ends[step])
    def _(block):
        one(block, False)

    pieces = []
    for ref in (dk_ref, dv_ref):
        for h in range(heads):
            pieces.append(jnp.transpose(ref[:, cols(h)])[:head_dim].astype(BF16))
    if parity == 0:
        for n, piece in enumerate(pieces):
            kv_ref[0, n * head_dim : (n + 1) * head_dim, :] = piece
    else:
        for n, piece in enumerate(pieces):
            all_ref[0, 2 * unit + n * head_dim : 2 * unit + (n + 1) * head_dim, :] = piece
        for part in range(2):
            rows = at(step - 1 + part)
            for h in range(heads):
                dq = (dq_in_ref[cols(h), rows] + dq_ref[cols(h), rows]).astype(BF16).astype(F32)
                all_ref[0, part * unit + h * head_dim : part * unit + (h + 1) * head_dim, :] = (
                    dq * scale_ref[...]
                )[:head_dim].astype(BF16)


def attend_back(ends, aug, k, v, others, parity, heads, head_dim):
    width, length = aug.shape
    steps = length // TILE // 2
    unit = heads * head_dim
    whole = lambda *shape: pl.BlockSpec(shape, lambda n, st: (0,) * len(shape))
    row = pl.BlockSpec((TILE, width), lambda n, st: (2 * n + parity, 0))
    out = lambda rows: pl.BlockSpec((1, rows, TILE), lambda n, st: (n, 0, 0))
    scratch = [pltpu.VMEM((TILE, width), F32)] * 2
    if parity == 0:
        in_specs = [whole(*value.shape) for value in others]
        out_shape = [
            jax.ShapeDtypeStruct((steps, 2 * unit, TILE), BF16),
            jax.ShapeDtypeStruct((width, length), BF16),
            jax.ShapeDtypeStruct((width, length), F32),
        ]
        out_specs = [out(2 * unit), whole(width, length), whole(width, length)]
    else:
        in_specs = [whole(*value.shape) for value in others]
        out_shape = jax.ShapeDtypeStruct((steps, 4 * unit, TILE), BF16)
        out_specs = out(4 * unit)
        scratch = [pltpu.VMEM((width, length), F32)] + scratch
    return pl.pallas_call(
        functools.partial(attend_back_kernel, heads=heads, head_dim=head_dim, parity=parity),
        out_shape=out_shape,
        grid_spec=pltpu.PrefetchScalarGridSpec(
            num_scalar_prefetch=1,
            grid=(steps,),
            in_specs=[whole(width, length), row, row, *in_specs],
            out_specs=out_specs,
            scratch_shapes=scratch,
        ),
        compiler_params=pltpu.CompilerParams(vmem_limit_bytes=VMEM_LIMIT),
        cost_estimate=pl.CostEstimate(
            flops=1, bytes_accessed=1, transcendentals=0
        ),
        name="attend_back",
    )(ends, aug, k, v, *others)


def project_back_kernel(
    rest_ref, even_ref, w_ref, up_ref, narrow_ref, x_ref, middle_ref, gain_ref, in_ref, down_ref, grad_up_ref, sum_ref, thin_ref
):
    step = pl.program_id(0)
    unit = even_ref.shape[1] // 2

    @pl.when(step == 0)
    def _():
        sum_ref[...] = jnp.zeros_like(sum_ref)
        thin_ref[...] = jnp.zeros_like(thin_ref)

    odd = rest_ref[0, unit:, :]
    even = jnp.concatenate([rest_ref[0, :unit, :], even_ref[0]], axis=0)
    grad_up = None
    for n, joined in enumerate((even, odd)):
        part = slice(n * TILE, (n + 1) * TILE)
        sum_ref[part, :] += dot_tn(joined, w_ref[0])
        thin_ref[:, part] += dot_nn(up_ref[0], joined)
        term = dot_nt(narrow_ref[:, part], joined)
        grad_up = term if grad_up is None else grad_up + term
    grad_up_ref[0] = grad_up

    @pl.when(step == pl.num_programs(0) - 1)
    def _():
        down = None
        for n in range(2):
            part = slice(n * TILE, (n + 1) * TILE)
            x = x_ref[part, :].astype(F32)
            scale = lax.rsqrt(jnp.mean(x * x, axis=-1, keepdims=True) + EPSILON)
            normed = (x * scale * gain_ref[...]).astype(BF16)
            grad = sum_ref[part, :] * gain_ref[...]
            mean = jnp.mean(grad * x, axis=-1, keepdims=True)
            in_ref[part, :] = (
                middle_ref[part, :] + scale * grad - x * (scale * scale * scale) * mean
            ).astype(BF16)
            term = dot_nn(thin_ref[:, part].astype(BF16), normed)
            down = term if down is None else down + term
        down_ref[...] = down


def project_back(rest, even, weight, up, narrow_turned, x, grad_middle, gain):
    blocks, columns, model = weight.shape
    rank, rows = narrow_turned.shape
    each = lambda value: pl.BlockSpec((1, *value.shape[1:]), lambda n: (n, 0, 0))
    fixed = lambda shape: pl.BlockSpec(shape, lambda n: (0,) * len(shape))
    return pl.pallas_call(
        project_back_kernel,
        out_shape=[
            jax.ShapeDtypeStruct((rows, model), BF16),
            jax.ShapeDtypeStruct((rank, model), F32),
            jax.ShapeDtypeStruct((blocks, rank, columns), F32),
        ],
        grid=(blocks,),
        in_specs=[
            each(rest),
            each(even),
            each(weight),
            each(up),
            fixed((rank, rows)),
            fixed((rows, model)),
            fixed((rows, model)),
            fixed((1, model)),
        ],
        out_specs=[
            fixed((rows, model)),
            fixed((rank, model)),
            pl.BlockSpec((1, rank, columns), lambda n: (n, 0, 0)),
        ],
        scratch_shapes=[pltpu.VMEM((rows, model), F32), pltpu.VMEM((rank, rows), F32)],
        compiler_params=pltpu.CompilerParams(vmem_limit_bytes=VMEM_LIMIT),
        cost_estimate=pl.CostEstimate(flops=1, bytes_accessed=1, transcendentals=0),
        name="project_back",
    )(rest, even, weight, up, narrow_turned, x, grad_middle, gain)


def rms_scale(values):
    return lax.rsqrt(jnp.mean(values * values, axis=-1, keepdims=True) + EPSILON)


def rms_back(values, scale_rows, grad_normed):
    cubed = scale_rows * scale_rows * scale_rows
    return scale_rows * grad_normed - values * cubed * jnp.mean(
        grad_normed * values, axis=-1, keepdims=True
    )


def after(value, *others):
    return lax.optimization_barrier((value, others))[0]


def together(*values):
    return lax.optimization_barrier(values)


def own_and_sent(value, own, masks):
    return [
        piece_of(value, own) if m == 0 else xor_permute(piece_of(value, own ^ m), "sp", m) for m in masks
    ]


def in_order(pieces, own):
    stacked = jnp.stack(pieces)
    return jnp.stack([piece_of(stacked, n ^ own) for n in range(len(pieces))], axis=0)


def shares_of_all(table, n_fs, pieces):
    to = lambda value, mask: xor_permute(value, "fs", mask)
    if n_fs != 8 or table.shape[0] % 2:
        return [table] + [to(table, m) for m in range(1, n_fs)]
    half = table.shape[0] // 2
    y, x, core, pieces[3] = together(to(table, 4), to(table, 2), to(table, 1), pieces[3])
    top, bottom, core_y, core_x = to(y[:half], 2), to(x[half:], 4), to(y, 1), to(x, 1)
    both = jnp.concatenate([top, bottom], axis=0)
    return [table, core, x, core_x, y, core_y, both, to(both, 1)]


def over_sequences(part, groups, n_sp):
    mask = groups
    while mask < n_sp:
        part = part + xor_permute(part, "sp", mask)
        mask <<= 1
    return [part] + [xor_permute(part, "sp", m) for m in range(1, groups)]


def fold(pieces, adapter_index, adapters, own):
    by_seq = in_order(pieces, own)
    tables = []
    for a in range(adapters):
        table = jnp.zeros_like(pieces[0])
        for s in range(len(pieces)):
            table = table + jnp.where(adapter_index[s, 0] == a, by_seq[s], 0.0)
        tables.append(table)
    return jnp.stack(tables)


def joined_rows(every):
    n, adapters, rows, model = every.shape
    return jnp.swapaxes(every, 0, 1).reshape(adapters, n * rows, model)


def local(
    layer_input,
    output_grad,
    segment_ids,
    adapter_index,
    gain_attention,
    gain_feedforward,
    query_scale,
    weight_qkv,
    weight_mixer,
    weight_expand,
    weight_contract,
    qkv_down,
    qkv_up,
    mixer_down,
    mixer_up,
    expand_down,
    expand_up,
    contract_down,
    contract_up,
):
    sequences, tokens, model = layer_input.shape
    head_dim = query_scale.shape[0]
    n_fs, n_sp = lax.axis_size("fs"), lax.axis_size("sp")
    adapters, rank = qkv_down.shape[0], qkv_down.shape[2]
    length = segment_ids.shape[1]
    folds = n_sp // sequences
    heads = model // head_dim // n_fs
    unit = heads * head_dim
    width = heads * LANES
    rows = sequences * tokens
    fs = lax.axis_index("fs")
    sp = lax.axis_index("sp")
    own = sp % sequences
    fold_of = sp // sequences

    pick = piece_of(adapter_index, own)[0]
    downs = [piece_of(t, pick) for t in (qkv_down, mixer_down, expand_down, contract_down)]
    ups = [piece_of(t, pick) for t in (qkv_up, mixer_up, expand_up, contract_up)]

    def merged(weight, down, up):
        cols = weight.shape[1]
        own_up = lax.dynamic_slice_in_dim(up, fs * cols, cols, 1)
        return (weight.astype(F32) + dot_nn(down, own_up)).astype(BF16)

    shard = merged(weight_qkv, downs[0], ups[0])
    inverse = pow(3, -1, n_fs)
    received = [
        lax.ppermute(
            shard[:, t * unit : (t + 1) * unit], "fs", [(d, (3 * d + t) % n_fs) for d in range(n_fs)]
        )
        for t in range(3)
    ]
    places = [(3 * ((inverse * (fs - t)) % n_fs) + t) // n_fs for t in range(3)]
    w_parts = []
    for b in range(3):
        part = jnp.zeros_like(received[0])
        for t in range(3):
            part = jnp.where(places[t] == b, received[t], part)
        w_parts.append(part)
    w_own = jnp.concatenate(w_parts, axis=1)
    w_padded = jnp.pad(
        w_own.reshape(model, 3 * heads, head_dim), ((0, 0), (0, 0), (0, LANES - head_dim))
    ).reshape(model, 3 * width)

    segs = piece_of(segment_ids, own)
    scale = query_scale * (1.0 / math.sqrt(head_dim))
    scale_pad = jnp.pad(scale, (0, LANES - head_dim))[None]
    col_scale = jnp.concatenate([jnp.tile(scale_pad, (1, heads)), jnp.ones((1, 2 * width), F32)], axis=1)
    lane = jnp.arange(LANES)[None, :]
    marks = lane >= head_dim + PARTS
    same = lane == segs[:, None] + (head_dim + PARTS)
    qpad = same.astype(BF16)
    kpad = jnp.where(
        marks, jnp.where(same, 0.0, -BIG), jnp.where(lane >= head_dim, 1.0, 0.0)
    ).astype(BF16)

    project_args = (gain_attention[None], w_padded, col_scale, qpad, kpad)
    as_table = lambda *s: jnp.stack(s).astype(jnp.int32)
    if n_fs == 8 and folds == 1 and sequences == 4 and 2 * tokens == TILE:
        pieces = own_and_sent(layer_input, own, (0, 1))
        pieces += own_and_sent(layer_input, own, (2, 3))
        odd = own % 2 == 1
        upper = own // 2

        def pair(low, high):
            return jnp.where(odd, jnp.concatenate([high, low], 0), jnp.concatenate([low, high], 0))

        def to(value, mask):
            return xor_permute(value, "fs", mask)

        def fill(blocks, place, earlier):
            sources = [block for _, block in blocks]
            tiles = as_table(*[(fs ^ mask) * 2 + place for mask, _ in blocks])
            return project(sources, tiles, *project_args, earlier, heads, head_dim, length)

        other = 1 - upper
        first = pair(pieces[0], pieces[1])
        half = TILE // 2
        sent = after(first, *received)
        y1, x1, c1 = to(sent, 4), to(sent, 2), to(sent, 1)
        y1, x1, c1 = together(y1, x1, c1)
        top1, bottom1, cy1, cx1 = to(y1[:half], 2), to(x1[half:], 4), to(y1, 1), to(x1, 1)
        qkv = fill([(0, first), (1, c1), (4, y1), (2, x1)], upper, None)
        *qkv, top1, bottom1, cy1, cx1, p2, p3 = together(*qkv, top1, bottom1, cy1, cx1, pieces[2], pieces[3])
        both1 = jnp.concatenate([top1, bottom1], axis=0)
        second = pair(p2, p3)
        y2, x2, c2, cb1 = to(second, 4), to(second, 2), to(second, 1), to(both1, 1)
        qkv = fill([(5, cy1), (3, cx1)], upper, qkv)
        *qkv, y2, x2, c2, cb1 = together(*qkv, y2, x2, c2, cb1)
        top2, bottom2, cy2, cx2 = to(y2[:half], 2), to(x2[half:], 4), to(y2, 1), to(x2, 1)
        qkv = fill([(6, both1), (7, cb1)], upper, qkv)
        qkv = fill([(0, second), (1, c2)], other, qkv)
        *qkv, top2, bottom2, cy2, cx2 = together(*qkv, top2, bottom2, cy2, cx2)
        both2 = jnp.concatenate([top2, bottom2], axis=0)
        cb2 = to(both2, 1)
        qkv = fill([(4, y2), (2, x2), (5, cy2), (3, cx2)], other, qkv)
        *qkv, cb2 = together(*qkv, cb2)
        qkv = fill([(6, both2), (7, cb2)], other, qkv)
        x_own = jnp.where(
            upper == 0, jnp.concatenate([first, second], 0), jnp.concatenate([second, first], 0)
        )
        x_sent, x_here = (p2, p3), (both2,)
    else:
        pieces = own_and_sent(layer_input, own, range(sequences))
        x_own = in_order(pieces, own).reshape(rows, model)
        gathered = lax.all_gather(x_own, ("fs", "sp"), axis=0)
        gathered = gathered.reshape(n_fs, folds, sequences, rows, model)
        gathered = lax.dynamic_index_in_dim(gathered, own, 2, keepdims=False)
        blocks = gathered.reshape(n_fs * folds, rows, model)
        tiles = jnp.arange(length // TILE, dtype=jnp.int32)
        qkv = project([blocks], tiles, *project_args, None, heads, head_dim, length)
        x_sent, x_here = (x_own,), (blocks,)
    q, k, v = qkv

    three = jnp.stack(
        [
            merged(w, d, u).T
            for w, d, u in zip((weight_mixer, weight_expand, weight_contract), downs[1:], ups[1:])
        ]
    )
    w_mixer, w_expand, w_contract = lax.all_gather(after(three, *x_here), "fs", axis=1, tiled=True)
    g_pieces = own_and_sent(after(output_grad, *x_sent), own, range(sequences))

    firsts, lasts = segs[::TILE], segs[TILE - 1 :: TILE]
    starts = jnp.sum(segs[None, :] < firsts[:, None], axis=1, dtype=jnp.int32) // TILE
    ends = (jnp.sum(segs[None, :] <= lasts[:, None], axis=1, dtype=jnp.int32) + TILE - 1) // TILE

    def sections_out(value):
        if folds > 1:
            cut = value.reshape(n_fs, folds, *value.shape[1:])
            value = lax.dynamic_index_in_dim(cut, fold_of, 1, keepdims=False)
        return lax.all_to_all(value, "fs", split_axis=0, concat_axis=0, tiled=True)

    o_even, aug = attend(starts, q, k, v, None, 0, heads, head_dim)
    a_even = sections_out(o_even)
    o_odd, aug = attend(starts, q, k, v, aug, 1, heads, head_dim)
    o_odd, a_even, g_pieces = together(o_odd, a_even, g_pieces)
    a_odd = sections_out(o_odd)
    attended = jnp.concatenate([a_even, a_odd], axis=2).reshape(model, rows)
    g_own = in_order(g_pieces, own).reshape(rows, model)

    x_f = x_own.astype(F32)
    scale_one = rms_scale(x_f)
    normed_one = (x_f * scale_one * gain_attention).astype(BF16)
    narrow = lambda u, down: dot_nn(u, down).astype(BF16)
    mixer = lax.dot_general(attended, w_mixer, (((0,), (1,)), ((), ())), preferred_element_type=F32)
    middle = x_f + mixer
    scale_two = rms_scale(middle)
    normed_two = (middle * scale_two * gain_feedforward).astype(BF16)
    expanded = dot_nt(normed_two, w_expand)
    gate = jax.nn.sigmoid(expanded)
    hidden = (expanded * gate).astype(BF16)
    contracted = dot_nt(hidden, w_contract)
    layer_output = (middle + contracted).astype(BF16).reshape(sequences, tokens, model)

    def adapter_back(u, grad, down, up):
        grad_up = dot_tn(narrow(u, down), grad)
        grad_narrow = dot_nt(grad, up).astype(BF16)
        return [dot_tn(grad_narrow, u), grad_up]

    grad_hidden = dot_nn(g_own, w_contract)
    grad_expanded = (grad_hidden * gate * (1.0 + expanded * (1.0 - gate))).astype(BF16)
    grad_normed_two = dot_nn(grad_expanded, w_expand)
    grad_middle = g_own.astype(F32) + rms_back(middle, scale_two, grad_normed_two * gain_feedforward)
    grad_mixer = grad_middle.astype(BF16)
    grad_attended = lax.dot_general(w_mixer, grad_mixer, (((0,), (1,)), ((), ())), preferred_element_type=F32)
    grad_heads = lax.all_to_all(
        grad_attended.astype(BF16).reshape(n_fs, unit, rows), "fs", split_axis=0, concat_axis=0, tiled=True
    )
    if folds > 1:
        every = lax.all_gather(grad_heads, "sp", axis=0)
        every = every.reshape(folds, sequences, n_fs, unit, rows)
        every = lax.dynamic_index_in_dim(every, own, 1, keepdims=False)
        grad_heads = jnp.swapaxes(every, 0, 1).reshape(n_fs * folds, unit, rows)

    narrow_mixer = dot_tn(attended, downs[1]).astype(BF16)
    early = jnp.concatenate(
        [
            lax.dot_general(
                dot_nt(grad_mixer, ups[1]).astype(BF16), attended, (((0,), (1,)), ((), ())), preferred_element_type=F32
            ),
            dot_tn(narrow_mixer, grad_mixer),
            *adapter_back(normed_two, grad_expanded, downs[2], ups[2]),
            *adapter_back(hidden, g_own, downs[3], ups[3]),
        ],
        axis=0,
    )
    grad_heads, early, layer_output = together(grad_heads, early, layer_output)
    w_all = lax.all_gather(after(w_own.T, grad_heads), "fs", axis=0)
    early = lax.all_to_all(
        early.reshape(n_fs, early.shape[0] // n_fs, model), "fs", split_axis=0, concat_axis=0, tiled=True
    )

    kv_even, g_aug, dq = attend_back(ends, aug, k, v, (grad_heads, o_even, o_odd), 0, heads, head_dim)
    kv_even, g_aug, dq, early = together(kv_even, g_aug, dq, early)
    kv_even = sections_out(kv_even)
    early = jnp.sum(early, axis=0)
    grads_odd = attend_back(ends, aug, k, v, (g_aug, dq, scale_pad.T), 1, heads, head_dim)
    grads_odd, kv_even, early, w_all = together(grads_odd, kv_even, early, w_all)
    out_pieces = own_and_sent(after(layer_output, grads_odd), own, range(sequences))
    grads_odd = sections_out(grads_odd)
    grads_odd, out_pieces = together(grads_odd, out_pieces)
    layer_output = in_order(out_pieces, own)

    up_all = (
        ups[0].reshape(rank, 3, n_fs, unit).transpose(2, 0, 1, 3).reshape(n_fs, rank, 3 * unit)
    )
    narrow_turned = lax.dot_general(
        downs[0], normed_one, (((0,), (1,)), ((), ())), preferred_element_type=F32
    ).astype(BF16)
    input_grad, grad_down, grad_up = project_back(
        grads_odd, kv_even, w_all, up_all, narrow_turned, x_own, grad_middle, gain_attention[None]
    )
    input_grad = input_grad.reshape(sequences, tokens, model)
    grad_up = grad_up.reshape(n_fs, rank, 3, unit).transpose(1, 2, 0, 3).reshape(3 * rank, model)
    late = jnp.concatenate([grad_down, grad_up], axis=0)
    split = late.reshape(n_fs, late.shape[0] // n_fs, model)
    late = [
        piece_of(split, fs) if m == 0 else xor_permute(piece_of(split, fs ^ m), "fs", m) for m in range(n_fs)
    ]
    in_pieces = own_and_sent(input_grad, own, range(sequences))
    late, in_pieces[1] = together(late, in_pieces[1])
    part = jnp.concatenate([sum(late[1:], late[0]), early], axis=0)
    part = over_sequences(part, sequences, n_sp)
    part, in_pieces[2] = together(part, in_pieces[2])
    table = shares_of_all(fold(part, adapter_index, adapters, own), n_fs, in_pieces)
    table = in_order(table, fs)
    input_grad = in_order(in_pieces, own)

    factor = 1.0 / math.sqrt(length)
    outs = []
    late_rows = late[0].shape[0]
    late = joined_rows(table[:, :, :late_rows]) * factor
    early = joined_rows(table[:, :, late_rows:]) * factor
    for tables, wides in ((late, (3,)), (early, (1, 1, 1))):
        first = 0
        for wide in wides:
            outs.append(jnp.swapaxes(tables[:, first : first + rank], 1, 2))
            first += rank
            outs.append(tables[:, first : first + rank * wide].reshape(adapters, rank, wide * model))
            first += rank * wide
    return (layer_output, input_grad, *outs)


def solution(mesh):
    tokens = P(None, ("fs", "sp"), None)
    in_specs = (tokens, tokens) + (P(),) * 5 + (P(None, "fs"),) * 4 + (P(),) * 8
    out_specs = (tokens, tokens) + (P(),) * 8
    return jax.shard_map(local, mesh=mesh, in_specs=in_specs, out_specs=out_specs, check_vma=False)
```

```python
import functools
import math

import jax
import jax.numpy as jnp
from jax import lax
from jax.experimental import pallas as pl
from jax.experimental.pallas import tpu as pltpu
from jax.sharding import PartitionSpec as P

EPSILON = 1e-06
BIG = 1e30
LANES = 128
PARTS = 3
TILE = 256
VMEM_LIMIT = 64000000
F32 = jnp.float32
BF16 = jnp.bfloat16
NT = (((1,), (1,)), ((), ()))
TN = (((0,), (0,)), ((), ()))


def dot_nn(a, b):
    return jnp.dot(a, b, preferred_element_type=F32)


def dot_nt(a, b):
    return lax.dot_general(a, b, NT, preferred_element_type=F32)


def dot_tn(a, b):
    return lax.dot_general(a, b, TN, preferred_element_type=F32)


def xor_permute(value, axis, mask):
    count = lax.axis_size(axis)
    return lax.ppermute(value, axis, [(a, a ^ mask) for a in range(count)])


def piece_of(stacked, index):
    return lax.dynamic_index_in_dim(stacked, index, 0, keepdims=False)


def project_kernel(tiles, *refs, count, heads, head_dim):
    x_refs, (gain_ref, w_ref, scale_ref, qpad_ref, kpad_ref) = refs[:count], refs[count : count + 5]
    q_ref, k_ref, v_ref, x_ref = refs[-4:]
    if count > 1:
        for n in range(count):

            @pl.when(pl.program_id(0) == n)
            def _():
                x_ref[...] = x_refs[n][...]

        x = x_ref[...].astype(F32)
    else:
        x = x_refs[0][0].astype(F32)
    mean = jnp.mean(x * x, axis=-1, keepdims=True)
    normed = (x * lax.rsqrt(mean + EPSILON) * gain_ref[...]).astype(BF16)
    rows = dot_nn(normed, w_ref[...]) * scale_ref[...]
    width = heads * LANES
    lane = lax.broadcasted_iota(jnp.int32, (1, width), 1) % LANES
    q_ref[...] = (rows[:, :width] + jnp.tile(qpad_ref[...].astype(F32), (1, heads))).astype(BF16)
    k_ref[...] = (rows[:, width : 2 * width] + jnp.tile(kpad_ref[...].astype(F32), (1, heads))).astype(BF16)
    ones = jnp.where((lane >= head_dim) & (lane < head_dim + PARTS), 1.0, 0.0)
    v_ref[...] = (rows[:, 2 * width :] + ones).astype(BF16)


def project(sources, tiles, gain, weight, scale, qpad, kpad, earlier, heads, head_dim, length):
    model = weight.shape[0]
    step = TILE
    count = len(sources)
    steps = tiles.shape[0]
    width = heads * LANES
    out = pl.BlockSpec((step, width), lambda n, t: (t[n], 0))
    pad = pl.BlockSpec((step, LANES), lambda n, t: (t[n], 0))
    fixed = lambda shape: pl.BlockSpec(shape, lambda n, t: (0,) * len(shape))
    if count > 1:
        in_specs = [fixed((step, model))] * count
    else:
        per = sources[0].shape[1] // step
        in_specs = [pl.BlockSpec((1, step, model), lambda n, t: (n // per, n % per, 0))]
    in_specs += [fixed((1, model)), fixed((model, 3 * width)), fixed((1, 3 * width)), pad, pad]
    operands = [*sources, gain, weight, scale, qpad, kpad]
    aliases = {}
    if earlier is not None:
        in_specs += [pl.BlockSpec(memory_space=pl.ANY)] * 3
        aliases = {1 + len(operands) + n: n for n in range(3)}
        operands += list(earlier)
    return pl.pallas_call(
        functools.partial(project_kernel, count=count, heads=heads, head_dim=head_dim),
        out_shape=[jax.ShapeDtypeStruct((length, width), BF16)] * 3,
        grid_spec=pltpu.PrefetchScalarGridSpec(
            num_scalar_prefetch=1,
            grid=(steps,),
            in_specs=in_specs,
            out_specs=[out] * 3,
            scratch_shapes=[pltpu.VMEM((step, model), BF16)],
        ),
        input_output_aliases=aliases,
        compiler_params=pltpu.CompilerParams(vmem_limit_bytes=VMEM_LIMIT),
        cost_estimate=pl.CostEstimate(
            flops=1,
            bytes_accessed=1,
            transcendentals=0,
        ),
        name="project",
    )(tiles, *operands)


def spread(row, index, first):
    high = row.astype(BF16).astype(F32)
    middle = (row - high).astype(BF16).astype(F32)
    last = row - high - middle
    return jnp.where(index == first, high, jnp.where(index == first + 1, middle, last))


def at(block):
    return pl.ds(pl.multiple_of(block * TILE, TILE), TILE)


def attend_kernel(starts, q_ref, k_ref, v_ref, *refs, heads, head_dim, parity):
    o_ref, aug_ref = refs[-2:]
    step = 2 * pl.program_id(0) + parity
    first = starts[step]
    index = lax.broadcasted_iota(jnp.int32, (LANES, 1), 0)
    marks = (index >= head_dim) & (index < head_dim + PARTS)

    def cols(h):
        return pl.ds(h * LANES, LANES)

    turned = [jnp.transpose(q_ref[:, cols(h)].astype(F32)) for h in range(heads)]
    queries = [t.astype(BF16) for t in turned]

    def one(block, carry, masked):
        scores = [dot_nn(k_ref[at(block), cols(h)], queries[h]) for h in range(heads)]
        out = []
        for h, s in enumerate(scores):
            if masked:
                key = lax.broadcasted_iota(jnp.int32, (TILE, TILE), 0)
                query = lax.broadcasted_iota(jnp.int32, (TILE, TILE), 1)
                s = jnp.where(key <= query, s, -BIG)
            peak = jnp.max(s, axis=0, keepdims=True)
            if not masked:
                peak = jnp.maximum(carry[h][0], peak)
            p = jnp.exp(s - peak).astype(BF16)
            total = dot_tn(v_ref[at(block), cols(h)], p)
            if not masked:
                total = carry[h][1] * jnp.exp(carry[h][0] - peak) + total
            out.append((peak, total))
        return tuple(out)

    carry = one(step, None, True)
    carry = lax.fori_loop(first, step, lambda block, c: one(block, c, False), carry)
    for h in range(heads):
        peak, total = carry[h]
        weight = total[head_dim : head_dim + 1]
        o_ref[0, h * head_dim : (h + 1) * head_dim, :] = (total / weight)[:head_dim].astype(BF16)
        lse = -(peak + jnp.log(weight))
        aug_ref[cols(h), :] = jnp.where(marks, spread(lse, index, head_dim), turned[h]).astype(BF16)


def attend(starts, q, k, v, earlier, parity, heads, head_dim):
    length, width = q.shape
    steps = length // TILE // 2
    whole = pl.BlockSpec((length, width), lambda n, st: (0, 0))
    in_specs = [pl.BlockSpec((TILE, width), lambda n, st: (2 * n + parity, 0)), whole, whole]
    operands = [q, k, v]
    aliases = {}
    if earlier is not None:
        in_specs.append(pl.BlockSpec(memory_space=pl.ANY))
        operands.append(earlier)
        aliases = {4: 1}
    return pl.pallas_call(
        functools.partial(attend_kernel, heads=heads, head_dim=head_dim, parity=parity),
        out_shape=[
            jax.ShapeDtypeStruct((steps, heads * head_dim, TILE), BF16),
            jax.ShapeDtypeStruct((width, length), BF16),
        ],
        grid_spec=pltpu.PrefetchScalarGridSpec(
            num_scalar_prefetch=1,
            grid=(steps,),
            in_specs=in_specs,
            out_specs=[
                pl.BlockSpec((1, heads * head_dim, TILE), lambda n, st: (n, 0, 0)),
                pl.BlockSpec((width, TILE), lambda n, st: (0, 2 * n + parity)),
            ],
        ),
        input_output_aliases=aliases,
        compiler_params=pltpu.CompilerParams(vmem_limit_bytes=VMEM_LIMIT),
        cost_estimate=pl.CostEstimate(
            flops=1, bytes_accessed=1, transcendentals=0
        ),
        name="attend",
    )(starts, *operands)


def attend_back_kernel(ends, aug_ref, k_ref, v_ref, *refs, heads, head_dim, parity):
    step = 2 * pl.program_id(0) + parity
    length = aug_ref.shape[1]
    unit = heads * head_dim
    if parity == 0:
        g_ref, even_ref, odd_ref, kv_ref, g_out_ref, dq_ref, dk_ref, dv_ref = refs
        gaug_ref = g_out_ref
    else:
        gaug_ref, dq_in_ref, scale_ref, all_ref, dq_ref, dk_ref, dv_ref = refs

    def cols(h):
        return pl.ds(h * LANES, LANES)

    def own(h):
        return slice(h * head_dim, (h + 1) * head_dim)

    @pl.when(step == parity)
    def _():
        dq_ref[...] = jnp.zeros_like(dq_ref)
        if parity == 0:
            index = lax.broadcasted_iota(jnp.int32, (LANES - head_dim, 1), 0)

            @pl.loop(0, length // TILE // 2)
            def _(n):
                for part, o_ref in enumerate((even_ref, odd_ref)):
                    rows = at(2 * n + part)
                    g = g_ref[n, :, part * TILE : (part + 1) * TILE]
                    product = g.astype(F32) * o_ref[n].astype(F32)
                    for h in range(heads):
                        delta = -jnp.sum(product[own(h)], axis=0, keepdims=True)
                        gaug_ref[h * LANES : h * LANES + head_dim, rows] = g[own(h)]
                        gaug_ref[h * LANES + head_dim : (h + 1) * LANES, rows] = jnp.where(
                            index < PARTS, spread(delta, index, 0), 0.0
                        ).astype(BF16)

    dk_ref[...] = jnp.zeros_like(dk_ref)
    dv_ref[...] = jnp.zeros_like(dv_ref)
    keys = [k_ref[:, cols(h)] for h in range(heads)]
    turned = [jnp.transpose(k.astype(F32)).astype(BF16) for k in keys]

    def one(block, masked):
        for h in range(heads):
            q = aug_ref[cols(h), at(block)]
            g = gaug_ref[cols(h), at(block)]
            s = dot_nn(keys[h], q)
            if masked:
                key = lax.broadcasted_iota(jnp.int32, (TILE, TILE), 0)
                query = lax.broadcasted_iota(jnp.int32, (TILE, TILE), 1)
                s = jnp.where(key <= query, s, -BIG)
            p = jnp.exp(s)
            d = dot_nn(v_ref[:, cols(h)], g)
            dv_ref[:, cols(h)] += dot_nt(p.astype(BF16), g)
            ds = (p * d).astype(BF16)
            dk_ref[:, cols(h)] += dot_nt(ds, q)
            dq_ref[cols(h), at(block)] += dot_nn(turned[h], ds)

    one(step, True)

    @pl.loop(step + 1, ends[step])
    def _(block):
        one(block, False)

    pieces = []
    for ref in (dk_ref, dv_ref):
        for h in range(heads):
            pieces.append(jnp.transpose(ref[:, cols(h)])[:head_dim].astype(BF16))
    if parity == 0:
        for n, piece in enumerate(pieces):
            kv_ref[0, n * head_dim : (n + 1) * head_dim, :] = piece
    else:
        for n, piece in enumerate(pieces):
            all_ref[0, 2 * unit + n * head_dim : 2 * unit + (n + 1) * head_dim, :] = piece
        for part in range(2):
            rows = at(step - 1 + part)
            for h in range(heads):
                dq = (dq_in_ref[cols(h), rows] + dq_ref[cols(h), rows]).astype(BF16).astype(F32)
                all_ref[0, part * unit + h * head_dim : part * unit + (h + 1) * head_dim, :] = (
                    dq * scale_ref[...]
                )[:head_dim].astype(BF16)


def attend_back(ends, aug, k, v, others, parity, heads, head_dim):
    width, length = aug.shape
    steps = length // TILE // 2
    unit = heads * head_dim
    whole = lambda *shape: pl.BlockSpec(shape, lambda n, st: (0,) * len(shape))
    row = pl.BlockSpec((TILE, width), lambda n, st: (2 * n + parity, 0))
    out = lambda rows: pl.BlockSpec((1, rows, TILE), lambda n, st: (n, 0, 0))
    scratch = [pltpu.VMEM((TILE, width), F32)] * 2
    if parity == 0:
        in_specs = [whole(*value.shape) for value in others]
        out_shape = [
            jax.ShapeDtypeStruct((steps, 2 * unit, TILE), BF16),
            jax.ShapeDtypeStruct((width, length), BF16),
            jax.ShapeDtypeStruct((width, length), F32),
        ]
        out_specs = [out(2 * unit), whole(width, length), whole(width, length)]
    else:
        in_specs = [whole(*value.shape) for value in others]
        out_shape = jax.ShapeDtypeStruct((steps, 4 * unit, TILE), BF16)
        out_specs = out(4 * unit)
        scratch = [pltpu.VMEM((width, length), F32)] + scratch
    return pl.pallas_call(
        functools.partial(attend_back_kernel, heads=heads, head_dim=head_dim, parity=parity),
        out_shape=out_shape,
        grid_spec=pltpu.PrefetchScalarGridSpec(
            num_scalar_prefetch=1,
            grid=(steps,),
            in_specs=[whole(width, length), row, row, *in_specs],
            out_specs=out_specs,
            scratch_shapes=scratch,
        ),
        compiler_params=pltpu.CompilerParams(vmem_limit_bytes=VMEM_LIMIT),
        cost_estimate=pl.CostEstimate(
            flops=1, bytes_accessed=1, transcendentals=0
        ),
        name="attend_back",
    )(ends, aug, k, v, *others)


def project_back_kernel(
    rest_ref, even_ref, w_ref, up_ref, narrow_ref, x_ref, middle_ref, gain_ref, in_ref, down_ref, grad_up_ref, sum_ref, thin_ref
):
    step = pl.program_id(0)
    unit = even_ref.shape[1] // 2

    @pl.when(step == 0)
    def _():
        sum_ref[...] = jnp.zeros_like(sum_ref)
        thin_ref[...] = jnp.zeros_like(thin_ref)

    odd = rest_ref[0, unit:, :]
    even = jnp.concatenate([rest_ref[0, :unit, :], even_ref[0]], axis=0)
    grad_up = None
    for n, joined in enumerate((even, odd)):
        part = slice(n * TILE, (n + 1) * TILE)
        sum_ref[part, :] += dot_tn(joined, w_ref[0])
        thin_ref[:, part] += dot_nn(up_ref[0], joined)
        term = dot_nt(narrow_ref[:, part], joined)
        grad_up = term if grad_up is None else grad_up + term
    grad_up_ref[0] = grad_up

    @pl.when(step == pl.num_programs(0) - 1)
    def _():
        down = None
        for n in range(2):
            part = slice(n * TILE, (n + 1) * TILE)
            x = x_ref[part, :].astype(F32)
            scale = lax.rsqrt(jnp.mean(x * x, axis=-1, keepdims=True) + EPSILON)
            normed = (x * scale * gain_ref[...]).astype(BF16)
            grad = sum_ref[part, :] * gain_ref[...]
            mean = jnp.mean(grad * x, axis=-1, keepdims=True)
            in_ref[part, :] = (
                middle_ref[part, :] + scale * grad - x * (scale * scale * scale) * mean
            ).astype(BF16)
            term = dot_nn(thin_ref[:, part].astype(BF16), normed)
            down = term if down is None else down + term
        down_ref[...] = down


def project_back(rest, even, weight, up, narrow_turned, x, grad_middle, gain):
    blocks, columns, model = weight.shape
    rank, rows = narrow_turned.shape
    each = lambda value: pl.BlockSpec((1, *value.shape[1:]), lambda n: (n, 0, 0))
    fixed = lambda shape: pl.BlockSpec(shape, lambda n: (0,) * len(shape))
    return pl.pallas_call(
        project_back_kernel,
        out_shape=[
            jax.ShapeDtypeStruct((rows, model), BF16),
            jax.ShapeDtypeStruct((rank, model), F32),
            jax.ShapeDtypeStruct((blocks, rank, columns), F32),
        ],
        grid=(blocks,),
        in_specs=[
            each(rest),
            each(even),
            each(weight),
            each(up),
            fixed((rank, rows)),
            fixed((rows, model)),
            fixed((rows, model)),
            fixed((1, model)),
        ],
        out_specs=[
            fixed((rows, model)),
            fixed((rank, model)),
            pl.BlockSpec((1, rank, columns), lambda n: (n, 0, 0)),
        ],
        scratch_shapes=[pltpu.VMEM((rows, model), F32), pltpu.VMEM((rank, rows), F32)],
        compiler_params=pltpu.CompilerParams(vmem_limit_bytes=VMEM_LIMIT),
        cost_estimate=pl.CostEstimate(flops=1, bytes_accessed=1, transcendentals=0),
        name="project_back",
    )(rest, even, weight, up, narrow_turned, x, grad_middle, gain)


def rms_scale(values):
    return lax.rsqrt(jnp.mean(values * values, axis=-1, keepdims=True) + EPSILON)


def rms_back(values, scale_rows, grad_normed):
    cubed = scale_rows * scale_rows * scale_rows
    return scale_rows * grad_normed - values * cubed * jnp.mean(
        grad_normed * values, axis=-1, keepdims=True
    )


def after(value, *others):
    return lax.optimization_barrier((value, others))[0]


def together(*values):
    return lax.optimization_barrier(values)


def own_and_sent(value, own, masks):
    return [
        piece_of(value, own) if m == 0 else xor_permute(piece_of(value, own ^ m), "sp", m) for m in masks
    ]


def in_order(pieces, own):
    stacked = jnp.stack(pieces)
    return jnp.stack([piece_of(stacked, n ^ own) for n in range(len(pieces))], axis=0)


def shares_of_all(table, n_fs):
    to = lambda value, mask: xor_permute(value, "fs", mask)
    if n_fs != 8 or table.shape[0] % 2:
        return [table] + [to(table, m) for m in range(1, n_fs)]
    half = table.shape[0] // 2
    y, x, core = to(table, 4), to(table, 2), to(table, 1)
    top, bottom, core_y, core_x = to(y[:half], 2), to(x[half:], 4), to(y, 1), to(x, 1)
    both = jnp.concatenate([top, bottom], axis=0)
    return [table, core, x, core_x, y, core_y, both, to(both, 1)]


def over_sequences(part, groups, n_sp):
    mask = groups
    while mask < n_sp:
        part = part + xor_permute(part, "sp", mask)
        mask <<= 1
    return [part] + [xor_permute(part, "sp", m) for m in range(1, groups)]


def fold(pieces, adapter_index, adapters, own):
    by_seq = in_order(pieces, own)
    tables = []
    for a in range(adapters):
        table = jnp.zeros_like(pieces[0])
        for s in range(len(pieces)):
            table = table + jnp.where(adapter_index[s, 0] == a, by_seq[s], 0.0)
        tables.append(table)
    return jnp.stack(tables)


def joined_rows(every):
    n, adapters, rows, model = every.shape
    return jnp.swapaxes(every, 0, 1).reshape(adapters, n * rows, model)


def local(
    layer_input,
    output_grad,
    segment_ids,
    adapter_index,
    gain_attention,
    gain_feedforward,
    query_scale,
    weight_qkv,
    weight_mixer,
    weight_expand,
    weight_contract,
    qkv_down,
    qkv_up,
    mixer_down,
    mixer_up,
    expand_down,
    expand_up,
    contract_down,
    contract_up,
):
    sequences, tokens, model = layer_input.shape
    head_dim = query_scale.shape[0]
    n_fs, n_sp = lax.axis_size("fs"), lax.axis_size("sp")
    adapters, rank = qkv_down.shape[0], qkv_down.shape[2]
    length = segment_ids.shape[1]
    folds = n_sp // sequences
    heads = model // head_dim // n_fs
    unit = heads * head_dim
    width = heads * LANES
    rows = sequences * tokens
    fs = lax.axis_index("fs")
    sp = lax.axis_index("sp")
    own = sp % sequences
    fold_of = sp // sequences

    pick = piece_of(adapter_index, own)[0]
    downs = [piece_of(t, pick) for t in (qkv_down, mixer_down, expand_down, contract_down)]
    ups = [piece_of(t, pick) for t in (qkv_up, mixer_up, expand_up, contract_up)]

    def merged(weight, down, up):
        cols = weight.shape[1]
        own_up = lax.dynamic_slice_in_dim(up, fs * cols, cols, 1)
        return (weight.astype(F32) + dot_nn(down, own_up)).astype(BF16)

    shard = merged(weight_qkv, downs[0], ups[0])
    inverse = pow(3, -1, n_fs)
    received = [
        lax.ppermute(
            shard[:, t * unit : (t + 1) * unit], "fs", [(d, (3 * d + t) % n_fs) for d in range(n_fs)]
        )
        for t in range(3)
    ]
    places = [(3 * ((inverse * (fs - t)) % n_fs) + t) // n_fs for t in range(3)]
    w_parts = []
    for b in range(3):
        part = jnp.zeros_like(received[0])
        for t in range(3):
            part = jnp.where(places[t] == b, received[t], part)
        w_parts.append(part)
    w_own = jnp.concatenate(w_parts, axis=1)
    w_padded = jnp.pad(
        w_own.reshape(model, 3 * heads, head_dim), ((0, 0), (0, 0), (0, LANES - head_dim))
    ).reshape(model, 3 * width)

    segs = piece_of(segment_ids, own)
    scale = query_scale * (1.0 / math.sqrt(head_dim))
    scale_pad = jnp.pad(scale, (0, LANES - head_dim))[None]
    col_scale = jnp.concatenate([jnp.tile(scale_pad, (1, heads)), jnp.ones((1, 2 * width), F32)], axis=1)
    lane = jnp.arange(LANES)[None, :]
    marks = lane >= head_dim + PARTS
    same = lane == segs[:, None] + (head_dim + PARTS)
    qpad = same.astype(BF16)
    kpad = jnp.where(
        marks, jnp.where(same, 0.0, -BIG), jnp.where(lane >= head_dim, 1.0, 0.0)
    ).astype(BF16)

    project_args = (gain_attention[None], w_padded, col_scale, qpad, kpad)
    as_table = lambda *s: jnp.stack(s).astype(jnp.int32)
    if n_fs == 8 and folds == 1 and sequences == 4 and 2 * tokens == TILE:
        pieces = own_and_sent(layer_input, own, (0, 1))
        pieces += own_and_sent(layer_input, own, (2, 3))
        odd = own % 2 == 1
        upper = own // 2

        def pair(low, high):
            return jnp.where(odd, jnp.concatenate([high, low], 0), jnp.concatenate([low, high], 0))

        def to(value, mask):
            return xor_permute(value, "fs", mask)

        def fill(blocks, place, earlier):
            sources = [block for _, block in blocks]
            tiles = as_table(*[(fs ^ mask) * 2 + place for mask, _ in blocks])
            return project(sources, tiles, *project_args, earlier, heads, head_dim, length)

        other = 1 - upper
        first = pair(pieces[0], pieces[1])
        half = TILE // 2
        sent = after(first, *received)
        y1, x1, c1 = to(sent, 4), to(sent, 2), to(sent, 1)
        y1, x1, c1 = together(y1, x1, c1)
        top1, bottom1, cy1, cx1 = to(y1[:half], 2), to(x1[half:], 4), to(y1, 1), to(x1, 1)
        qkv = fill([(0, first), (1, c1), (4, y1), (2, x1)], upper, None)
        *qkv, top1, bottom1, cy1, cx1, p2, p3 = together(*qkv, top1, bottom1, cy1, cx1, pieces[2], pieces[3])
        both1 = jnp.concatenate([top1, bottom1], axis=0)
        second = pair(p2, p3)
        y2, x2, c2, cb1 = to(second, 4), to(second, 2), to(second, 1), to(both1, 1)
        qkv = fill([(5, cy1), (3, cx1)], upper, qkv)
        *qkv, y2, x2, c2, cb1 = together(*qkv, y2, x2, c2, cb1)
        top2, bottom2, cy2, cx2 = to(y2[:half], 2), to(x2[half:], 4), to(y2, 1), to(x2, 1)
        qkv = fill([(6, both1), (7, cb1)], upper, qkv)
        qkv = fill([(0, second), (1, c2)], other, qkv)
        *qkv, top2, bottom2, cy2, cx2 = together(*qkv, top2, bottom2, cy2, cx2)
        both2 = jnp.concatenate([top2, bottom2], axis=0)
        cb2 = to(both2, 1)
        qkv = fill([(4, y2), (2, x2), (5, cy2), (3, cx2)], other, qkv)
        *qkv, cb2 = together(*qkv, cb2)
        qkv = fill([(6, both2), (7, cb2)], other, qkv)
        x_own = jnp.where(
            upper == 0, jnp.concatenate([first, second], 0), jnp.concatenate([second, first], 0)
        )
        x_sent, x_here = (p2, p3), (both2,)
    else:
        pieces = own_and_sent(layer_input, own, range(sequences))
        x_own = in_order(pieces, own).reshape(rows, model)
        gathered = lax.all_gather(x_own, ("fs", "sp"), axis=0)
        gathered = gathered.reshape(n_fs, folds, sequences, rows, model)
        gathered = lax.dynamic_index_in_dim(gathered, own, 2, keepdims=False)
        blocks = gathered.reshape(n_fs * folds, rows, model)
        tiles = jnp.arange(length // TILE, dtype=jnp.int32)
        qkv = project([blocks], tiles, *project_args, None, heads, head_dim, length)
        x_sent, x_here = (x_own,), (blocks,)
    q, k, v = qkv

    three = jnp.stack(
        [
            merged(w, d, u).T
            for w, d, u in zip((weight_mixer, weight_expand, weight_contract), downs[1:], ups[1:])
        ]
    )
    w_mixer, w_expand, w_contract = lax.all_gather(after(three, *x_here), "fs", axis=1, tiled=True)
    g_pieces = own_and_sent(after(output_grad, *x_sent), own, range(sequences))

    firsts, lasts = segs[::TILE], segs[TILE - 1 :: TILE]
    starts = jnp.sum(segs[None, :] < firsts[:, None], axis=1, dtype=jnp.int32) // TILE
    ends = (jnp.sum(segs[None, :] <= lasts[:, None], axis=1, dtype=jnp.int32) + TILE - 1) // TILE

    def sections_out(value):
        if folds > 1:
            cut = value.reshape(n_fs, folds, *value.shape[1:])
            value = lax.dynamic_index_in_dim(cut, fold_of, 1, keepdims=False)
        return lax.all_to_all(value, "fs", split_axis=0, concat_axis=0, tiled=True)

    o_even, aug = attend(starts, q, k, v, None, 0, heads, head_dim)
    a_even = sections_out(o_even)
    o_odd, aug = attend(starts, q, k, v, aug, 1, heads, head_dim)
    o_odd, a_even, g_pieces = together(o_odd, a_even, g_pieces)
    a_odd = sections_out(o_odd)
    attended = jnp.concatenate([a_even, a_odd], axis=2).reshape(model, rows)
    g_own = in_order(g_pieces, own).reshape(rows, model)

    x_f = x_own.astype(F32)
    scale_one = rms_scale(x_f)
    normed_one = (x_f * scale_one * gain_attention).astype(BF16)
    narrow = lambda u, down: dot_nn(u, down).astype(BF16)
    mixer = lax.dot_general(attended, w_mixer, (((0,), (1,)), ((), ())), preferred_element_type=F32)
    middle = x_f + mixer
    scale_two = rms_scale(middle)
    normed_two = (middle * scale_two * gain_feedforward).astype(BF16)
    expanded = dot_nt(normed_two, w_expand)
    gate = jax.nn.sigmoid(expanded)
    hidden = (expanded * gate).astype(BF16)
    contracted = dot_nt(hidden, w_contract)
    layer_output = (middle + contracted).astype(BF16).reshape(sequences, tokens, model)

    def adapter_back(u, grad, down, up):
        grad_up = dot_tn(narrow(u, down), grad)
        grad_narrow = dot_nt(grad, up).astype(BF16)
        return [dot_tn(grad_narrow, u), grad_up]

    grad_hidden = dot_nn(g_own, w_contract)
    grad_expanded = (grad_hidden * gate * (1.0 + expanded * (1.0 - gate))).astype(BF16)
    grad_normed_two = dot_nn(grad_expanded, w_expand)
    grad_middle = g_own.astype(F32) + rms_back(middle, scale_two, grad_normed_two * gain_feedforward)
    grad_mixer = grad_middle.astype(BF16)
    grad_attended = lax.dot_general(w_mixer, grad_mixer, (((0,), (1,)), ((), ())), preferred_element_type=F32)
    grad_heads = lax.all_to_all(
        grad_attended.astype(BF16).reshape(n_fs, unit, rows), "fs", split_axis=0, concat_axis=0, tiled=True
    )
    if folds > 1:
        every = lax.all_gather(grad_heads, "sp", axis=0)
        every = every.reshape(folds, sequences, n_fs, unit, rows)
        every = lax.dynamic_index_in_dim(every, own, 1, keepdims=False)
        grad_heads = jnp.swapaxes(every, 0, 1).reshape(n_fs * folds, unit, rows)

    narrow_mixer = dot_tn(attended, downs[1]).astype(BF16)
    early = jnp.concatenate(
        [
            lax.dot_general(
                dot_nt(grad_mixer, ups[1]).astype(BF16), attended, (((0,), (1,)), ((), ())), preferred_element_type=F32
            ),
            dot_tn(narrow_mixer, grad_mixer),
            *adapter_back(normed_two, grad_expanded, downs[2], ups[2]),
            *adapter_back(hidden, g_own, downs[3], ups[3]),
        ],
        axis=0,
    )
    grad_heads, early, layer_output = together(grad_heads, early, layer_output)
    w_all = lax.all_gather(after(w_own.T, attended), "fs", axis=0)
    early = lax.all_to_all(
        early.reshape(n_fs, early.shape[0] // n_fs, model), "fs", split_axis=0, concat_axis=0, tiled=True
    )

    kv_even, g_aug, dq = attend_back(ends, aug, k, v, (grad_heads, o_even, o_odd), 0, heads, head_dim)
    kv_even, g_aug, dq, early = together(kv_even, g_aug, dq, early)
    kv_even = sections_out(kv_even)
    early = jnp.sum(early, axis=0)
    grads_odd = attend_back(ends, aug, k, v, (g_aug, dq, scale_pad.T), 1, heads, head_dim)
    grads_odd, kv_even, early, w_all = together(grads_odd, kv_even, early, w_all)
    out_pieces = own_and_sent(after(layer_output, grads_odd), own, range(sequences))
    grads_odd = sections_out(grads_odd)
    grads_odd, out_pieces = together(grads_odd, out_pieces)
    layer_output = in_order(out_pieces, own)

    up_all = (
        ups[0].reshape(rank, 3, n_fs, unit).transpose(2, 0, 1, 3).reshape(n_fs, rank, 3 * unit)
    )
    narrow_turned = lax.dot_general(
        downs[0], normed_one, (((0,), (1,)), ((), ())), preferred_element_type=F32
    ).astype(BF16)
    input_grad, grad_down, grad_up = project_back(
        grads_odd, kv_even, w_all, up_all, narrow_turned, x_own, grad_middle, gain_attention[None]
    )
    input_grad = input_grad.reshape(sequences, tokens, model)
    grad_up = grad_up.reshape(n_fs, rank, 3, unit).transpose(1, 2, 0, 3).reshape(3 * rank, model)
    late = jnp.concatenate([grad_down, grad_up], axis=0)
    split = late.reshape(n_fs, late.shape[0] // n_fs, model)
    late = [
        piece_of(split, fs) if m == 0 else xor_permute(piece_of(split, fs ^ m), "fs", m) for m in range(n_fs)
    ]
    if folds == 1:
        input_grad = lax.all_to_all(input_grad, "sp", split_axis=0, concat_axis=0, tiled=True)
    else:
        input_grad = in_order(own_and_sent(input_grad, own, range(sequences)), own)
    part = jnp.concatenate([sum(late[1:], late[0]), early], axis=0)
    part = over_sequences(part, sequences, n_sp)
    part, input_grad = together(part, input_grad)
    table = shares_of_all(fold(part, adapter_index, adapters, own), n_fs)
    table = in_order(table, fs)

    factor = 1.0 / math.sqrt(length)
    outs = []
    late_rows = late[0].shape[0]
    late = joined_rows(table[:, :, :late_rows]) * factor
    early = joined_rows(table[:, :, late_rows:]) * factor
    for tables, wides in ((late, (3,)), (early, (1, 1, 1))):
        first = 0
        for wide in wides:
            outs.append(jnp.swapaxes(tables[:, first : first + rank], 1, 2))
            first += rank
            outs.append(tables[:, first : first + rank * wide].reshape(adapters, rank, wide * model))
            first += rank * wide
    return (layer_output, input_grad, *outs)


def solution(mesh):
    tokens = P(None, ("fs", "sp"), None)
    in_specs = (tokens, tokens) + (P(),) * 5 + (P(None, "fs"),) * 4 + (P(),) * 8
    out_specs = (tokens, tokens) + (P(),) * 8
    return jax.shard_map(local, mesh=mesh, in_specs=in_specs, out_specs=out_specs, check_vma=False)
```

```python
import functools
import math

import jax
import jax.numpy as jnp
from jax import lax
from jax.experimental import pallas as pl
from jax.experimental.pallas import tpu as pltpu
from jax.sharding import PartitionSpec as P

EPSILON = 1e-06
BIG = 1e30
LANES = 128
PARTS = 3
TILE = 256
VMEM_LIMIT = 64000000
F32 = jnp.float32
BF16 = jnp.bfloat16
NT = (((1,), (1,)), ((), ()))
TN = (((0,), (0,)), ((), ()))


def dot_nn(a, b):
    return jnp.dot(a, b, preferred_element_type=F32)


def dot_nt(a, b):
    return lax.dot_general(a, b, NT, preferred_element_type=F32)


def dot_tn(a, b):
    return lax.dot_general(a, b, TN, preferred_element_type=F32)


def xor_permute(value, axis, mask):
    count = lax.axis_size(axis)
    return lax.ppermute(value, axis, [(a, a ^ mask) for a in range(count)])


def piece_of(stacked, index):
    return lax.dynamic_index_in_dim(stacked, index, 0, keepdims=False)


def project_kernel(tiles, *refs, count, heads, head_dim):
    x_refs, (gain_ref, w_ref, scale_ref, qpad_ref, kpad_ref) = refs[:count], refs[count : count + 5]
    q_ref, k_ref, v_ref, x_ref = refs[-4:]
    if count > 1:
        for n in range(count):

            @pl.when(pl.program_id(0) == n)
            def _():
                x_ref[...] = x_refs[n][...]

        x = x_ref[...].astype(F32)
    else:
        x = x_refs[0][0].astype(F32)
    mean = jnp.mean(x * x, axis=-1, keepdims=True)
    normed = (x * lax.rsqrt(mean + EPSILON) * gain_ref[...]).astype(BF16)
    rows = dot_nn(normed, w_ref[...]) * scale_ref[...]
    width = heads * LANES
    lane = lax.broadcasted_iota(jnp.int32, (1, width), 1) % LANES
    q_ref[...] = (rows[:, :width] + jnp.tile(qpad_ref[...].astype(F32), (1, heads))).astype(BF16)
    k_ref[...] = (rows[:, width : 2 * width] + jnp.tile(kpad_ref[...].astype(F32), (1, heads))).astype(BF16)
    ones = jnp.where((lane >= head_dim) & (lane < head_dim + PARTS), 1.0, 0.0)
    v_ref[...] = (rows[:, 2 * width :] + ones).astype(BF16)


def project(sources, tiles, gain, weight, scale, qpad, kpad, earlier, heads, head_dim, length):
    model = weight.shape[0]
    step = TILE
    count = len(sources)
    steps = tiles.shape[0]
    width = heads * LANES
    out = pl.BlockSpec((step, width), lambda n, t: (t[n], 0))
    pad = pl.BlockSpec((step, LANES), lambda n, t: (t[n], 0))
    fixed = lambda shape: pl.BlockSpec(shape, lambda n, t: (0,) * len(shape))
    if count > 1:
        in_specs = [fixed((step, model))] * count
    else:
        per = sources[0].shape[1] // step
        in_specs = [pl.BlockSpec((1, step, model), lambda n, t: (n // per, n % per, 0))]
    in_specs += [fixed((1, model)), fixed((model, 3 * width)), fixed((1, 3 * width)), pad, pad]
    operands = [*sources, gain, weight, scale, qpad, kpad]
    aliases = {}
    if earlier is not None:
        in_specs += [pl.BlockSpec(memory_space=pl.ANY)] * 3
        aliases = {1 + len(operands) + n: n for n in range(3)}
        operands += list(earlier)
    return pl.pallas_call(
        functools.partial(project_kernel, count=count, heads=heads, head_dim=head_dim),
        out_shape=[jax.ShapeDtypeStruct((length, width), BF16)] * 3,
        grid_spec=pltpu.PrefetchScalarGridSpec(
            num_scalar_prefetch=1,
            grid=(steps,),
            in_specs=in_specs,
            out_specs=[out] * 3,
            scratch_shapes=[pltpu.VMEM((step, model), BF16)],
        ),
        input_output_aliases=aliases,
        compiler_params=pltpu.CompilerParams(vmem_limit_bytes=VMEM_LIMIT),
        cost_estimate=pl.CostEstimate(
            flops=1,
            bytes_accessed=1,
            transcendentals=0,
        ),
        name="project",
    )(tiles, *operands)


def spread(row, index, first):
    high = row.astype(BF16).astype(F32)
    middle = (row - high).astype(BF16).astype(F32)
    last = row - high - middle
    return jnp.where(index == first, high, jnp.where(index == first + 1, middle, last))


def at(block):
    return pl.ds(pl.multiple_of(block * TILE, TILE), TILE)


def attend_kernel(starts, q_ref, k_ref, v_ref, *refs, heads, head_dim, parity):
    o_ref, aug_ref = refs[-2:]
    step = 2 * pl.program_id(0) + parity
    first = starts[step]
    index = lax.broadcasted_iota(jnp.int32, (LANES, 1), 0)
    marks = (index >= head_dim) & (index < head_dim + PARTS)

    def cols(h):
        return pl.ds(h * LANES, LANES)

    turned = [jnp.transpose(q_ref[:, cols(h)].astype(F32)) for h in range(heads)]
    queries = [t.astype(BF16) for t in turned]

    def one(block, carry, masked):
        scores = [dot_nn(k_ref[at(block), cols(h)], queries[h]) for h in range(heads)]
        out = []
        for h, s in enumerate(scores):
            if masked:
                key = lax.broadcasted_iota(jnp.int32, (TILE, TILE), 0)
                query = lax.broadcasted_iota(jnp.int32, (TILE, TILE), 1)
                s = jnp.where(key <= query, s, -BIG)
            peak = jnp.max(s, axis=0, keepdims=True)
            if not masked:
                peak = jnp.maximum(carry[h][0], peak)
            p = jnp.exp(s - peak).astype(BF16)
            total = dot_tn(v_ref[at(block), cols(h)], p)
            if not masked:
                total = carry[h][1] * jnp.exp(carry[h][0] - peak) + total
            out.append((peak, total))
        return tuple(out)

    carry = one(step, None, True)
    carry = lax.fori_loop(first, step, lambda block, c: one(block, c, False), carry)
    for h in range(heads):
        peak, total = carry[h]
        weight = total[head_dim : head_dim + 1]
        o_ref[0, h * head_dim : (h + 1) * head_dim, :] = (total / weight)[:head_dim].astype(BF16)
        lse = -(peak + jnp.log(weight))
        aug_ref[cols(h), :] = jnp.where(marks, spread(lse, index, head_dim), turned[h]).astype(BF16)


def attend(starts, q, k, v, earlier, parity, heads, head_dim):
    length, width = q.shape
    steps = length // TILE // 2
    whole = pl.BlockSpec((length, width), lambda n, st: (0, 0))
    in_specs = [pl.BlockSpec((TILE, width), lambda n, st: (2 * n + parity, 0)), whole, whole]
    operands = [q, k, v]
    aliases = {}
    if earlier is not None:
        in_specs.append(pl.BlockSpec(memory_space=pl.ANY))
        operands.append(earlier)
        aliases = {4: 1}
    return pl.pallas_call(
        functools.partial(attend_kernel, heads=heads, head_dim=head_dim, parity=parity),
        out_shape=[
            jax.ShapeDtypeStruct((steps, heads * head_dim, TILE), BF16),
            jax.ShapeDtypeStruct((width, length), BF16),
        ],
        grid_spec=pltpu.PrefetchScalarGridSpec(
            num_scalar_prefetch=1,
            grid=(steps,),
            in_specs=in_specs,
            out_specs=[
                pl.BlockSpec((1, heads * head_dim, TILE), lambda n, st: (n, 0, 0)),
                pl.BlockSpec((width, TILE), lambda n, st: (0, 2 * n + parity)),
            ],
        ),
        input_output_aliases=aliases,
        compiler_params=pltpu.CompilerParams(vmem_limit_bytes=VMEM_LIMIT),
        cost_estimate=pl.CostEstimate(
            flops=1, bytes_accessed=1, transcendentals=0
        ),
        name="attend",
    )(starts, *operands)


def attend_back_kernel(ends, aug_ref, k_ref, v_ref, *refs, heads, head_dim, parity):
    step = 2 * pl.program_id(0) + parity
    length = aug_ref.shape[1]
    unit = heads * head_dim
    if parity == 0:
        g_ref, even_ref, odd_ref, kv_ref, g_out_ref, dq_ref, dk_ref, dv_ref = refs
        gaug_ref = g_out_ref
    else:
        gaug_ref, dq_in_ref, scale_ref, all_ref, dq_ref, dk_ref, dv_ref = refs

    def cols(h):
        return pl.ds(h * LANES, LANES)

    def own(h):
        return slice(h * head_dim, (h + 1) * head_dim)

    @pl.when(step == parity)
    def _():
        dq_ref[...] = jnp.zeros_like(dq_ref)
        if parity == 0:
            index = lax.broadcasted_iota(jnp.int32, (LANES - head_dim, 1), 0)

            @pl.loop(0, length // TILE // 2)
            def _(n):
                for part, o_ref in enumerate((even_ref, odd_ref)):
                    rows = at(2 * n + part)
                    g = g_ref[n, :, part * TILE : (part + 1) * TILE]
                    product = g.astype(F32) * o_ref[n].astype(F32)
                    for h in range(heads):
                        delta = -jnp.sum(product[own(h)], axis=0, keepdims=True)
                        gaug_ref[h * LANES : h * LANES + head_dim, rows] = g[own(h)]
                        gaug_ref[h * LANES + head_dim : (h + 1) * LANES, rows] = jnp.where(
                            index < PARTS, spread(delta, index, 0), 0.0
                        ).astype(BF16)

    dk_ref[...] = jnp.zeros_like(dk_ref)
    dv_ref[...] = jnp.zeros_like(dv_ref)
    keys = [k_ref[:, cols(h)] for h in range(heads)]
    turned = [jnp.transpose(k.astype(F32)).astype(BF16) for k in keys]

    def one(block, masked):
        for h in range(heads):
            q = aug_ref[cols(h), at(block)]
            g = gaug_ref[cols(h), at(block)]
            s = dot_nn(keys[h], q)
            if masked:
                key = lax.broadcasted_iota(jnp.int32, (TILE, TILE), 0)
                query = lax.broadcasted_iota(jnp.int32, (TILE, TILE), 1)
                s = jnp.where(key <= query, s, -BIG)
            p = jnp.exp(s)
            d = dot_nn(v_ref[:, cols(h)], g)
            dv_ref[:, cols(h)] += dot_nt(p.astype(BF16), g)
            ds = (p * d).astype(BF16)
            dk_ref[:, cols(h)] += dot_nt(ds, q)
            dq_ref[cols(h), at(block)] += dot_nn(turned[h], ds)

    one(step, True)

    @pl.loop(step + 1, ends[step])
    def _(block):
        one(block, False)

    pieces = []
    for ref in (dk_ref, dv_ref):
        for h in range(heads):
            pieces.append(jnp.transpose(ref[:, cols(h)])[:head_dim].astype(BF16))
    if parity == 0:
        for n, piece in enumerate(pieces):
            kv_ref[0, n * head_dim : (n + 1) * head_dim, :] = piece
    else:
        for n, piece in enumerate(pieces):
            all_ref[0, 2 * unit + n * head_dim : 2 * unit + (n + 1) * head_dim, :] = piece
        for part in range(2):
            rows = at(step - 1 + part)
            for h in range(heads):
                dq = (dq_in_ref[cols(h), rows] + dq_ref[cols(h), rows]).astype(BF16).astype(F32)
                all_ref[0, part * unit + h * head_dim : part * unit + (h + 1) * head_dim, :] = (
                    dq * scale_ref[...]
                )[:head_dim].astype(BF16)


def attend_back(ends, aug, k, v, others, parity, heads, head_dim):
    width, length = aug.shape
    steps = length // TILE // 2
    unit = heads * head_dim
    whole = lambda *shape: pl.BlockSpec(shape, lambda n, st: (0,) * len(shape))
    row = pl.BlockSpec((TILE, width), lambda n, st: (2 * n + parity, 0))
    out = lambda rows: pl.BlockSpec((1, rows, TILE), lambda n, st: (n, 0, 0))
    scratch = [pltpu.VMEM((TILE, width), F32)] * 2
    if parity == 0:
        in_specs = [whole(*value.shape) for value in others]
        out_shape = [
            jax.ShapeDtypeStruct((steps, 2 * unit, TILE), BF16),
            jax.ShapeDtypeStruct((width, length), BF16),
            jax.ShapeDtypeStruct((width, length), F32),
        ]
        out_specs = [out(2 * unit), whole(width, length), whole(width, length)]
    else:
        in_specs = [whole(*value.shape) for value in others]
        out_shape = jax.ShapeDtypeStruct((steps, 4 * unit, TILE), BF16)
        out_specs = out(4 * unit)
        scratch = [pltpu.VMEM((width, length), F32)] + scratch
    return pl.pallas_call(
        functools.partial(attend_back_kernel, heads=heads, head_dim=head_dim, parity=parity),
        out_shape=out_shape,
        grid_spec=pltpu.PrefetchScalarGridSpec(
            num_scalar_prefetch=1,
            grid=(steps,),
            in_specs=[whole(width, length), row, row, *in_specs],
            out_specs=out_specs,
            scratch_shapes=scratch,
        ),
        compiler_params=pltpu.CompilerParams(vmem_limit_bytes=VMEM_LIMIT),
        cost_estimate=pl.CostEstimate(
            flops=1, bytes_accessed=1, transcendentals=0
        ),
        name="attend_back",
    )(ends, aug, k, v, *others)


def project_back_kernel(
    rest_ref, even_ref, w_ref, up_ref, narrow_ref, x_ref, middle_ref, gain_ref, in_ref, down_ref, grad_up_ref, sum_ref, thin_ref
):
    step = pl.program_id(0)
    unit = even_ref.shape[1] // 2

    @pl.when(step == 0)
    def _():
        sum_ref[...] = jnp.zeros_like(sum_ref)
        thin_ref[...] = jnp.zeros_like(thin_ref)

    odd = rest_ref[0, unit:, :]
    even = jnp.concatenate([rest_ref[0, :unit, :], even_ref[0]], axis=0)
    grad_up = None
    for n, joined in enumerate((even, odd)):
        part = slice(n * TILE, (n + 1) * TILE)
        sum_ref[part, :] += dot_tn(joined, w_ref[0])
        thin_ref[:, part] += dot_nn(up_ref[0], joined)
        term = dot_nt(narrow_ref[:, part], joined)
        grad_up = term if grad_up is None else grad_up + term
    grad_up_ref[0] = grad_up

    @pl.when(step == pl.num_programs(0) - 1)
    def _():
        down = None
        for n in range(2):
            part = slice(n * TILE, (n + 1) * TILE)
            x = x_ref[part, :].astype(F32)
            scale = lax.rsqrt(jnp.mean(x * x, axis=-1, keepdims=True) + EPSILON)
            normed = (x * scale * gain_ref[...]).astype(BF16)
            grad = sum_ref[part, :] * gain_ref[...]
            mean = jnp.mean(grad * x, axis=-1, keepdims=True)
            in_ref[part, :] = (
                middle_ref[part, :] + scale * grad - x * (scale * scale * scale) * mean
            ).astype(BF16)
            term = dot_nn(thin_ref[:, part].astype(BF16), normed)
            down = term if down is None else down + term
        down_ref[...] = down


def project_back(rest, even, weight, up, narrow_turned, x, grad_middle, gain):
    blocks, columns, model = weight.shape
    rank, rows = narrow_turned.shape
    each = lambda value: pl.BlockSpec((1, *value.shape[1:]), lambda n: (n, 0, 0))
    fixed = lambda shape: pl.BlockSpec(shape, lambda n: (0,) * len(shape))
    return pl.pallas_call(
        project_back_kernel,
        out_shape=[
            jax.ShapeDtypeStruct((rows, model), BF16),
            jax.ShapeDtypeStruct((rank, model), F32),
            jax.ShapeDtypeStruct((blocks, rank, columns), F32),
        ],
        grid=(blocks,),
        in_specs=[
            each(rest),
            each(even),
            each(weight),
            each(up),
            fixed((rank, rows)),
            fixed((rows, model)),
            fixed((rows, model)),
            fixed((1, model)),
        ],
        out_specs=[
            fixed((rows, model)),
            fixed((rank, model)),
            pl.BlockSpec((1, rank, columns), lambda n: (n, 0, 0)),
        ],
        scratch_shapes=[pltpu.VMEM((rows, model), F32), pltpu.VMEM((rank, rows), F32)],
        compiler_params=pltpu.CompilerParams(vmem_limit_bytes=VMEM_LIMIT),
        cost_estimate=pl.CostEstimate(flops=1, bytes_accessed=1, transcendentals=0),
        name="project_back",
    )(rest, even, weight, up, narrow_turned, x, grad_middle, gain)


def rms_scale(values):
    return lax.rsqrt(jnp.mean(values * values, axis=-1, keepdims=True) + EPSILON)


def rms_back(values, scale_rows, grad_normed):
    cubed = scale_rows * scale_rows * scale_rows
    return scale_rows * grad_normed - values * cubed * jnp.mean(
        grad_normed * values, axis=-1, keepdims=True
    )


def after(value, *others):
    return lax.optimization_barrier((value, others))[0]


def together(*values):
    return lax.optimization_barrier(values)


def own_and_sent(value, own, masks):
    return [
        piece_of(value, own) if m == 0 else xor_permute(piece_of(value, own ^ m), "sp", m) for m in masks
    ]


def in_order(pieces, own):
    stacked = jnp.stack(pieces)
    return jnp.stack([piece_of(stacked, n ^ own) for n in range(len(pieces))], axis=0)


def shares_of_all(table, n_fs, beside):
    to = lambda value, mask: xor_permute(value, "fs", mask)
    if n_fs != 8 or table.shape[0] % 2:
        return [table] + [to(table, m) for m in range(1, n_fs)], beside
    half = table.shape[0] // 2
    y, x, core, beside = together(to(table, 4), to(table, 2), to(table, 1), beside)
    top, bottom, core_y, core_x = to(y[:half], 2), to(x[half:], 4), to(y, 1), to(x, 1)
    both = jnp.concatenate([top, bottom], axis=0)
    return [table, core, x, core_x, y, core_y, both, to(both, 1)], beside


def over_sequences(part, groups, n_sp):
    mask = groups
    while mask < n_sp:
        part = part + xor_permute(part, "sp", mask)
        mask <<= 1
    return [part] + [xor_permute(part, "sp", m) for m in range(1, groups)]


def fold(pieces, adapter_index, adapters, own):
    by_seq = in_order(pieces, own)
    tables = []
    for a in range(adapters):
        table = jnp.zeros_like(pieces[0])
        for s in range(len(pieces)):
            table = table + jnp.where(adapter_index[s, 0] == a, by_seq[s], 0.0)
        tables.append(table)
    return jnp.stack(tables)


def joined_rows(every):
    n, adapters, rows, model = every.shape
    return jnp.swapaxes(every, 0, 1).reshape(adapters, n * rows, model)


def local(
    layer_input,
    output_grad,
    segment_ids,
    adapter_index,
    gain_attention,
    gain_feedforward,
    query_scale,
    weight_qkv,
    weight_mixer,
    weight_expand,
    weight_contract,
    qkv_down,
    qkv_up,
    mixer_down,
    mixer_up,
    expand_down,
    expand_up,
    contract_down,
    contract_up,
):
    sequences, tokens, model = layer_input.shape
    head_dim = query_scale.shape[0]
    n_fs, n_sp = lax.axis_size("fs"), lax.axis_size("sp")
    adapters, rank = qkv_down.shape[0], qkv_down.shape[2]
    length = segment_ids.shape[1]
    folds = n_sp // sequences
    heads = model // head_dim // n_fs
    unit = heads * head_dim
    width = heads * LANES
    rows = sequences * tokens
    fs = lax.axis_index("fs")
    sp = lax.axis_index("sp")
    own = sp % sequences
    fold_of = sp // sequences

    pick = piece_of(adapter_index, own)[0]
    downs = [piece_of(t, pick) for t in (qkv_down, mixer_down, expand_down, contract_down)]
    ups = [piece_of(t, pick) for t in (qkv_up, mixer_up, expand_up, contract_up)]

    def merged(weight, down, up):
        cols = weight.shape[1]
        own_up = lax.dynamic_slice_in_dim(up, fs * cols, cols, 1)
        return (weight.astype(F32) + dot_nn(down, own_up)).astype(BF16)

    shard = merged(weight_qkv, downs[0], ups[0])
    inverse = pow(3, -1, n_fs)
    received = [
        lax.ppermute(
            shard[:, t * unit : (t + 1) * unit], "fs", [(d, (3 * d + t) % n_fs) for d in range(n_fs)]
        )
        for t in range(3)
    ]
    places = [(3 * ((inverse * (fs - t)) % n_fs) + t) // n_fs for t in range(3)]
    w_parts = []
    for b in range(3):
        part = jnp.zeros_like(received[0])
        for t in range(3):
            part = jnp.where(places[t] == b, received[t], part)
        w_parts.append(part)
    w_own = jnp.concatenate(w_parts, axis=1)
    w_padded = jnp.pad(
        w_own.reshape(model, 3 * heads, head_dim), ((0, 0), (0, 0), (0, LANES - head_dim))
    ).reshape(model, 3 * width)

    segs = piece_of(segment_ids, own)
    scale = query_scale * (1.0 / math.sqrt(head_dim))
    scale_pad = jnp.pad(scale, (0, LANES - head_dim))[None]
    col_scale = jnp.concatenate([jnp.tile(scale_pad, (1, heads)), jnp.ones((1, 2 * width), F32)], axis=1)
    lane = jnp.arange(LANES)[None, :]
    marks = lane >= head_dim + PARTS
    same = lane == segs[:, None] + (head_dim + PARTS)
    qpad = same.astype(BF16)
    kpad = jnp.where(
        marks, jnp.where(same, 0.0, -BIG), jnp.where(lane >= head_dim, 1.0, 0.0)
    ).astype(BF16)

    project_args = (gain_attention[None], w_padded, col_scale, qpad, kpad)
    as_table = lambda *s: jnp.stack(s).astype(jnp.int32)
    if n_fs == 8 and folds == 1 and sequences == 4 and 2 * tokens == TILE:
        pieces = own_and_sent(layer_input, own, (0, 1))
        pieces += own_and_sent(layer_input, own, (2, 3))
        odd = own % 2 == 1
        upper = own // 2

        def pair(low, high):
            return jnp.where(odd, jnp.concatenate([high, low], 0), jnp.concatenate([low, high], 0))

        def to(value, mask):
            return xor_permute(value, "fs", mask)

        def fill(blocks, place, earlier):
            sources = [block for _, block in blocks]
            tiles = as_table(*[(fs ^ mask) * 2 + place for mask, _ in blocks])
            return project(sources, tiles, *project_args, earlier, heads, head_dim, length)

        other = 1 - upper
        first = pair(pieces[0], pieces[1])
        half = TILE // 2
        sent = after(first, *received)
        y1, x1, c1 = to(sent, 4), to(sent, 2), to(sent, 1)
        y1, x1, c1, w_padded = together(y1, x1, c1, w_padded)
        project_args = (gain_attention[None], w_padded, col_scale, qpad, kpad)
        top1, bottom1, cy1, cx1 = to(y1[:half], 2), to(x1[half:], 4), to(y1, 1), to(x1, 1)
        qkv = fill([(0, first), (1, c1), (4, y1), (2, x1)], upper, None)
        *qkv, top1, bottom1, cy1, cx1, p2, p3 = together(*qkv, top1, bottom1, cy1, cx1, pieces[2], pieces[3])
        both1 = jnp.concatenate([top1, bottom1], axis=0)
        second = pair(p2, p3)
        y2, x2, c2, cb1 = to(second, 4), to(second, 2), to(second, 1), to(both1, 1)
        qkv = fill([(5, cy1), (3, cx1)], upper, qkv)
        *qkv, y2, x2, c2, cb1 = together(*qkv, y2, x2, c2, cb1)
        top2, bottom2, cy2, cx2 = to(y2[:half], 2), to(x2[half:], 4), to(y2, 1), to(x2, 1)
        qkv = fill([(6, both1), (7, cb1)], upper, qkv)
        qkv = fill([(0, second), (1, c2)], other, qkv)
        *qkv, top2, bottom2, cy2, cx2 = together(*qkv, top2, bottom2, cy2, cx2)
        both2 = jnp.concatenate([top2, bottom2], axis=0)
        cb2 = to(both2, 1)
        qkv = fill([(4, y2), (2, x2), (5, cy2), (3, cx2)], other, qkv)
        *qkv, cb2 = together(*qkv, cb2)
        qkv = fill([(6, both2), (7, cb2)], other, qkv)
        x_own = jnp.where(
            upper == 0, jnp.concatenate([first, second], 0), jnp.concatenate([second, first], 0)
        )
        x_sent, x_here = (p2, p3), (both2,)
    else:
        pieces = own_and_sent(layer_input, own, range(sequences))
        x_own = in_order(pieces, own).reshape(rows, model)
        gathered = lax.all_gather(x_own, ("fs", "sp"), axis=0)
        gathered = gathered.reshape(n_fs, folds, sequences, rows, model)
        gathered = lax.dynamic_index_in_dim(gathered, own, 2, keepdims=False)
        blocks = gathered.reshape(n_fs * folds, rows, model)
        tiles = jnp.arange(length // TILE, dtype=jnp.int32)
        qkv = project([blocks], tiles, *project_args, None, heads, head_dim, length)
        x_sent, x_here = (x_own,), (blocks,)
    q, k, v = qkv

    three = jnp.stack(
        [
            merged(w, d, u).T
            for w, d, u in zip((weight_mixer, weight_expand, weight_contract), downs[1:], ups[1:])
        ]
    )
    w_mixer, w_expand, w_contract = lax.all_gather(after(three, *x_here), "fs", axis=1, tiled=True)
    g_pieces = own_and_sent(after(output_grad, *x_sent), own, range(sequences))

    firsts, lasts = segs[::TILE], segs[TILE - 1 :: TILE]
    starts = jnp.sum(segs[None, :] < firsts[:, None], axis=1, dtype=jnp.int32) // TILE
    ends = (jnp.sum(segs[None, :] <= lasts[:, None], axis=1, dtype=jnp.int32) + TILE - 1) // TILE

    def sections_out(value):
        if folds > 1:
            cut = value.reshape(n_fs, folds, *value.shape[1:])
            value = lax.dynamic_index_in_dim(cut, fold_of, 1, keepdims=False)
        return lax.all_to_all(value, "fs", split_axis=0, concat_axis=0, tiled=True)

    o_even, aug = attend(starts, q, k, v, None, 0, heads, head_dim)
    a_even = sections_out(o_even)
    o_odd, aug = attend(starts, q, k, v, aug, 1, heads, head_dim)
    o_odd, a_even, g_pieces = together(o_odd, a_even, g_pieces)
    a_odd = sections_out(o_odd)
    attended = jnp.concatenate([a_even, a_odd], axis=2).reshape(model, rows)
    g_own = in_order(g_pieces, own).reshape(rows, model)

    x_f = x_own.astype(F32)
    scale_one = rms_scale(x_f)
    normed_one = (x_f * scale_one * gain_attention).astype(BF16)
    narrow = lambda u, down: dot_nn(u, down).astype(BF16)
    mixer = lax.dot_general(attended, w_mixer, (((0,), (1,)), ((), ())), preferred_element_type=F32)
    middle = x_f + mixer
    scale_two = rms_scale(middle)
    normed_two = (middle * scale_two * gain_feedforward).astype(BF16)
    expanded = dot_nt(normed_two, w_expand)
    gate = jax.nn.sigmoid(expanded)
    hidden = (expanded * gate).astype(BF16)
    contracted = dot_nt(hidden, w_contract)
    layer_output = (middle + contracted).astype(BF16).reshape(sequences, tokens, model)

    def adapter_back(u, grad, down, up):
        grad_up = dot_tn(narrow(u, down), grad)
        grad_narrow = dot_nt(grad, up).astype(BF16)
        return [dot_tn(grad_narrow, u), grad_up]

    grad_hidden = dot_nn(g_own, w_contract)
    grad_expanded = (grad_hidden * gate * (1.0 + expanded * (1.0 - gate))).astype(BF16)
    grad_normed_two = dot_nn(grad_expanded, w_expand)
    grad_middle = g_own.astype(F32) + rms_back(middle, scale_two, grad_normed_two * gain_feedforward)
    grad_mixer = grad_middle.astype(BF16)
    grad_attended = lax.dot_general(w_mixer, grad_mixer, (((0,), (1,)), ((), ())), preferred_element_type=F32)
    grad_heads = lax.all_to_all(
        grad_attended.astype(BF16).reshape(n_fs, unit, rows), "fs", split_axis=0, concat_axis=0, tiled=True
    )
    if folds > 1:
        every = lax.all_gather(grad_heads, "sp", axis=0)
        every = every.reshape(folds, sequences, n_fs, unit, rows)
        every = lax.dynamic_index_in_dim(every, own, 1, keepdims=False)
        grad_heads = jnp.swapaxes(every, 0, 1).reshape(n_fs * folds, unit, rows)

    narrow_mixer = dot_tn(attended, downs[1]).astype(BF16)
    early = jnp.concatenate(
        [
            lax.dot_general(
                dot_nt(grad_mixer, ups[1]).astype(BF16), attended, (((0,), (1,)), ((), ())), preferred_element_type=F32
            ),
            dot_tn(narrow_mixer, grad_mixer),
            *adapter_back(normed_two, grad_expanded, downs[2], ups[2]),
            *adapter_back(hidden, g_own, downs[3], ups[3]),
        ],
        axis=0,
    )
    grad_heads, early, layer_output = together(grad_heads, early, layer_output)
    w_all = lax.all_gather(after(w_own.T, attended), "fs", axis=0)
    early = lax.all_to_all(
        early.reshape(n_fs, early.shape[0] // n_fs, model), "fs", split_axis=0, concat_axis=0, tiled=True
    )

    kv_even, g_aug, dq = attend_back(ends, aug, k, v, (grad_heads, o_even, o_odd), 0, heads, head_dim)
    kv_even, g_aug, dq, early = together(kv_even, g_aug, dq, early)
    kv_even = sections_out(kv_even)
    early = jnp.sum(early, axis=0)
    grads_odd = attend_back(ends, aug, k, v, (g_aug, dq, scale_pad.T), 1, heads, head_dim)
    grads_odd, kv_even, early, w_all = together(grads_odd, kv_even, early, w_all)
    out_pieces = own_and_sent(after(layer_output, grads_odd), own, range(sequences))
    grads_odd = sections_out(grads_odd)
    grads_odd, out_pieces = together(grads_odd, out_pieces)
    layer_output = in_order(out_pieces, own)

    up_all = (
        ups[0].reshape(rank, 3, n_fs, unit).transpose(2, 0, 1, 3).reshape(n_fs, rank, 3 * unit)
    )
    narrow_turned = lax.dot_general(
        downs[0], normed_one, (((0,), (1,)), ((), ())), preferred_element_type=F32
    ).astype(BF16)
    input_grad, grad_down, grad_up = project_back(
        grads_odd, kv_even, w_all, up_all, narrow_turned, x_own, grad_middle, gain_attention[None]
    )
    input_grad = input_grad.reshape(sequences, tokens, model)
    grad_up = grad_up.reshape(n_fs, rank, 3, unit).transpose(1, 2, 0, 3).reshape(3 * rank, model)
    late = jnp.concatenate([grad_down, grad_up], axis=0)
    split = late.reshape(n_fs, late.shape[0] // n_fs, model)
    late = [
        piece_of(split, fs) if m == 0 else xor_permute(piece_of(split, fs ^ m), "fs", m) for m in range(n_fs)
    ]
    if folds == 1:
        input_grad = lax.all_to_all(input_grad, "sp", split_axis=0, concat_axis=0, tiled=True)
    else:
        input_grad = in_order(own_and_sent(input_grad, own, range(sequences)), own)
    part = jnp.concatenate([sum(late[1:], late[0]), early], axis=0)
    part = over_sequences(part, sequences, n_sp)
    table, input_grad = shares_of_all(fold(part, adapter_index, adapters, own), n_fs, input_grad)
    table = in_order(table, fs)

    factor = 1.0 / math.sqrt(length)
    outs = []
    late_rows = late[0].shape[0]
    late = joined_rows(table[:, :, :late_rows]) * factor
    early = joined_rows(table[:, :, late_rows:]) * factor
    for tables, wides in ((late, (3,)), (early, (1, 1, 1))):
        first = 0
        for wide in wides:
            outs.append(jnp.swapaxes(tables[:, first : first + rank], 1, 2))
            first += rank
            outs.append(tables[:, first : first + rank * wide].reshape(adapters, rank, wide * model))
            first += rank * wide
    return (layer_output, input_grad, *outs)


def solution(mesh):
    tokens = P(None, ("fs", "sp"), None)
    in_specs = (tokens, tokens) + (P(),) * 5 + (P(None, "fs"),) * 4 + (P(),) * 8
    out_specs = (tokens, tokens) + (P(),) * 8
    return jax.shard_map(local, mesh=mesh, in_specs=in_specs, out_specs=out_specs, check_vma=False)
```
